32 devices in a mesh: fsdp: 8 (over z, x), context: 4 (over y, core).
Axes of the slice: x: 2, y: 2, z: 4, core: 2. Of those that a mesh axis runs over, the one named last changes fastest.
Arguments:
- tokens: bfloat16 [16, 1024, 1536], P('fsdp', 'context'), may hold values from -6 to 6
- segments: int32 [16, 1024], P('fsdp', 'context'), may hold values from 0 to 15, never falling along the last dimension, each value on 1 to 512 neighbouring positions
- w_query: bfloat16 [1536, 1536], P('fsdp'), may hold values from -0.15625 to 0.15625
- w_key: bfloat16 [1536, 768], P('fsdp'), may hold values from -0.15625 to 0.15625
- w_value: bfloat16 [1536, 768], P('fsdp'), may hold values from -0.15625 to 0.15625
- w_out: bfloat16 [1536, 1536], P('fsdp'), may hold values from -0.875 to 0.875
- w_gate: bfloat16 [1536, 4096], P('fsdp', 'context'), may hold values from -0.15625 to 0.15625
- w_up: bfloat16 [1536, 4096], P('fsdp', 'context'), may hold values from -0.15625 to 0.15625
- w_down: bfloat16 [4096, 1536], P('context', 'fsdp'), may hold values from -0.09375 to 0.09375
- gain_attn: bfloat16 [1536], P('fsdp'), may hold values from 0.5 to 1.5
- gain_mlp: bfloat16 [1536], P('fsdp'), may hold values from 0.5 to 1.5
- cotangent: bfloat16 [16, 1024, 1536], P('fsdp', 'context'), may hold values from -6 to 6
Outputs:
- output: bfloat16 [16, 1024, 1536], P('fsdp', 'context')
- grad_tokens: float32 [16, 1024, 1536], P('fsdp', 'context')
- grad_w_query: float32 [1536, 1536], P('fsdp')
- grad_w_key: float32 [1536, 768], P('fsdp')
- grad_w_value: float32 [1536, 768], P('fsdp')
- grad_w_out: float32 [1536, 1536], P('fsdp')
- grad_w_gate: float32 [1536, 4096], P('fsdp', 'context')
- grad_w_up: float32 [1536, 4096], P('fsdp', 'context')
- grad_w_down: float32 [4096, 1536], P('context', 'fsdp')
- grad_gain_attn: float32 [1536], P('fsdp')
- grad_gain_mlp: float32 [1536], P('fsdp')
The draws below stay inside these ranges and needn't reach their ends.
Inputs may be any that keep to these rules, and one draw needn't show every extreme that they name: `segments`: in each sequence segment numbers never fall and all 16 documents appear; the longest has exactly 512 tokens.
All inputs are finite; a program needn't handle non-finite values.
Results may differ from the reference program's by a relative error of at most 0.02.
Values may be sent and summed in bfloat16 or wider, within the bound.
No kernel may reach another device: no remote copies, remote signals or barrier semaphores. Data moves between devices by JAX's collectives and lax.ppermute only.
A program may use at most 256 MiB of HBM per device.

```python
import math
import jax
import jax.numpy as jnp
import numpy as np
from jax import lax

D = 1536
H = 16
KVH = 8
HD = 96
FF = 4096
LEN = 1024
DOCS = 16
DOC_MOST = 512
SEQS = 16


def block_levels(key, extent, shards, least, high):
    level, own = 1.0, jax.random.fold_in(key, 6)
    for axis_at, parts in shards:
        heights = jnp.exp(jax.random.uniform(jax.random.fold_in(own, axis_at), (parts,), jnp.float32, least / len(shards), high / len(shards)))
        level = level * jnp.repeat(heights, extent[axis_at] // parts).reshape([-1 if axis == axis_at else 1 for axis in range(len(extent))])
    return level


def profile(amount, total, bound, skew):
    portions = [(1 << 20) // math.isqrt(standing ** skew) + 1 for standing in range(2, amount + 1)]
    spare, holding = total - bound - (amount - 1), [1] * (amount - 1)
    while spare > 0:
        free = [i for i in range(amount - 1) if holding[i] < bound]
        whole, remaining = sum([portions[i] for i in free]), spare
        for i in free:
            extra = min(bound - holding[i], max(1, remaining * portions[i] // whole), spare)
            holding[i] = holding[i] + extra
            spare = spare - extra
    return np.array([bound] + holding)


def uneven_parts(own_key, count, total, bound, slope):
    if count == 2:
        one = jax.random.randint(own_key, (), max(1, total - bound), min(bound, total - 1) + 1)
        return jnp.stack([one, total - one])
    tallies = jnp.asarray(profile(count, total, bound, slope), jnp.int32)
    twos = (count - 1) // 2
    donor, receiver = tallies[1:1 + 2 * twos:2], tallies[2:2 + 2 * twos:2]
    slack = jnp.minimum(donor - 1, bound - receiver)
    passed = jax.random.randint(jax.random.fold_in(own_key, 1), (twos,), 0, 1 << 20) % (slack + 1)
    tallies = tallies.at[1:1 + 2 * twos:2].set(donor - passed).at[2:2 + 2 * twos:2].set(receiver + passed)
    return tallies[jax.random.permutation(jax.random.fold_in(own_key, 2), count)]


def scatter_about(rng, shape, spread, most, pieces=(), kind=jnp.bfloat16):
    array = jax.random.normal(rng, shape, jnp.float32) * spread
    if len(pieces) > 0:
        array = block_levels(rng, shape, pieces, -0.22, 0.18) * array
    return jnp.clip(array, min=-most, max=most).astype(kind)


def setup_inputs(seed: int = 0) -> dict:
    arg_keys = jax.random.split(jax.random.key(seed), 13)
    tokens = scatter_about(arg_keys[0], (SEQS, LEN, D), 1.0, 6.0, ((0, 8), (1, 4)))
    segments = jax.vmap(lambda own: jnp.searchsorted(jnp.cumsum(uneven_parts(own, DOCS, LEN, DOC_MOST, 2)), jnp.arange(LEN), side="right"))(jax.random.split(arg_keys[1], SEQS)).reshape((SEQS, LEN)).astype(jnp.int32)
    w_query = scatter_about(arg_keys[2], (D, H * HD), D ** -0.5, 0.15625, ((0, 8),))
    w_key = scatter_about(arg_keys[3], (D, KVH * HD), D ** -0.5, 0.15625, ((0, 8),))
    w_value = scatter_about(arg_keys[4], (D, KVH * HD), D ** -0.5, 0.15625, ((0, 8),))
    w_out = scatter_about(arg_keys[5], (H * HD, D), 48 ** -0.5, 0.875, ((0, 8),))
    w_gate = scatter_about(arg_keys[6], (D, FF), D ** -0.5, 0.15625, ((0, 8), (1, 4)))
    w_up = scatter_about(arg_keys[7], (D, FF), D ** -0.5, 0.15625, ((0, 8), (1, 4)))
    w_down = scatter_about(arg_keys[8], (FF, D), FF ** -0.5, 0.09375, ((0, 4), (1, 8)))
    gain_attn = jnp.clip(1.0 + 0.1 * jax.random.normal(arg_keys[9], (D,), jnp.float32), 0.5, 1.5).astype(jnp.bfloat16)
    gain_mlp = jnp.clip(1.0 + 0.1 * jax.random.normal(arg_keys[10], (D,), jnp.float32), 0.5, 1.5).astype(jnp.bfloat16)
    cotangent = scatter_about(arg_keys[11], (SEQS, LEN, D), 1.0, 6.0, ((0, 8), (1, 4)))
    return dict(tokens=tokens, segments=segments, w_query=w_query, w_key=w_key, w_value=w_value, w_out=w_out, w_gate=w_gate, w_up=w_up, w_down=w_down, gain_attn=gain_attn, gain_mlp=gain_mlp, cotangent=cotangent)


@jax.custom_vjp
def low(v):
    return lax.optimization_barrier(v.astype(jnp.bfloat16)).astype(jnp.float32)

@jax.custom_vjp
def low_back(v):
    return v

def low_keep(v):
    return (low(v), None)

def low_pass(kept, grad):
    return (grad,)

def back_keep(v):
    return (v, None)

def back_low(kept, grad):
    return (low(grad),)
low.defvjp(low_keep, low_pass)
low_back.defvjp(back_keep, back_low)
EPSILON = 1e-05
THETA = 100000.0
TOP_PRECISION = lax.Precision.HIGHEST

def rms_scale(values, gain):
    return values * lax.rsqrt(lax.optimization_barrier(jnp.mean(values * values, axis=-1, keepdims=True)) + EPSILON) * gain

def rotate(values, cosines, sines):
    half_width = values.shape[-1] // 2
    leading = values[..., :half_width]
    trailing = values[..., half_width:]
    return jnp.concatenate([leading * cosines - trailing * sines, trailing * cosines + leading * sines], axis=-1)

def layer(inputs, seg_ids, w_query, w_key, w_value, w_out, w_gate, w_up, w_down, gain_attn, gain_mlp):
    length = inputs.shape[0]
    groups = H // KVH
    logit_scale = 1.0 / math.sqrt(HD)
    token_index = jnp.arange(length, dtype=jnp.int32)
    starts = jnp.concatenate([jnp.ones((1,), dtype=bool), seg_ids[1:] != seg_ids[:-1]])
    first_index = lax.cummax(jnp.where(starts, token_index, 0), axis=0)
    positions = (token_index - first_index).astype(jnp.float32)
    frequency = jnp.power(THETA, -(jnp.arange(HD // 2, dtype=jnp.float32) * 2.0 / HD))
    angles = positions[:, None] * frequency[None, :]
    cosines = jnp.cos(angles)[:, None, :]
    sines = jnp.sin(angles)[:, None, :]
    normed = low(rms_scale(inputs, gain_attn))
    queries = low_back(jnp.dot(normed, w_query, precision=TOP_PRECISION)).reshape(length, H, HD)
    key_rows = low_back(jnp.dot(normed, w_key, precision=TOP_PRECISION)).reshape(length, KVH, HD)
    value_matrix_rows = low_back(low(jnp.dot(normed, w_value, precision=TOP_PRECISION))).reshape(length, KVH, HD)
    qrot = low(rotate(queries, cosines, sines)).reshape(length, KVH, groups, HD)
    rotary_keys = low(rotate(key_rows, cosines, sines))
    block_rows = math.gcd(length, 512)
    block_count = length // block_rows

    def attend(items):
        query_block, q_seg, q_index = items
        unscaled_scores = jnp.einsum('wxif,axf->xiwa', query_block, rotary_keys, precision=TOP_PRECISION) * logit_scale
        unscaled_scores = low_back(unscaled_scores)
        allowed = (q_seg[:, None] == seg_ids[None, :]) & (token_index[None, :] <= q_index[:, None])
        scores = jnp.where(allowed[None, None], unscaled_scores, -1e+30)
        top_score = lax.optimization_barrier(jnp.max(scores, axis=-1, keepdims=True))
        weights = jnp.exp(scores - top_score)
        attention_probabilities = weights / lax.optimization_barrier(jnp.sum(weights, axis=-1, keepdims=True))
        return jnp.einsum('uvqe,eua->quva', low(attention_probabilities), value_matrix_rows, precision=TOP_PRECISION)
    mixed = lax.map(jax.checkpoint(attend), (qrot.reshape(block_count, block_rows, KVH, groups, HD), seg_ids.reshape(block_count, block_rows), token_index.reshape(block_count, block_rows)))
    mixed = low_back(low(mixed.reshape(length, H * HD)))
    resid = inputs + low_back(jnp.dot(mixed, w_out, precision=TOP_PRECISION))
    normed_two = low(rms_scale(resid, gain_mlp))
    gate_act = low_back(jnp.dot(normed_two, w_gate, precision=TOP_PRECISION))
    up_act = low_back(jnp.dot(normed_two, w_up, precision=TOP_PRECISION))
    hidden = low(jax.nn.silu(gate_act) * up_act)
    return resid + low_back(jnp.dot(hidden, w_down, precision=TOP_PRECISION))

def reference(tokens, segments, w_query, w_key, w_value, w_out, w_gate, w_up, w_down, gain_attn, gain_mlp, cotangent):
    weights = (w_query.astype(jnp.float32), w_key.astype(jnp.float32), w_value.astype(jnp.float32), w_out.astype(jnp.float32), w_gate.astype(jnp.float32), w_up.astype(jnp.float32), w_down.astype(jnp.float32), gain_attn.astype(jnp.float32), gain_mlp.astype(jnp.float32))

    def one_sequence(totals, items):
        inputs, seg_ids, grad_out = items

        def forward(inputs_f, *params):
            return layer(inputs_f, seg_ids, *params)
        result, pullback = jax.vjp(forward, inputs.astype(jnp.float32), *weights)
        grads = pullback(grad_out.astype(jnp.float32))
        totals = tuple((total + grad for total, grad in zip(totals, grads[1:])))
        return (totals, (result.astype(jnp.bfloat16), grads[0]))
    zeros = tuple((jnp.zeros_like(weight) for weight in weights))
    sums, (outputs, grad_inputs) = lax.scan(one_sequence, zeros, (tokens, segments, cotangent))
    return (outputs, grad_inputs, sums[0], sums[1], sums[2], sums[3], sums[4], sums[5], sums[6], sums[7], sums[8])
```

```python
import functools
import math

import jax
import jax.numpy as jnp
import numpy as np
from jax import lax
from jax.experimental import pallas as pl
from jax.experimental.pallas import tpu as pltpu
from jax.sharding import PartitionSpec as P

H = 16
KVH = 8
HD = 96


EPSILON = 1e-05
THETA = 100000.0


def rms_scale(values, gain):
    return values * lax.rsqrt(jnp.mean(values * values, axis=-1, keepdims=True) + EPSILON) * gain


def rotate(values, cosines, sines):
    half_width = values.shape[-1] // 2
    leading = values[..., :half_width]
    trailing = values[..., half_width:]
    return jnp.concatenate(
        [leading * cosines - trailing * sines, trailing * cosines + leading * sines], axis=-1
    )


def gated(gate_act, up_act):
    return jax.nn.silu(gate_act) * up_act


def inner(left, right):
    return jnp.einsum("ti,tj->ij", left, right, preferred_element_type=jnp.float32)


def outer_back(grad_rows, weight):
    return jnp.einsum("ti,ji->tj", grad_rows, weight, preferred_element_type=jnp.float32)


def reduce_grads(parts):
    shares = (
        lax.psum_scatter(
            parts[0].astype(jnp.bfloat16), "fsdp", scatter_dimension=0, tiled=True
        ).astype(jnp.float32),
        lax.psum_scatter(
            parts[1].astype(jnp.bfloat16), "fsdp", scatter_dimension=0, tiled=True
        ).astype(jnp.float32),
        lax.psum_scatter(
            parts[2].astype(jnp.bfloat16), "fsdp", scatter_dimension=0, tiled=True
        ).astype(jnp.float32),
        lax.psum_scatter(
            parts[3].astype(jnp.bfloat16), "fsdp", scatter_dimension=0, tiled=True
        ).astype(jnp.float32),
        lax.psum_scatter(
            parts[4].astype(jnp.bfloat16), "fsdp", scatter_dimension=0, tiled=True
        ).astype(jnp.float32),
        lax.psum_scatter(
            parts[5].astype(jnp.bfloat16), "fsdp", scatter_dimension=0, tiled=True
        ).astype(jnp.float32),
    )
    result = (
        lax.psum(shares[0].astype(jnp.bfloat16), "context").astype(jnp.float32),
        lax.psum(shares[1].astype(jnp.bfloat16), "context").astype(jnp.float32),
        lax.psum(shares[2].astype(jnp.bfloat16), "context").astype(jnp.float32),
        lax.psum(shares[3].astype(jnp.bfloat16), "context").astype(jnp.float32),
        lax.psum(shares[4].astype(jnp.bfloat16), "context").astype(jnp.float32),
        lax.psum(shares[5].astype(jnp.bfloat16), "context").astype(jnp.float32),
    )
    return result


def gather_attention(shard_query, shard_key, shard_value, shard_out, shard_gain_a, shard_gain_m):
    return (
        lax.all_gather(shard_query, "fsdp", axis=0, tiled=True),
        lax.all_gather(shard_key, "fsdp", axis=0, tiled=True),
        lax.all_gather(shard_value, "fsdp", axis=0, tiled=True),
        lax.all_gather(shard_out, "fsdp", axis=0, tiled=True),
        lax.all_gather(shard_gain_a, "fsdp", axis=0, tiled=True),
        lax.all_gather(shard_gain_m, "fsdp", axis=0, tiled=True),
    )


def gather_mlp(shard_gate, shard_up, shard_down):
    return (
        lax.all_gather(shard_gate, "fsdp", axis=0, tiled=True),
        lax.all_gather(shard_up, "fsdp", axis=0, tiled=True),
        lax.all_gather(shard_down, "fsdp", axis=1, tiled=True),
    )


def on_device_general(
    tokens,
    segments,
    w_query,
    w_key,
    w_value,
    w_out,
    w_gate,
    w_up,
    w_down,
    gain_attn,
    gain_mlp,
    cotangent,
):
    seq_count, tok_local, model_width = tokens.shape
    row_count = seq_count * tok_local
    groups = H // KVH
    kv_width = KVH * HD
    logit_scale = 1.0 / math.sqrt(HD)
    whole_seg = lax.all_gather(segments, "context", axis=1, tiled=True)
    length = whole_seg.shape[1]
    all_rows = seq_count * length
    offset = lax.axis_index("context") * tok_local
    key_index = jnp.arange(length, dtype=jnp.int32)
    query_index = offset + jnp.arange(tok_local, dtype=jnp.int32)
    starts = jnp.concatenate(
        [jnp.ones((seq_count, 1), dtype=bool), whole_seg[:, 1:] != whole_seg[:, :-1]], axis=1
    )
    first_index = lax.cummax(jnp.where(starts, key_index[None, :], 0), axis=1)
    positions = lax.dynamic_slice_in_dim(key_index[None, :] - first_index, offset, tok_local, 1)
    frequency = jnp.power(THETA, -(jnp.arange(HD // 2, dtype=jnp.float32) * 2.0 / HD))
    angles = positions.astype(jnp.float32)[:, :, None] * frequency[None, None, :]
    cosines = jnp.cos(angles).reshape(row_count, 1, HD // 2)
    sines = jnp.sin(angles).reshape(row_count, 1, HD // 2)
    x_flat = tokens.reshape(row_count, model_width).astype(jnp.float32)

    def masked_scores(query_sequence, k_seq, q_seg, k_seg):
        unscaled_scores = (
            jnp.einsum(
                "wxif,axf->xiwa",
                query_sequence,
                k_seq.reshape(length, KVH, HD),
                preferred_element_type=jnp.float32,
            )
            * logit_scale
        )
        allowed = (q_seg[:, None] == k_seg[None, :]) & (key_index[None, :] <= query_index[:, None])
        return jnp.where(allowed[None, None], unscaled_scores, -1e30)

    def attend(items):
        query_sequence, k_seq, v_seq, q_seg, k_seg = items
        scores = masked_scores(query_sequence, k_seq, q_seg, k_seg)
        top_score = jnp.max(scores, axis=-1, keepdims=True)
        weights = jnp.exp(scores - top_score)
        total = jnp.sum(weights, axis=-1, keepdims=True)
        attention_probabilities = (weights / total).astype(jnp.bfloat16)
        mixed_seq = jnp.einsum(
            "uvqe,eua->quva",
            attention_probabilities,
            v_seq.reshape(length, KVH, HD),
            preferred_element_type=jnp.float32,
        ).astype(jnp.bfloat16)
        return (mixed_seq, top_score + jnp.log(total))

    def forward(attn_weights, mlp_weights):
        full_query, full_key, full_value, full_out, full_gain_a, full_gain_m = attn_weights
        normed = rms_scale(x_flat, full_gain_a.astype(jnp.float32)).astype(jnp.bfloat16)
        queries = jnp.dot(normed, full_query, preferred_element_type=jnp.float32).reshape(
            row_count, H, HD
        )
        key_rows = jnp.dot(normed, full_key, preferred_element_type=jnp.float32).reshape(
            row_count, KVH, HD
        )
        value_matrix_rows = jnp.dot(normed, full_value, preferred_element_type=jnp.float32).astype(
            jnp.bfloat16
        )
        qrot = (
            rotate(queries, cosines, sines)
            .astype(jnp.bfloat16)
            .reshape(seq_count, tok_local, KVH, groups, HD)
        )
        rotary_keys = (
            rotate(key_rows, cosines, sines)
            .astype(jnp.bfloat16)
            .reshape(seq_count, tok_local, kv_width)
        )
        all_keys, all_values = (
            lax.all_gather(rotary_keys, "context", axis=1, tiled=True),
            lax.all_gather(
                value_matrix_rows.reshape(seq_count, tok_local, kv_width),
                "context",
                axis=1,
                tiled=True,
            ),
        )
        mixed, log_totals = lax.map(attend, (qrot, all_keys, all_values, segments, whole_seg))
        mixed_flat = mixed.reshape(row_count, H * HD)
        resid = x_flat + jnp.dot(mixed_flat, full_out, preferred_element_type=jnp.float32)
        full_gate, full_up, full_down = mlp_weights
        normed_two = rms_scale(resid, full_gain_m.astype(jnp.float32)).astype(jnp.bfloat16)
        all_normed_two = lax.all_gather(
            normed_two.reshape(seq_count, tok_local, model_width), "context", axis=1, tiled=True
        ).reshape(all_rows, model_width)
        gate_act = jnp.dot(all_normed_two, full_gate, preferred_element_type=jnp.float32)
        up_act = jnp.dot(all_normed_two, full_up, preferred_element_type=jnp.float32)
        hidden = gated(gate_act, up_act).astype(jnp.bfloat16)
        partial_down = jnp.dot(hidden, full_down, preferred_element_type=jnp.float32)
        down_sum = (
            lax.psum_scatter(
                partial_down.reshape(seq_count, length, model_width).astype(jnp.bfloat16),
                "context",
                scatter_dimension=1,
                tiled=True,
            )
            .astype(jnp.float32)
            .reshape(row_count, model_width)
        )
        final = resid + down_sum
        return (
            final,
            normed,
            qrot,
            all_keys,
            all_values,
            mixed,
            log_totals,
            resid,
            all_normed_two,
            gate_act,
            up_act,
            hidden,
        )

    attn_weights = gather_attention(w_query, w_key, w_value, w_out, gain_attn, gain_mlp)
    mlp_weights = gather_mlp(w_gate, w_up, w_down)
    state = forward(attn_weights, mlp_weights)
    output = state[0].astype(jnp.bfloat16).reshape(seq_count, tok_local, model_width)
    (
        final,
        normed,
        qrot,
        all_keys,
        all_values,
        mixed,
        log_totals,
        resid,
        all_normed_two,
        gate_act,
        up_act,
        hidden,
    ) = state
    full_query, full_key, full_value, full_out, full_gain_a, full_gain_m = attn_weights
    full_gate, full_up, full_down = mlp_weights
    grad_out = cotangent.reshape(row_count, model_width)
    all_grad_out = lax.all_gather(cotangent, "context", axis=1, tiled=True).reshape(
        all_rows, model_width
    )
    grad_down_t = inner(all_grad_out, hidden)
    grad_hidden = outer_back(all_grad_out, full_down)
    gate_pull = jax.vjp(gated, gate_act, up_act)[1]
    grad_gate_f, grad_up_f = gate_pull(grad_hidden)
    grad_gate_act = grad_gate_f.astype(jnp.bfloat16)
    grad_up_act = grad_up_f.astype(jnp.bfloat16)
    grad_gate = inner(all_normed_two, grad_gate_act)
    grad_up = inner(all_normed_two, grad_up_act)
    part_normed_two = outer_back(grad_gate_act, full_gate) + outer_back(grad_up_act, full_up)
    grad_normed_two = lax.psum_scatter(
        part_normed_two.reshape(seq_count, length, model_width),
        "context",
        scatter_dimension=1,
        tiled=True,
    ).reshape(row_count, model_width)
    norm_pull = jax.vjp(rms_scale, resid, full_gain_m.astype(jnp.float32))[1]
    back_resid, grad_gain_m = norm_pull(grad_normed_two)
    mlp_shares = (
        lax.psum_scatter(
            grad_gate.astype(jnp.bfloat16), "fsdp", scatter_dimension=0, tiled=True
        ).astype(jnp.float32),
        lax.psum_scatter(
            grad_up.astype(jnp.bfloat16), "fsdp", scatter_dimension=0, tiled=True
        ).astype(jnp.float32),
        lax.psum_scatter(
            grad_down_t.astype(jnp.bfloat16), "fsdp", scatter_dimension=0, tiled=True
        ).astype(jnp.float32),
    )
    grad_resid = grad_out.astype(jnp.float32) + back_resid
    grad_attn = grad_resid.astype(jnp.bfloat16)
    mixed_flat = mixed.reshape(row_count, H * HD)
    grad_out_w = inner(mixed_flat, grad_attn)
    grad_mixed = (
        outer_back(grad_attn, full_out)
        .astype(jnp.bfloat16)
        .reshape(seq_count, tok_local, KVH, groups, HD)
    )

    def attend_back(items):
        query_sequence, k_seq, v_seq, q_seg, k_seg, log_total, grad_seq = items
        scores = masked_scores(query_sequence, k_seq, q_seg, k_seg)
        attention_probabilities = jnp.exp(scores - log_total)
        grad_probs = jnp.einsum(
            "wxif,axf->xiwa",
            grad_seq,
            v_seq.reshape(length, KVH, HD),
            preferred_element_type=jnp.float32,
        )
        weighted = jnp.sum(attention_probabilities * grad_probs, axis=-1, keepdims=True)
        score_gradient = (attention_probabilities * (grad_probs - weighted)).astype(jnp.bfloat16)
        grad_q = (
            jnp.einsum(
                "uvqe,eua->quva",
                score_gradient,
                k_seq.reshape(length, KVH, HD),
                preferred_element_type=jnp.float32,
            )
            * logit_scale
        )
        grad_k = (
            jnp.einsum(
                "jnbp,bjny->pjy", score_gradient, query_sequence, preferred_element_type=jnp.float32
            )
            * logit_scale
        )
        grad_v = jnp.einsum(
            "jnbp,bjny->pjy",
            attention_probabilities.astype(jnp.bfloat16),
            grad_seq,
            preferred_element_type=jnp.float32,
        )
        return (grad_q, grad_k.reshape(length, kv_width), grad_v.reshape(length, kv_width))

    grad_qrot, part_keys, part_values = lax.map(
        attend_back, (qrot, all_keys, all_values, segments, whole_seg, log_totals, grad_mixed)
    )
    grad_krot, grad_vals = (
        lax.psum_scatter(
            part_keys.astype(jnp.bfloat16), "context", scatter_dimension=1, tiled=True
        ).astype(jnp.float32),
        lax.psum_scatter(
            part_values.astype(jnp.bfloat16), "context", scatter_dimension=1, tiled=True
        ).astype(jnp.float32),
    )
    grad_queries = (
        rotate(grad_qrot.reshape(row_count, H, HD), cosines, -sines)
        .astype(jnp.bfloat16)
        .reshape(row_count, H * HD)
    )
    grad_keys = (
        rotate(grad_krot.reshape(row_count, KVH, HD), cosines, -sines)
        .astype(jnp.bfloat16)
        .reshape(row_count, kv_width)
    )
    grad_values = grad_vals.reshape(row_count, kv_width).astype(jnp.bfloat16)
    grad_query_w = inner(normed, grad_queries)
    grad_key_w = inner(normed, grad_keys)
    grad_value_w = inner(normed, grad_values)
    grad_normed = (
        outer_back(grad_queries, full_query)
        + outer_back(grad_keys, full_key)
        + outer_back(grad_values, full_value)
    )
    first_pull = jax.vjp(rms_scale, x_flat, full_gain_a.astype(jnp.float32))[1]
    back_input, grad_gain_a = first_pull(grad_normed)
    attn_grads = reduce_grads(
        (grad_query_w, grad_key_w, grad_value_w, grad_out_w, grad_gain_a, grad_gain_m)
    )
    grad_input = (grad_resid + back_input).reshape(seq_count, tok_local, model_width)
    return (
        output,
        grad_input,
        attn_grads[0],
        attn_grads[1],
        attn_grads[2],
        attn_grads[3],
        mlp_shares[0],
        mlp_shares[1],
        jnp.transpose(mlp_shares[2]),
        attn_grads[4],
        attn_grads[5],
    )


BF = jnp.bfloat16
F32 = jnp.float32
LANES = 128
HALF = HD // 2
NEG = -1e30
SCALE = 1.0 / math.sqrt(HD)
SCALE_LOG2 = SCALE * math.log2(math.e)
CTX = 4
QH = H // CTX
KH = KVH // CTX
BLK = 256
NT = (((1,), (1,)), ((), ()))
TN = (((0,), (0,)), ((), ()))


def dot_nt(a, b):
    return lax.dot_general(a, b, NT, preferred_element_type=F32)


def dot_tn(a, b):
    return lax.dot_general(a, b, TN, preferred_element_type=F32)


def dot_nn(a, b):
    return jnp.dot(a, b, preferred_element_type=F32)


def lane_iota(rows, width):
    return lax.broadcasted_iota(jnp.int32, (rows, width), 1)


def params(mb, sem):
    return pltpu.CompilerParams(vmem_limit_bytes=mb << 20, dimension_semantics=sem)


def cost(flops, nbytes, trans=0):
    return pl.CostEstimate(flops=int(flops), bytes_accessed=int(nbytes), transcendentals=int(trans))


def packed_columns():
    src = []
    for group in range(6):
        if group < 4:
            member, half = group // 2, group % 2
            for g in range(KH):
                head = 2 * g + member
                src += [head * HD + half * HALF + t for t in range(HALF)]
        else:
            half = group - 4
            for g in range(KH):
                src += [QH * HD + g * HD + half * HALF + t for t in range(HALF)]
        src += [(QH + KH) * HD + group * 32 + t for t in range(32)]
    return np.array(src, np.int32)


def pack_matrix():
    n = (QH + 2 * KH) * HD
    src = jnp.asarray(packed_columns())
    return (lax.broadcasted_iota(jnp.int32, (n, n), 0) == src[None, :]).astype(BF)


def rms_rows(x, gain):
    r = lax.rsqrt(jnp.mean(x * x, axis=-1, keepdims=True) + EPSILON)
    return x * r * gain


def qkv_kernel(c_ref, f_ref, x0, x1, x2, x3, gain, w, cos, sin, normed, q, k, v, w_out, xs, ws):
    @pl.when((pl.program_id(0) == 0) & (pl.program_id(1) == 0))
    def _():
        count, rows, _ = w.shape
        for b in range(count):
            ws[b * rows : (b + 1) * rows, :] = w[b ^ f_ref[0], :, 0 : ws.shape[1]]
        w_out[...] = ws[...]

    for d, ref in enumerate((x0, x1, x2, x3)):

        @pl.when(pl.program_id(0) == d)
        def _():
            xs[...] = ref[0]

    n = rms_rows(xs[...].astype(F32), gain[...]).astype(BF)
    normed[...] = n
    t = dot_nn(n, ws[...])
    y = [t[:, LANES * p : LANES * (p + 1)] for p in range(6)]
    c, s = cos[...], sin[...]
    rot = []
    for p in range(0, 6, 2):
        rot += [y[p] * c - y[p + 1] * s, y[p + 1] * c + y[p] * s]
    for p in range(4):
        q[:, LANES * p : LANES * (p + 1)] = rot[p].astype(BF)
    for p in range(2):
        k[:, LANES * p : LANES * (p + 1)] = rot[4 + p].astype(BF)
    quarter = lane_iota(y[0].shape[0], LANES) // 32

    def place(parts):
        out = jnp.ones_like(y[0])
        for dst, p in parts:
            piece = y[p] if dst == 3 else pltpu.roll(y[p], 32 * (dst + 1), 1)
            out = jnp.where(quarter == dst, piece, out)
        return out.astype(BF)

    v[:, 0:128] = place(((0, 0), (1, 1), (2, 2), (3, 0)))
    v[:, 128:256] = place(((0, 1), (1, 2)))
    v[:, 256:384] = place(((2, 3), (3, 4)))
    v[:, 384:512] = place(((0, 5), (1, 3), (2, 4), (3, 5)))


def qkv_call(c, f, xs, gain, w, cos, sin):
    seqs, tok, width = xs[0].shape
    total = seqs * CTX * tok
    cols = 768

    def own(d):
        return pl.BlockSpec(
            (1, tok, width),
            lambda i, s, c, f: (jnp.where(i == d, s, jnp.where(i < d, 0, seqs - 1)), 0, 0),
        )

    def rows(n):
        return pl.BlockSpec((tok, n), lambda i, s, c, f: (s * CTX + (i ^ c[0]), 0))

    return pl.pallas_call(
        qkv_kernel,
        grid_spec=pltpu.PrefetchScalarGridSpec(
            num_scalar_prefetch=2,
            grid=(CTX, seqs),
            in_specs=[
                own(0),
                own(1),
                own(2),
                own(3),
                pl.BlockSpec((1, width), lambda i, s, c, f: (0, 0)),
                pl.BlockSpec(w.shape, lambda i, s, c, f: (0, 0, 0)),
                rows(LANES),
                rows(LANES),
            ],
            out_specs=[
                rows(width),
                rows(512),
                rows(256),
                rows(512),
                pl.BlockSpec((width, cols), lambda i, s, c, f: (0, 0)),
            ],
            scratch_shapes=[pltpu.VMEM((tok, width), BF), pltpu.VMEM((width, cols), BF)],
        ),
        out_shape=[
            jax.ShapeDtypeStruct((total, width), BF),
            jax.ShapeDtypeStruct((total, 512), BF),
            jax.ShapeDtypeStruct((total, 256), BF),
            jax.ShapeDtypeStruct((total, 512), BF),
            jax.ShapeDtypeStruct((width, cols), BF),
        ],
        compiler_params=params(48, ("arbitrary", "arbitrary")),
        cost_estimate=cost(2 * total * width * 768, total * width * 4 + width * 768 * 4 + total * 3584),
        name="qkv",
    )(c, f, *xs, gain, w, cos, sin)


def head_masks(rows):
    lane = lane_iota(rows, 256)
    inner_lane = lane % LANES
    by_kv = [inner_lane < HALF, (inner_lane >= HALF) & (inner_lane < HD)]
    in_mixed = [
        lane < HD,
        (lane >= HD) & (lane < 2 * HD),
        (lane >= 64) & (lane < 64 + HD),
        lane >= 64 + HD,
    ]
    return lane, by_kv, in_mixed


def attend_kernel(js_ref, c_ref, q, k, v, start, mixed, lse, vt_s, m_s, o_s):
    s_id, i = pl.program_id(0), pl.program_id(1)
    blocks = k.shape[0] // BLK
    lane, by_kv, in_mixed = head_masks(BLK)
    sub = lax.broadcasted_iota(jnp.int32, (256, BLK), 0)
    take_a = (sub < HD) | ((sub >= 192) & (sub < 224))
    take_b = ((sub >= 64) & (sub < 64 + HD)) | (sub < 32)
    zero = jnp.zeros((BLK, 256), BF)

    @pl.when(i == 0)
    def _():
        for b in range(blocks):
            vt_s[b] = jnp.transpose(v[b * BLK : (b + 1) * BLK, :])

    m_s[...] = jnp.full_like(m_s, -jnp.inf)
    o_s[...] = jnp.zeros_like(o_s)
    col = i * BLK + lax.broadcasted_iota(jnp.int32, (BLK, BLK), 1)
    first = start[0, 0]
    low = js_ref[s_id * CTX + i]

    def step(t, _):
        j = i - t
        kb = k[pl.ds(pl.multiple_of(j * BLK, BLK), BLK), :]
        row = j * BLK + lax.broadcasted_iota(jnp.int32, (BLK, BLK), 0)
        bias = jnp.where((row >= first) & (row <= col), 0.0, NEG)
        for win, take in enumerate((take_a, take_b)):
            vt = vt_s[j, 256 * win : 256 * (win + 1), :]
            outs, alphas = [], []
            for m in range(2):
                h = 2 * win + m
                qh = jnp.where(by_kv[win], q[:, 256 * m : 256 * (m + 1)], zero)
                sc = dot_nt(kb, qh) * SCALE_LOG2 + bias
                m_old = m_s[h : h + 1, :]
                m_new = jnp.maximum(m_old, jnp.max(sc, axis=0, keepdims=True))
                p = jnp.exp2(sc - m_new)
                alphas.append(jnp.exp2(m_old - m_new))
                m_s[h : h + 1, :] = m_new
                outs.append(dot_nn(vt, p.astype(BF)))
            o_s[win] = o_s[win] * jnp.where(take, alphas[0], alphas[1]) + jnp.where(take, outs[0], outs[1])
        return 0

    lax.fori_loop(0, i - low + 1, step, 0)
    sums = [o_s[0, 192:193, :], o_s[0, 224:225, :], o_s[1, 0:1, :], o_s[1, 32:33, :]]
    inv = [1.0 / x for x in sums]
    a = jnp.transpose(o_s[0] * jnp.where(take_a, inv[0], inv[1]))
    b = jnp.transpose(o_s[1] * jnp.where(take_b, inv[2], inv[3]))
    mixed[0, 0, :, 0:128] = a[:, 0:128].astype(BF)
    mixed[0, 0, :, 128:256] = jnp.where(lane[:, :LANES] < 64, a[:, 128:256], b[:, 0:128]).astype(BF)
    mixed[0, 0, :, 256:384] = b[:, 128:256].astype(BF)
    lse[0, 0] = jnp.zeros_like(lse[0, 0])
    for h in range(QH):
        lse[0, 0, h : h + 1, :] = m_s[h : h + 1, :] + jnp.log2(sums[h])


def attend_call(c, js, q, k, v, start, seqs, length):
    blocks = length // BLK
    return pl.pallas_call(
        attend_kernel,
        grid_spec=pltpu.PrefetchScalarGridSpec(
            num_scalar_prefetch=2,
            grid=(seqs, blocks),
            in_specs=[
                pl.BlockSpec((BLK, 512), lambda s, i, js, c: (s * CTX + i, 0)),
                pl.BlockSpec((length, 256), lambda s, i, js, c: (s, 0)),
                pl.BlockSpec((length, 512), lambda s, i, js, c: (s, 0)),
                pl.BlockSpec((1, 1, 1, BLK), lambda s, i, js, c: (s, i, 0, 0)),
            ],
            out_specs=[
                pl.BlockSpec((1, 1, BLK, QH * HD), lambda s, i, js, c: (i ^ c[0], s, 0, 0)),
                pl.BlockSpec((1, 1, 8, BLK), lambda s, i, js, c: (s, i, 0, 0)),
            ],
            scratch_shapes=[
                pltpu.VMEM((blocks, 512, BLK), BF),
                pltpu.VMEM((8, BLK), F32),
                pltpu.VMEM((2, 256, BLK), F32),
            ],
        ),
        out_shape=[
            jax.ShapeDtypeStruct((CTX, seqs, BLK, QH * HD), BF),
            jax.ShapeDtypeStruct((seqs, blocks, 8, BLK), F32),
        ],
        compiler_params=params(40, ("arbitrary", "arbitrary")),
        cost_estimate=cost(6e9, 8e6, 4e6),
        name="attend",
    )(js, c, q, k, v, start)


def attend_back_kernel(
    js_ref, c_ref, q, k, v, o, d0, d1, d23, lse, start, cos, sin, out, do_s, dl_s, kt_s, dq_s, dk_s, dv_s
):
    s_id = pl.program_id(0)
    c = c_ref[0]
    blocks = q.shape[0] // BLK
    lane, by_kv, in_mixed = head_masks(BLK)
    zero = jnp.zeros((BLK, 256), BF)
    mixed_lane = lane_iota(8, QH * HD)
    mixed_row = lax.broadcasted_iota(jnp.int32, (8, QH * HD), 0)
    picks = (mixed_lane // HD == mixed_row).astype(F32)
    for d in range(CTX):
        b = d ^ c
        rows = pl.ds(pl.multiple_of(b * BLK, BLK), BLK)
        g = d0[0, 0] if d == 0 else d1[0] if d == 1 else d23[d - 2, 0]
        do_s[rows, :] = g
        prod = g.astype(F32) * o[d, 0].astype(F32)
        dl_s[b] = lax.dot_general(
            picks, prod, NT, preferred_element_type=F32, precision=lax.Precision.HIGHEST
        )
    for b in range(blocks):
        kt_s[b] = jnp.transpose(k[b * BLK : (b + 1) * BLK, :])
    sub_in = lax.broadcasted_iota(jnp.int32, (256, BLK), 0) % LANES
    sub_kv = [sub_in < HALF, (sub_in >= HALF) & (sub_in < HD)]
    dq_s[...] = jnp.zeros_like(dq_s)
    dk_s[...] = jnp.zeros_like(dk_s)
    dv_s[...] = jnp.zeros_like(dv_s)

    def outer(i, _):
        qs = pl.ds(pl.multiple_of(i * BLK, BLK), BLK)
        col = i * BLK + lax.broadcasted_iota(jnp.int32, (BLK, BLK), 1)
        first = start[0, i]
        delta = dl_s[i]
        logs = lse[0, i]

        def step(t, _):
            j = i - t
            ks = pl.ds(pl.multiple_of(j * BLK, BLK), BLK)
            kb = k[ks, :]
            kt = kt_s[j]
            row = j * BLK + lax.broadcasted_iota(jnp.int32, (BLK, BLK), 0)
            bias = jnp.where((row >= first) & (row <= col), 0.0, NEG)
            dk = jnp.zeros((BLK, 256), F32)
            dq = [jnp.zeros((256, BLK), F32) for _ in range(2)]
            for win in range(KH):
                vb = v[ks, 256 * win : 256 * (win + 1)]
                kg = jnp.where(sub_kv[win], kt, zero)
                dv = jnp.zeros((BLK, 256), F32)
                for m in range(2):
                    h = 2 * win + m
                    qh = jnp.where(by_kv[win], q[qs, 256 * m : 256 * (m + 1)], zero)
                    do = jnp.where(in_mixed[h], do_s[qs, LANES * win : LANES * win + 256], zero)
                    sc = dot_nt(kb, qh) * SCALE_LOG2 + bias
                    p = jnp.exp2(sc - logs[h : h + 1, :])
                    dp = dot_nt(vb, do)
                    ds = (p * (dp - delta[h : h + 1, :])).astype(BF)
                    dv = dv + dot_nn(p.astype(BF), do)
                    dk = dk + dot_nn(ds, qh)
                    dq[m] = dq[m] + dot_nn(kg, ds)
                dv_s[ks, 256 * win : 256 * (win + 1)] += dv
            dk_s[ks, :] += dk
            for m in range(2):
                dq_s[i, m] += dq[m]
            return 0

        lax.fori_loop(0, i - js_ref[s_id * CTX + i] + 1, step, 0)
        return 0

    lax.fori_loop(0, blocks, outer, 0)
    head_lane = lane[:, :LANES] < HD

    def finish(i, _):
        rows = pl.ds(pl.multiple_of(i * BLK, BLK), BLK)
        cs, sn = cos[rows, :] * SCALE, sin[rows, :] * SCALE
        a0, a1 = dv_s[rows, 0:128], dv_s[rows, 128:256]
        b0, b1 = dv_s[rows, 256:384], dv_s[rows, 384:512]

        def r(x, n):
            return pltpu.roll(x, n, 1)

        pieces = [
            r(a0, 96) + a0,
            r(a0, 64) + r(a1, 96),
            r(a0, 32) + r(a1, 64),
            r(b0, 32) + r(b1, 64),
            b0 + r(b1, 32),
            r(b1, 96) + b1,
        ]
        grads = []
        for m in range(2):
            dq = jnp.transpose(dq_s[i, m])
            grads += [dq[:, 0:128], dq[:, 128:256]]
        grads += [dk_s[rows, 0:128], dk_s[rows, 128:256]]
        for p in range(0, 6, 2):
            first_half = grads[p] * cs + grads[p + 1] * sn
            second_half = grads[p + 1] * cs - grads[p] * sn
            out[rows, LANES * p : LANES * (p + 1)] = jnp.where(head_lane, first_half, pieces[p]).astype(BF)
            out[rows, LANES * (p + 1) : LANES * (p + 2)] = jnp.where(
                head_lane, second_half, pieces[p + 1]
            ).astype(BF)
        return 0

    lax.fori_loop(0, blocks, finish, 0)


def attend_back_call(c, js, q, k, v, o, d0, d1, d23, lse, start, cos, sin, seqs, length):
    blocks = length // BLK
    width = QH * HD
    return pl.pallas_call(
        attend_back_kernel,
        grid_spec=pltpu.PrefetchScalarGridSpec(
            num_scalar_prefetch=2,
            grid=(seqs,),
            in_specs=[
                pl.BlockSpec((length, 512), lambda s, js, c: (s, 0)),
                pl.BlockSpec((length, 256), lambda s, js, c: (s, 0)),
                pl.BlockSpec((length, 512), lambda s, js, c: (s, 0)),
                pl.BlockSpec((CTX, 1, BLK, width), lambda s, js, c: (0, s, 0, 0)),
                pl.BlockSpec((1, 1, BLK, width), lambda s, js, c: (0, s, 0, 0)),
                pl.BlockSpec((1, BLK, width), lambda s, js, c: (s, 0, 0)),
                pl.BlockSpec((2, 1, BLK, width), lambda s, js, c: (0, s, 0, 0)),
                pl.BlockSpec((1, blocks, 8, BLK), lambda s, js, c: (s, 0, 0, 0)),
                pl.BlockSpec((1, blocks, 1, BLK), lambda s, js, c: (s, 0, 0, 0)),
                pl.BlockSpec((length, LANES), lambda s, js, c: (s, 0)),
                pl.BlockSpec((length, LANES), lambda s, js, c: (s, 0)),
            ],
            out_specs=pl.BlockSpec((length, 768), lambda s, js, c: (s, 0)),
            scratch_shapes=[
                pltpu.VMEM((length, width), BF),
                pltpu.VMEM((blocks, 8, BLK), F32),
                pltpu.VMEM((blocks, 256, BLK), BF),
                pltpu.VMEM((blocks, 2, 256, BLK), F32),
                pltpu.VMEM((length, 256), F32),
                pltpu.VMEM((length, 512), F32),
            ],
        ),
        out_shape=jax.ShapeDtypeStruct((seqs * length, 768), BF),
        compiler_params=params(48, ("arbitrary",)),
        cost_estimate=cost(2e10, 1.2e7, 4e6),
        name="attend_back",
    )(js, c, q, k, v, o, d0, d1, d23, lse, start, cos, sin)


def assemble_kernel(c_ref, f_ref, p0, p1, p2, p3, out):
    quarter = p0.shape[-1]
    for b in range(CTX):
        for d, ref in enumerate((p0, p1, p2, p3)):

            @pl.when((b ^ c_ref[0]) == d)
            def _():
                out[:, b * quarter : (b + 1) * quarter] = ref[0]


def assemble_call(c, f, parts):
    count, rows, quarter = parts[0].shape
    part = pl.BlockSpec((1, rows, quarter), lambda b, c, f: (b ^ f[0], 0, 0))
    return pl.pallas_call(
        assemble_kernel,
        grid_spec=pltpu.PrefetchScalarGridSpec(
            num_scalar_prefetch=2,
            grid=(count,),
            in_specs=[part] * CTX,
            out_specs=pl.BlockSpec((rows, CTX * quarter), lambda b, c, f: (b, 0)),
        ),
        out_shape=jax.ShapeDtypeStruct((count * rows, CTX * quarter), BF),
        compiler_params=params(20, ("arbitrary",)),
        cost_estimate=cost(0, count * rows * quarter * 16),
        name="assemble",
    )(c, f, *parts)


def out_kernel(c_ref, x, m0, m1, m2, m3, w, gain, resid, normed):
    c = c_ref[0]
    acc = x[0].astype(F32)
    for d, ref in enumerate((m0, m1, m2, m3)):
        rows = pl.ds(pl.multiple_of((d ^ c) * (QH * HD), QH * HD), QH * HD)
        acc = acc + dot_nn(ref[0, 0], w[rows, :])
    resid[0] = acc
    normed[0] = rms_rows(acc, gain[...]).astype(BF)


def out_call(c, x, mixed, r1, r2, w, gain):
    seqs, tok, width = x.shape
    inner_w = QH * HD

    def slot(n):
        return pl.BlockSpec((1, 1, tok, inner_w), lambda s, c: (n, s, 0, 0))

    tile = pl.BlockSpec((1, tok, width), lambda s, c: (s, 0, 0))
    return pl.pallas_call(
        out_kernel,
        grid_spec=pltpu.PrefetchScalarGridSpec(
            num_scalar_prefetch=1,
            grid=(seqs,),
            in_specs=[
                tile,
                slot(0),
                slot(0),
                slot(0),
                slot(1),
                pl.BlockSpec((H * HD, width), lambda s, c: (0, 0)),
                pl.BlockSpec((1, width), lambda s, c: (0, 0)),
            ],
            out_specs=[tile, tile],
        ),
        out_shape=[
            jax.ShapeDtypeStruct((seqs, tok, width), F32),
            jax.ShapeDtypeStruct((seqs, tok, width), BF),
        ],
        compiler_params=params(48, ("arbitrary",)),
        cost_estimate=cost(2 * seqs * tok * width * width, width * width * 2 + seqs * tok * width * 10),
        name="out_proj",
    )(c, x, mixed, r1, r2, r2, w, gain)


def rms_back(v, gain, dy):
    r = lax.rsqrt(jnp.mean(v * v, axis=-1, keepdims=True) + EPSILON)
    dyg = dy * gain
    inner_sum = jnp.mean(dyg * v, axis=-1, keepdims=True)
    return r * dyg - v * (r * r * r * inner_sum), dy * v * r


def out_back_kernel(c_ref, part_a, part_b, resid, gain, dy, w, dresid, dattn, dmixed, dgain):
    c = c_ref[0]
    dn = part_a[0].astype(F32) + part_b[0].astype(F32)
    dr, dg = rms_back(resid[0], gain[...], dn)
    total = dy[0].astype(F32) + dr
    dresid[0] = total
    low = total.astype(BF)
    dattn[0] = low
    dgain[0] = jnp.broadcast_to(jnp.sum(dg, axis=0, keepdims=True), dgain.shape[1:])
    for d in range(CTX):
        rows = pl.ds(pl.multiple_of((d ^ c) * (QH * HD), QH * HD), QH * HD)
        dmixed[d, 0] = dot_nt(low, w[rows, :]).astype(BF)


def out_back_call(c, part_a, part_b, resid, gain, dy, w):
    seqs, tok, width = dy.shape
    inner_w = QH * HD
    tile = pl.BlockSpec((1, tok, width), lambda s, c: (s, 0, 0))
    return pl.pallas_call(
        out_back_kernel,
        grid_spec=pltpu.PrefetchScalarGridSpec(
            num_scalar_prefetch=1,
            grid=(seqs,),
            in_specs=[
                tile,
                tile,
                tile,
                pl.BlockSpec((1, width), lambda s, c: (0, 0)),
                tile,
                pl.BlockSpec((H * HD, width), lambda s, c: (0, 0)),
            ],
            out_specs=[
                tile,
                tile,
                pl.BlockSpec((CTX, 1, tok, inner_w), lambda s, c: (0, s, 0, 0)),
                pl.BlockSpec((1, 8, width), lambda s, c: (s, 0, 0)),
            ],
        ),
        out_shape=[
            jax.ShapeDtypeStruct((seqs, tok, width), F32),
            jax.ShapeDtypeStruct((seqs, tok, width), BF),
            jax.ShapeDtypeStruct((CTX, seqs, tok, inner_w), BF),
            jax.ShapeDtypeStruct((seqs, 8, width), F32),
        ],
        compiler_params=params(56, ("arbitrary",)),
        cost_estimate=cost(2 * seqs * tok * width * width, width * width * 2 + seqs * tok * width * 20),
        name="out_back",
    )(c, part_a, part_b, resid, gain, dy, w)


def mlp_kernel(n2, dy, wg, wu, wd, hidden, grads):
    n, g_out = n2[...], dy[...]
    gate = dot_nn(n, wg[...])
    up = dot_nn(n, wu[...])
    dh = dot_nn(g_out, wd[...])
    sig = 1.0 / (1.0 + jnp.exp(-gate))
    act = gate * sig
    hidden[...] = (act * up).astype(BF)
    cols = wg.shape[1]
    grads[0] = (dh * up * (sig + act * (1.0 - sig))).astype(BF)
    grads[1] = (dh * act).astype(BF)


def mlp_call(n2, dy, w):
    rows, width = n2.shape
    ff = w.shape[1] // 3
    tile = BLK
    steps = ff // tile
    full = pl.BlockSpec((rows, width), lambda j: (0, 0))
    return pl.pallas_call(
        mlp_kernel,
        grid=(steps,),
        in_specs=[
            full,
            full,
            pl.BlockSpec((width, tile), lambda j: (0, j)),
            pl.BlockSpec((width, tile), lambda j: (0, j + steps)),
            pl.BlockSpec((width, tile), lambda j: (0, j + 2 * steps)),
        ],
        out_specs=[
            pl.BlockSpec((rows, tile), lambda j: (0, j)),
            pl.BlockSpec((2, rows, tile), lambda j: (0, 0, j)),
        ],
        out_shape=[
            jax.ShapeDtypeStruct((rows, ff), BF),
            jax.ShapeDtypeStruct((2, rows, ff), BF),
        ],
        compiler_params=params(40, ("arbitrary",)),
        cost_estimate=cost(6 * rows * width * ff, width * ff * 6 + rows * width * 4 + rows * ff * 6, rows * ff),
        name="mlp",
    )(n2, dy, w, w, w)


def sum_nt_kernel(slots, *refs):
    count = len(slots)
    out = refs[-1]
    acc = None
    for n in range(count):
        left = refs[n]
        part = dot_nt(left[0] if len(left.shape) == 3 else left[...], refs[count + n][...])
        acc = part if acc is None else acc + part
    out[...] = acc.astype(out.dtype)


def sum_nt_call(terms, tile):
    rows, k = terms[0][0].shape[-2:]
    n = terms[0][2].shape[0]
    lefts, rights = [], []
    for array, slot, weight, window in terms:
        if slot is None:
            lefts.append(pl.BlockSpec((rows, k), lambda j: (0, 0)))
        else:
            lefts.append(pl.BlockSpec((1, rows, k), functools.partial(lambda slot, j: (slot, 0, 0), slot)))
        rights.append(pl.BlockSpec((tile, k), functools.partial(lambda window, j: (j, window), window)))
    count = len(terms)
    return pl.pallas_call(
        functools.partial(sum_nt_kernel, tuple(t[1] for t in terms)),
        grid=(n // tile,),
        in_specs=lefts + rights,
        out_specs=pl.BlockSpec((rows, tile), lambda j: (0, j)),
        out_shape=jax.ShapeDtypeStruct((rows, n), BF),
        compiler_params=params(40, ("arbitrary",)),
        cost_estimate=cost(2 * rows * k * n * count, 2 * count * (rows * k + n * k) + 2 * rows * n),
        name="sum_nt",
    )(*[t[0] for t in terms], *[t[2] for t in terms])


def mlp_gram_kernel(count, *refs):
    dys, n2s = refs[:count], refs[count : 2 * count]
    hid, gu = refs[2 * count : 3 * count], refs[3 * count : 4 * count]
    out = refs[-1]

    @pl.when(pl.program_id(0) == 0)
    def _():
        acc = dot_tn(dys[0][...], hid[0][...])
        for n in range(1, count):
            acc = acc + dot_tn(dys[n][...], hid[n][...])
        out[...] = acc.astype(out.dtype)

    @pl.when(pl.program_id(0) != 0)
    def _():
        acc = dot_tn(n2s[0][...], gu[0][0])
        for n in range(1, count):
            acc = acc + dot_tn(n2s[n][...], gu[n][0])
        out[...] = acc.astype(out.dtype)


def mlp_gram_call(dys, n2s, hid, gu, tile_m):
    rows, m = dys[0].shape
    k = hid[0].shape[1]
    count = len(dys)
    return pl.pallas_call(
        functools.partial(mlp_gram_kernel, count),
        grid=(3, m // tile_m),
        in_specs=[pl.BlockSpec((rows, tile_m), lambda j, i: (0, jnp.where(j == 0, i, m // tile_m - 1)))] * count
        + [pl.BlockSpec((rows, tile_m), lambda j, i: (0, jnp.where(j == 0, 0, i)))] * count
        + [pl.BlockSpec((rows, k), lambda j, i: (0, 0))] * count
        + [pl.BlockSpec((1, rows, k), lambda j, i: (jnp.maximum(j - 1, 0), 0, 0))] * count,
        out_specs=pl.BlockSpec((tile_m, k), lambda j, i: (i, j)),
        out_shape=jax.ShapeDtypeStruct((m, 3 * k), BF),
        compiler_params=params(56, ("arbitrary", "arbitrary")),
        cost_estimate=cost(6 * rows * m * k * count, count * rows * (2 * m + 3 * k) * 2 + m * 3 * k * 2),
        name="mlp_gram",
    )(*dys, *n2s, *hid, *gu)


def split_gram_kernel(f_ref, left, right, extra, mine, theirs):
    acc = dot_tn(left[...], right[...]).astype(BF)
    rows = mine.shape[1]
    k = right.shape[1]
    side = f_ref[0] % 2

    @pl.when(side == 0)
    def _():
        mine[0, :, :k] = acc[:rows]
        theirs[0, :, :k] = acc[rows:]
        mine[0, :, k:] = extra[:rows]
        theirs[0, :, k:] = extra[rows:]

    @pl.when(side != 0)
    def _():
        mine[0, :, :k] = acc[rows:]
        theirs[0, :, :k] = acc[:rows]
        mine[0, :, k:] = extra[rows:]
        theirs[0, :, k:] = extra[:rows]


def split_gram_call(f, left, right, extra):
    tokens, m = left.shape
    k, e = right.shape[1], extra.shape[1]
    pair = m // 4
    out = pl.BlockSpec((1, pair // 2, k + e), lambda z, f: (z ^ (f[0] // 2), 0, 0))
    shape = jax.ShapeDtypeStruct((4, pair // 2, k + e), BF)
    return pl.pallas_call(
        split_gram_kernel,
        grid_spec=pltpu.PrefetchScalarGridSpec(
            num_scalar_prefetch=1,
            grid=(4,),
            in_specs=[
                pl.BlockSpec((tokens, pair), lambda z, f: (0, z)),
                pl.BlockSpec((tokens, k), lambda z, f: (0, 0)),
                pl.BlockSpec((pair, e), lambda z, f: (z, 0)),
            ],
            out_specs=[out, out],
        ),
        out_shape=[shape, shape],
        compiler_params=params(40, ("arbitrary",)),
        cost_estimate=cost(2 * tokens * m * k, tokens * (m + k) * 2 + m * k * 2),
        name="split_gram",
    )(f, left, right, extra)


def out_gram_kernel(c_ref, f_ref, m0, m1, m2, m3, dattn, out):
    side = f_ref[0] % 2
    rows = out.shape[3]
    for d, ref in enumerate((m0, m1, m2, m3)):

        @pl.when(pl.program_id(0) == d)
        def _():
            tok = ref.shape[1] * ref.shape[2]
            acc = dot_tn(ref[0].reshape(tok, ref.shape[3]), dattn[...]).astype(BF)

            @pl.when(side == 0)
            def _():
                out[0, 0, 0] = acc[:rows]
                out[0, 1, 0] = acc[rows:]

            @pl.when(side != 0)
            def _():
                out[0, 0, 0] = acc[rows:]
                out[0, 1, 0] = acc[:rows]


def out_gram_call(c, f, mixed, r1, r2, dattn):
    seqs, tok, inner_w = mixed.shape[1:]
    rows, width = dattn.shape
    quarter = width // CTX

    def slot(n):
        return pl.BlockSpec((1, seqs, tok, inner_w), lambda d, e, c, f: (n, 0, 0, 0))

    return pl.pallas_call(
        out_gram_kernel,
        grid_spec=pltpu.PrefetchScalarGridSpec(
            num_scalar_prefetch=2,
            grid=(CTX, CTX),
            in_specs=[
                slot(0),
                slot(0),
                slot(0),
                slot(1),
                pl.BlockSpec((rows, quarter), lambda d, e, c, f: (0, e ^ c[0])),
            ],
            out_specs=pl.BlockSpec(
                (1, 2, 1, inner_w // 2, quarter), lambda d, e, c, f: (e, 0, d ^ c[0] ^ (f[0] // 2), 0, 0)
            ),
        ),
        out_shape=jax.ShapeDtypeStruct((CTX, 2, 4, inner_w // 2, quarter), BF),
        compiler_params=params(40, ("arbitrary", "arbitrary")),
        cost_estimate=cost(2 * rows * width * width, width * width * 2 + rows * width * 4),
        name="out_gram",
    )(c, f, mixed, r1, r2, r2, dattn)


def unpack_kernel(c_ref, s0, s1, s2, s3, perm, o0, o1, o2, o3, gq, gk, gv, gg, go):
    c = c_ref[0]
    qw, kw = QH * HD, KH * HD
    n = perm.shape[0]
    for b in range(CTX):
        for d, (ref, out) in enumerate(((s0, o0), (s1, o1), (s2, o2), (s3, o3))):

            @pl.when((b ^ c) == d)
            def _():
                flat = dot_nt(ref[:, :n], perm[...])
                gq[:, b * qw : (b + 1) * qw] = flat[:, :qw]
                gk[:, b * kw : (b + 1) * kw] = flat[:, qw : qw + kw]
                gv[:, b * kw : (b + 1) * kw] = flat[:, qw + kw :]
                go[:, b * qw : (b + 1) * qw] = out[...].astype(F32)

    gg[...] = (
        s0[:, n:].astype(F32) + s1[:, n:].astype(F32) + s2[:, n:].astype(F32) + s3[:, n:].astype(F32)
    )


def unpack_call(c, parts, perm, outs):
    rows = parts[0].shape[0]
    extra = parts[0].shape[1] - perm.shape[0]
    vm = pl.BlockSpec(memory_space=pltpu.VMEM)
    return pl.pallas_call(
        unpack_kernel,
        in_specs=[pl.BlockSpec(memory_space=pltpu.SMEM)] + [vm] * 9,
        out_specs=[vm] * 5,
        out_shape=[
            jax.ShapeDtypeStruct((rows, H * HD), F32),
            jax.ShapeDtypeStruct((rows, KVH * HD), F32),
            jax.ShapeDtypeStruct((rows, KVH * HD), F32),
            jax.ShapeDtypeStruct((rows, extra), F32),
            jax.ShapeDtypeStruct((rows, CTX * outs[0].shape[1]), F32),
        ],
        compiler_params=pltpu.CompilerParams(vmem_limit_bytes=40 << 20),
        cost_estimate=cost(1e9, 1e7),
        name="unpack",
    )(c, *parts, perm, *outs)


def qkv_back_kernel(c_ref, g, w, out):
    out[0, 0] = dot_nt(g[...], w[...]).astype(BF)


def qkv_back_call(c, grads, w, seqs, base):
    width = w.shape[0]
    return pl.pallas_call(
        qkv_back_kernel,
        grid_spec=pltpu.PrefetchScalarGridSpec(
            num_scalar_prefetch=1,
            grid=(2, seqs),
            in_specs=[
                pl.BlockSpec((BLK, 768), lambda d, s, c: (s * CTX + ((d + base) ^ c[0]), 0)),
                pl.BlockSpec((width, 768), lambda d, s, c: (0, 0)),
            ],
            out_specs=pl.BlockSpec((1, 1, BLK, width), lambda d, s, c: (d, s, 0, 0)),
        ),
        out_shape=jax.ShapeDtypeStruct((2, seqs, BLK, width), BF),
        compiler_params=params(40, ("arbitrary", "arbitrary")),
        cost_estimate=cost(4 * seqs * BLK * 768 * width, width * 768 * 2 + 2 * seqs * BLK * (width + 768) * 2),
        name="qkv_back",
    )(c, grads, w)


def final_kernel(part_a, part_b, x, gain, dresid, out, dgain):
    dn = part_a[0].astype(F32) + part_b[0].astype(F32)
    dx, dg = rms_back(x[0].astype(F32), gain[...], dn)
    out[0] = dresid[0] + dx
    dgain[0] = jnp.broadcast_to(jnp.sum(dg, axis=0, keepdims=True), dgain.shape[1:])


def final_call(part_a, part_b, x, gain, dresid):
    seqs, tok, width = x.shape
    tile = pl.BlockSpec((1, tok, width), lambda s: (s, 0, 0))
    return pl.pallas_call(
        final_kernel,
        grid=(seqs,),
        in_specs=[tile, tile, tile, pl.BlockSpec((1, width), lambda s: (0, 0)), tile],
        out_specs=[tile, pl.BlockSpec((1, 8, width), lambda s: (s, 0, 0))],
        out_shape=[
            jax.ShapeDtypeStruct((seqs, tok, width), F32),
            jax.ShapeDtypeStruct((seqs, 8, width), F32),
        ],
        compiler_params=params(40, ("arbitrary",)),
        cost_estimate=cost(20 * seqs * tok * width, 14 * seqs * tok * width),
        name="final",
    )(part_a, part_b, x, gain, dresid)


CORE = [(i, i ^ 1) for i in range(CTX)]
ROW = [(i, i ^ 2) for i in range(CTX)]


def swap_core(x):
    return lax.ppermute(x, "context", CORE)


def swap_row(x):
    return lax.ppermute(x, "context", ROW)


def gather_blocks(x):
    far = swap_row(x)
    near = swap_core(x)
    return [x, near, far, swap_core(far)]


def after(x, *first):
    return lax.optimization_barrier((x,) + first)[0]


def swap_fsdp(x, bit):
    size = lax.axis_size("fsdp")
    return lax.ppermute(x, "fsdp", [(i, i ^ bit) for i in range(size)])


def gather_fsdp(x):
    near = swap_fsdp(x, 2)
    side = swap_fsdp(x, 1)
    far = swap_fsdp(jnp.stack([x, near]), 4)
    near_side = swap_fsdp(near, 1)
    far_side = swap_fsdp(far, 1)
    return jnp.stack([x, side, near, near_side, far[0], far_side[0], far[1], far_side[1]])


def reduce_fsdp(mine, theirs):
    a = add_low(mine, swap_fsdp(theirs, 1))
    b = add_low(a[0:2], swap_fsdp(a[2:4], 4))
    return add_low(b[0], swap_fsdp(b[1], 2))


def add_low(a, b):
    return (a.astype(F32) + b.astype(F32)).astype(BF)


def on_device(
    tokens,
    segments,
    w_query,
    w_key,
    w_value,
    w_out,
    w_gate,
    w_up,
    w_down,
    gain_attn,
    gain_mlp,
    cotangent,
):
    seqs, tok, width = tokens.shape
    rows = seqs * tok
    length = tok * CTX
    qkv_w = (QH + 2 * KH) * HD
    ctx = lax.axis_index("context")
    core = ctx % 2
    c = ctx.astype(jnp.int32).reshape(1)

    segs = gather_blocks(segments)
    xs = gather_blocks(after(tokens, *segs))
    dys = gather_blocks(after(cotangent, *xs))

    perm = pack_matrix()
    shard = jnp.concatenate(
        [
            lax.dynamic_slice_in_dim(w_query, ctx * (QH * HD), QH * HD, 1),
            lax.dynamic_slice_in_dim(w_key, ctx * (KH * HD), KH * HD, 1),
            lax.dynamic_slice_in_dim(w_value, ctx * (KH * HD), KH * HD, 1),
        ],
        axis=1,
    )
    shard = jnp.dot(shard, perm, preferred_element_type=F32).astype(BF)
    gains = jnp.pad(jnp.stack([gain_attn, gain_mlp], axis=1), ((0, 0), (0, LANES - 2)))
    shard = jnp.concatenate([shard, gains], axis=1)
    fsdp = lax.axis_index("fsdp").astype(jnp.int32).reshape(1)
    w_qkv = gather_fsdp(shard)
    down_t = jnp.transpose(w_down)
    ff = w_gate.shape[1] // 2
    w_parts = []
    for n in range(2):
        cols = slice(n * ff, (n + 1) * ff)
        part = jnp.concatenate([w_gate[:, cols], w_up[:, cols], down_t[:, cols]], axis=1)
        if n:
            part = after(part, *segs)
        w_parts.append(lax.all_gather(part, "fsdp", axis=0, tiled=True))
    gain_cols = w_qkv[:, :, qkv_w : qkv_w + 2]
    gain_cols = jnp.concatenate(
        [lax.dynamic_index_in_dim(gain_cols, b ^ fsdp[0], 0, keepdims=False) for b in range(8)], axis=0
    )
    gain_rows = jnp.transpose(gain_cols).astype(F32)
    gain_a, gain_m = gain_rows[0:1], gain_rows[1:2]
    quarter = width // CTX
    out_part = gather_fsdp(after(lax.dynamic_slice_in_dim(w_out, ctx * quarter, quarter, 1), w_qkv))
    out_parts = gather_blocks(out_part)
    w_out_full = assemble_call(c, fsdp, out_parts)

    seg_blocks = jnp.stack(segs)
    whole_seg = jnp.concatenate(
        [lax.dynamic_index_in_dim(seg_blocks, b ^ ctx, 0, keepdims=False) for b in range(CTX)], axis=1
    )
    index = jnp.arange(length, dtype=jnp.int32)
    starts = jnp.concatenate(
        [jnp.ones((seqs, 1), dtype=bool), whole_seg[:, 1:] != whole_seg[:, :-1]], axis=1
    )
    first = lax.cummax(jnp.where(starts, index[None, :], 0), axis=1)
    positions = (index[None, :] - first).astype(F32).reshape(seqs * length, 1)
    freq = np.zeros((LANES,), np.float32)
    base = (THETA ** -(np.arange(HALF, dtype=np.float64) * 2.0 / HD)).astype(np.float32)
    for g in range(KH):
        freq[g * HALF : (g + 1) * HALF] = base
    angles = positions * jnp.asarray(freq)[None, :]
    cos, sin = jnp.cos(angles), jnp.sin(angles)
    low_block = (first[:, ::BLK] // BLK).reshape(seqs * CTX).astype(jnp.int32)
    first_rows = first.reshape(seqs, CTX, 1, BLK)

    normed, q, k, v, w_packed = qkv_call(c, fsdp, xs, gain_a, w_qkv, cos, sin)
    mixed, lse = attend_call(c, low_block, q, k, v, first_rows, seqs, length)
    r1 = swap_core(jnp.stack([mixed[1], mixed[3]]))
    r2 = swap_row(jnp.stack([mixed[2], r1[1]]))
    resid, normed_two = out_call(c, tokens, mixed, r1, r2, w_out_full, gain_m)

    n2s = [n.reshape(rows, width) for n in gather_blocks(normed_two)]
    dys = [d.reshape(rows, width) for d in dys]
    hiddens, grads, shares = [], [], []
    for w in w_parts:
        pairs = [mlp_call(n2s[d], dys[d], w) for d in range(CTX)]
        hiddens.append([p[0] for p in pairs])
        grads.append([p[1] for p in pairs])
        gram = mlp_gram_call(dys, n2s, hiddens[-1], grads[-1], 512)
        shares.append(gram)

    def back_rows(d):
        terms = [(grads[n][d], slot, w_parts[n], slot) for n in range(2) for slot in range(2)]
        return sum_nt_call(terms, 512)

    def down_rows(d):
        return sum_nt_call([(hiddens[n][d], None, w_parts[n], 2) for n in range(2)], 512)

    dn3, dn2, dn1, dn0 = [back_rows(d) for d in (3, 2, 1, 0)]
    dn2 = add_low(dn2, swap_core(dn3))
    dn_b = swap_row(dn2)
    dn_a = add_low(dn0, swap_core(dn1))
    s_one = lax.psum_scatter(shares[0], "fsdp", scatter_dimension=0, tiled=True)
    s_two = lax.psum_scatter(after(shares[1], s_one), "fsdp", scatter_dimension=0, tiled=True)
    dn_b = after(dn_b, dn_a, *shares)
    dresid, dattn, dmixed, dgain_m = out_back_call(
        c, dn_a.reshape(tokens.shape), dn_b.reshape(tokens.shape), resid, gain_m, cotangent, w_out_full
    )

    b1 = swap_core(jnp.stack([dmixed[1], dmixed[3]]))
    b2 = swap_row(jnp.stack([dmixed[2], b1[1]]))
    g_out = out_gram_call(c, fsdp, mixed, r1, r2, dattn.reshape(rows, width))
    got = swap_core(jnp.stack([g_out[1], g_out[3]]))
    downs = [down_rows(d) for d in range(CTX)]
    down2 = add_low(downs[2], swap_core(downs[3]))
    down_b = swap_row(down2)
    down_a = add_low(downs[0], swap_core(downs[1]))
    got_row = swap_row(add_low(g_out[2], got[1]))
    g_out = add_low(add_low(g_out[0], got[0]), got_row)
    b2 = after(b2, down2, down_a, s_one)
    dqkv = attend_back_call(
        c, low_block, q, k, v, mixed, dmixed, b1[0], b2, lse, first_rows, cos, sin, seqs, length
    )
    s_out = reduce_fsdp(g_out[0], g_out[1])

    far = qkv_back_call(c, dqkv, w_packed, seqs, 2)
    dx2 = add_low(far[0], swap_core(far[1]))
    dx_b = swap_row(dx2)
    gain_m_col = jnp.pad(jnp.sum(dgain_m[:, 0], axis=0)[:, None], ((0, 0), (1, LANES - 2)))
    near = qkv_back_call(c, after(dqkv, dx2), w_packed, seqs, 0)
    dx_a = add_low(near[0], swap_core(near[1]))
    output = (
        resid + down_a.astype(F32).reshape(resid.shape) + down_b.astype(F32).reshape(resid.shape)
    ).astype(BF)
    grad_tokens, dgain_a = final_call(dx_a, after(dx_b, s_two), tokens, gain_a, dresid)
    gain_grads = jnp.pad(jnp.sum(dgain_a[:, 0], axis=0)[:, None], ((0, 0), (0, LANES - 1))) + gain_m_col
    s_qkv = reduce_fsdp(*split_gram_call(fsdp, normed, dqkv, gain_grads.astype(BF)))
    g_query, g_key, g_value, g_gain, g_w_out = unpack_call(
        c, gather_blocks(s_qkv), perm, gather_blocks(s_out)
    )
    return (
        output,
        grad_tokens,
        g_query,
        g_key,
        g_value,
        g_w_out,
        jnp.concatenate([s[:, ff : 2 * ff] for s in (s_one, s_two)], axis=1).astype(F32),
        jnp.concatenate([s[:, 2 * ff :] for s in (s_one, s_two)], axis=1).astype(F32),
        jnp.transpose(jnp.concatenate([s[:, :ff] for s in (s_one, s_two)], axis=1)).astype(F32),
        g_gain[:, 0],
        g_gain[:, 1],
    )


def solution(mesh):
    split_heads = mesh.shape["context"] == CTX
    return jax.shard_map(
        on_device if split_heads else on_device_general,
        mesh=mesh,
        in_specs=(
            P("fsdp", "context", None),
            P("fsdp", "context"),
            P("fsdp", None),
            P("fsdp", None),
            P("fsdp", None),
            P("fsdp", None),
            P("fsdp", "context"),
            P("fsdp", "context"),
            P("context", "fsdp"),
            P("fsdp"),
            P("fsdp"),
            P("fsdp", "context", None),
        ),
        out_specs=(
            P("fsdp", "context", None),
            P("fsdp", "context", None),
            P("fsdp", None),
            P("fsdp", None),
            P("fsdp", None),
            P("fsdp", None),
            P("fsdp", "context"),
            P("fsdp", "context"),
            P("context", "fsdp"),
            P("fsdp"),
            P("fsdp"),
        ),
        check_vma=False,
    )
```

```python
import functools
import math

import jax
import jax.numpy as jnp
import numpy as np
from jax import lax
from jax.experimental import pallas as pl
from jax.experimental.pallas import tpu as pltpu
from jax.sharding import PartitionSpec as P

H = 16
KVH = 8
HD = 96


EPSILON = 1e-05
THETA = 100000.0


def rms_scale(values, gain):
    return values * lax.rsqrt(jnp.mean(values * values, axis=-1, keepdims=True) + EPSILON) * gain


def rotate(values, cosines, sines):
    half_width = values.shape[-1] // 2
    leading = values[..., :half_width]
    trailing = values[..., half_width:]
    return jnp.concatenate(
        [leading * cosines - trailing * sines, trailing * cosines + leading * sines], axis=-1
    )


def gated(gate_act, up_act):
    return jax.nn.silu(gate_act) * up_act


def inner(left, right):
    return jnp.einsum("ti,tj->ij", left, right, preferred_element_type=jnp.float32)


def outer_back(grad_rows, weight):
    return jnp.einsum("ti,ji->tj", grad_rows, weight, preferred_element_type=jnp.float32)


def reduce_grads(parts):
    shares = (
        lax.psum_scatter(
            parts[0].astype(jnp.bfloat16), "fsdp", scatter_dimension=0, tiled=True
        ).astype(jnp.float32),
        lax.psum_scatter(
            parts[1].astype(jnp.bfloat16), "fsdp", scatter_dimension=0, tiled=True
        ).astype(jnp.float32),
        lax.psum_scatter(
            parts[2].astype(jnp.bfloat16), "fsdp", scatter_dimension=0, tiled=True
        ).astype(jnp.float32),
        lax.psum_scatter(
            parts[3].astype(jnp.bfloat16), "fsdp", scatter_dimension=0, tiled=True
        ).astype(jnp.float32),
        lax.psum_scatter(
            parts[4].astype(jnp.bfloat16), "fsdp", scatter_dimension=0, tiled=True
        ).astype(jnp.float32),
        lax.psum_scatter(
            parts[5].astype(jnp.bfloat16), "fsdp", scatter_dimension=0, tiled=True
        ).astype(jnp.float32),
    )
    result = (
        lax.psum(shares[0].astype(jnp.bfloat16), "context").astype(jnp.float32),
        lax.psum(shares[1].astype(jnp.bfloat16), "context").astype(jnp.float32),
        lax.psum(shares[2].astype(jnp.bfloat16), "context").astype(jnp.float32),
        lax.psum(shares[3].astype(jnp.bfloat16), "context").astype(jnp.float32),
        lax.psum(shares[4].astype(jnp.bfloat16), "context").astype(jnp.float32),
        lax.psum(shares[5].astype(jnp.bfloat16), "context").astype(jnp.float32),
    )
    return result


def gather_attention(shard_query, shard_key, shard_value, shard_out, shard_gain_a, shard_gain_m):
    return (
        lax.all_gather(shard_query, "fsdp", axis=0, tiled=True),
        lax.all_gather(shard_key, "fsdp", axis=0, tiled=True),
        lax.all_gather(shard_value, "fsdp", axis=0, tiled=True),
        lax.all_gather(shard_out, "fsdp", axis=0, tiled=True),
        lax.all_gather(shard_gain_a, "fsdp", axis=0, tiled=True),
        lax.all_gather(shard_gain_m, "fsdp", axis=0, tiled=True),
    )


def gather_mlp(shard_gate, shard_up, shard_down):
    return (
        lax.all_gather(shard_gate, "fsdp", axis=0, tiled=True),
        lax.all_gather(shard_up, "fsdp", axis=0, tiled=True),
        lax.all_gather(shard_down, "fsdp", axis=1, tiled=True),
    )


def on_device_general(
    tokens,
    segments,
    w_query,
    w_key,
    w_value,
    w_out,
    w_gate,
    w_up,
    w_down,
    gain_attn,
    gain_mlp,
    cotangent,
):
    seq_count, tok_local, model_width = tokens.shape
    row_count = seq_count * tok_local
    groups = H // KVH
    kv_width = KVH * HD
    logit_scale = 1.0 / math.sqrt(HD)
    whole_seg = lax.all_gather(segments, "context", axis=1, tiled=True)
    length = whole_seg.shape[1]
    all_rows = seq_count * length
    offset = lax.axis_index("context") * tok_local
    key_index = jnp.arange(length, dtype=jnp.int32)
    query_index = offset + jnp.arange(tok_local, dtype=jnp.int32)
    starts = jnp.concatenate(
        [jnp.ones((seq_count, 1), dtype=bool), whole_seg[:, 1:] != whole_seg[:, :-1]], axis=1
    )
    first_index = lax.cummax(jnp.where(starts, key_index[None, :], 0), axis=1)
    positions = lax.dynamic_slice_in_dim(key_index[None, :] - first_index, offset, tok_local, 1)
    frequency = jnp.power(THETA, -(jnp.arange(HD // 2, dtype=jnp.float32) * 2.0 / HD))
    angles = positions.astype(jnp.float32)[:, :, None] * frequency[None, None, :]
    cosines = jnp.cos(angles).reshape(row_count, 1, HD // 2)
    sines = jnp.sin(angles).reshape(row_count, 1, HD // 2)
    x_flat = tokens.reshape(row_count, model_width).astype(jnp.float32)

    def masked_scores(query_sequence, k_seq, q_seg, k_seg):
        unscaled_scores = (
            jnp.einsum(
                "wxif,axf->xiwa",
                query_sequence,
                k_seq.reshape(length, KVH, HD),
                preferred_element_type=jnp.float32,
            )
            * logit_scale
        )
        allowed = (q_seg[:, None] == k_seg[None, :]) & (key_index[None, :] <= query_index[:, None])
        return jnp.where(allowed[None, None], unscaled_scores, -1e30)

    def attend(items):
        query_sequence, k_seq, v_seq, q_seg, k_seg = items
        scores = masked_scores(query_sequence, k_seq, q_seg, k_seg)
        top_score = jnp.max(scores, axis=-1, keepdims=True)
        weights = jnp.exp(scores - top_score)
        total = jnp.sum(weights, axis=-1, keepdims=True)
        attention_probabilities = (weights / total).astype(jnp.bfloat16)
        mixed_seq = jnp.einsum(
            "uvqe,eua->quva",
            attention_probabilities,
            v_seq.reshape(length, KVH, HD),
            preferred_element_type=jnp.float32,
        ).astype(jnp.bfloat16)
        return (mixed_seq, top_score + jnp.log(total))

    def forward(attn_weights, mlp_weights):
        full_query, full_key, full_value, full_out, full_gain_a, full_gain_m = attn_weights
        normed = rms_scale(x_flat, full_gain_a.astype(jnp.float32)).astype(jnp.bfloat16)
        queries = jnp.dot(normed, full_query, preferred_element_type=jnp.float32).reshape(
            row_count, H, HD
        )
        key_rows = jnp.dot(normed, full_key, preferred_element_type=jnp.float32).reshape(
            row_count, KVH, HD
        )
        value_matrix_rows = jnp.dot(normed, full_value, preferred_element_type=jnp.float32).astype(
            jnp.bfloat16
        )
        qrot = (
            rotate(queries, cosines, sines)
            .astype(jnp.bfloat16)
            .reshape(seq_count, tok_local, KVH, groups, HD)
        )
        rotary_keys = (
            rotate(key_rows, cosines, sines)
            .astype(jnp.bfloat16)
            .reshape(seq_count, tok_local, kv_width)
        )
        all_keys, all_values = (
            lax.all_gather(rotary_keys, "context", axis=1, tiled=True),
            lax.all_gather(
                value_matrix_rows.reshape(seq_count, tok_local, kv_width),
                "context",
                axis=1,
                tiled=True,
            ),
        )
        mixed, log_totals = lax.map(attend, (qrot, all_keys, all_values, segments, whole_seg))
        mixed_flat = mixed.reshape(row_count, H * HD)
        resid = x_flat + jnp.dot(mixed_flat, full_out, preferred_element_type=jnp.float32)
        full_gate, full_up, full_down = mlp_weights
        normed_two = rms_scale(resid, full_gain_m.astype(jnp.float32)).astype(jnp.bfloat16)
        all_normed_two = lax.all_gather(
            normed_two.reshape(seq_count, tok_local, model_width), "context", axis=1, tiled=True
        ).reshape(all_rows, model_width)
        gate_act = jnp.dot(all_normed_two, full_gate, preferred_element_type=jnp.float32)
        up_act = jnp.dot(all_normed_two, full_up, preferred_element_type=jnp.float32)
        hidden = gated(gate_act, up_act).astype(jnp.bfloat16)
        partial_down = jnp.dot(hidden, full_down, preferred_element_type=jnp.float32)
        down_sum = (
            lax.psum_scatter(
                partial_down.reshape(seq_count, length, model_width).astype(jnp.bfloat16),
                "context",
                scatter_dimension=1,
                tiled=True,
            )
            .astype(jnp.float32)
            .reshape(row_count, model_width)
        )
        final = resid + down_sum
        return (
            final,
            normed,
            qrot,
            all_keys,
            all_values,
            mixed,
            log_totals,
            resid,
            all_normed_two,
            gate_act,
            up_act,
            hidden,
        )

    attn_weights = gather_attention(w_query, w_key, w_value, w_out, gain_attn, gain_mlp)
    mlp_weights = gather_mlp(w_gate, w_up, w_down)
    state = forward(attn_weights, mlp_weights)
    output = state[0].astype(jnp.bfloat16).reshape(seq_count, tok_local, model_width)
    (
        final,
        normed,
        qrot,
        all_keys,
        all_values,
        mixed,
        log_totals,
        resid,
        all_normed_two,
        gate_act,
        up_act,
        hidden,
    ) = state
    full_query, full_key, full_value, full_out, full_gain_a, full_gain_m = attn_weights
    full_gate, full_up, full_down = mlp_weights
    grad_out = cotangent.reshape(row_count, model_width)
    all_grad_out = lax.all_gather(cotangent, "context", axis=1, tiled=True).reshape(
        all_rows, model_width
    )
    grad_down_t = inner(all_grad_out, hidden)
    grad_hidden = outer_back(all_grad_out, full_down)
    gate_pull = jax.vjp(gated, gate_act, up_act)[1]
    grad_gate_f, grad_up_f = gate_pull(grad_hidden)
    grad_gate_act = grad_gate_f.astype(jnp.bfloat16)
    grad_up_act = grad_up_f.astype(jnp.bfloat16)
    grad_gate = inner(all_normed_two, grad_gate_act)
    grad_up = inner(all_normed_two, grad_up_act)
    part_normed_two = outer_back(grad_gate_act, full_gate) + outer_back(grad_up_act, full_up)
    grad_normed_two = lax.psum_scatter(
        part_normed_two.reshape(seq_count, length, model_width),
        "context",
        scatter_dimension=1,
        tiled=True,
    ).reshape(row_count, model_width)
    norm_pull = jax.vjp(rms_scale, resid, full_gain_m.astype(jnp.float32))[1]
    back_resid, grad_gain_m = norm_pull(grad_normed_two)
    mlp_shares = (
        lax.psum_scatter(
            grad_gate.astype(jnp.bfloat16), "fsdp", scatter_dimension=0, tiled=True
        ).astype(jnp.float32),
        lax.psum_scatter(
            grad_up.astype(jnp.bfloat16), "fsdp", scatter_dimension=0, tiled=True
        ).astype(jnp.float32),
        lax.psum_scatter(
            grad_down_t.astype(jnp.bfloat16), "fsdp", scatter_dimension=0, tiled=True
        ).astype(jnp.float32),
    )
    grad_resid = grad_out.astype(jnp.float32) + back_resid
    grad_attn = grad_resid.astype(jnp.bfloat16)
    mixed_flat = mixed.reshape(row_count, H * HD)
    grad_out_w = inner(mixed_flat, grad_attn)
    grad_mixed = (
        outer_back(grad_attn, full_out)
        .astype(jnp.bfloat16)
        .reshape(seq_count, tok_local, KVH, groups, HD)
    )

    def attend_back(items):
        query_sequence, k_seq, v_seq, q_seg, k_seg, log_total, grad_seq = items
        scores = masked_scores(query_sequence, k_seq, q_seg, k_seg)
        attention_probabilities = jnp.exp(scores - log_total)
        grad_probs = jnp.einsum(
            "wxif,axf->xiwa",
            grad_seq,
            v_seq.reshape(length, KVH, HD),
            preferred_element_type=jnp.float32,
        )
        weighted = jnp.sum(attention_probabilities * grad_probs, axis=-1, keepdims=True)
        score_gradient = (attention_probabilities * (grad_probs - weighted)).astype(jnp.bfloat16)
        grad_q = (
            jnp.einsum(
                "uvqe,eua->quva",
                score_gradient,
                k_seq.reshape(length, KVH, HD),
                preferred_element_type=jnp.float32,
            )
            * logit_scale
        )
        grad_k = (
            jnp.einsum(
                "jnbp,bjny->pjy", score_gradient, query_sequence, preferred_element_type=jnp.float32
            )
            * logit_scale
        )
        grad_v = jnp.einsum(
            "jnbp,bjny->pjy",
            attention_probabilities.astype(jnp.bfloat16),
            grad_seq,
            preferred_element_type=jnp.float32,
        )
        return (grad_q, grad_k.reshape(length, kv_width), grad_v.reshape(length, kv_width))

    grad_qrot, part_keys, part_values = lax.map(
        attend_back, (qrot, all_keys, all_values, segments, whole_seg, log_totals, grad_mixed)
    )
    grad_krot, grad_vals = (
        lax.psum_scatter(
            part_keys.astype(jnp.bfloat16), "context", scatter_dimension=1, tiled=True
        ).astype(jnp.float32),
        lax.psum_scatter(
            part_values.astype(jnp.bfloat16), "context", scatter_dimension=1, tiled=True
        ).astype(jnp.float32),
    )
    grad_queries = (
        rotate(grad_qrot.reshape(row_count, H, HD), cosines, -sines)
        .astype(jnp.bfloat16)
        .reshape(row_count, H * HD)
    )
    grad_keys = (
        rotate(grad_krot.reshape(row_count, KVH, HD), cosines, -sines)
        .astype(jnp.bfloat16)
        .reshape(row_count, kv_width)
    )
    grad_values = grad_vals.reshape(row_count, kv_width).astype(jnp.bfloat16)
    grad_query_w = inner(normed, grad_queries)
    grad_key_w = inner(normed, grad_keys)
    grad_value_w = inner(normed, grad_values)
    grad_normed = (
        outer_back(grad_queries, full_query)
        + outer_back(grad_keys, full_key)
        + outer_back(grad_values, full_value)
    )
    first_pull = jax.vjp(rms_scale, x_flat, full_gain_a.astype(jnp.float32))[1]
    back_input, grad_gain_a = first_pull(grad_normed)
    attn_grads = reduce_grads(
        (grad_query_w, grad_key_w, grad_value_w, grad_out_w, grad_gain_a, grad_gain_m)
    )
    grad_input = (grad_resid + back_input).reshape(seq_count, tok_local, model_width)
    return (
        output,
        grad_input,
        attn_grads[0],
        attn_grads[1],
        attn_grads[2],
        attn_grads[3],
        mlp_shares[0],
        mlp_shares[1],
        jnp.transpose(mlp_shares[2]),
        attn_grads[4],
        attn_grads[5],
    )


BF = jnp.bfloat16
F32 = jnp.float32
LANES = 128
HALF = HD // 2
NEG = -1e30
SCALE = 1.0 / math.sqrt(HD)
SCALE_LOG2 = SCALE * math.log2(math.e)
CTX = 4
QH = H // CTX
KH = KVH // CTX
BLK = 256
SHARE = 1.0
NT = (((1,), (1,)), ((), ()))
TN = (((0,), (0,)), ((), ()))


def dot_nt(a, b):
    return lax.dot_general(a, b, NT, preferred_element_type=F32)


def dot_tn(a, b):
    return lax.dot_general(a, b, TN, preferred_element_type=F32)


def dot_nn(a, b):
    return jnp.dot(a, b, preferred_element_type=F32)


def lane_iota(rows, width):
    return lax.broadcasted_iota(jnp.int32, (rows, width), 1)


def params(mb, sem):
    return pltpu.CompilerParams(vmem_limit_bytes=mb << 20, dimension_semantics=sem)


def cost(flops, nbytes, trans=0):
    return pl.CostEstimate(
        flops=int(flops * SHARE), bytes_accessed=int(nbytes * SHARE), transcendentals=int(trans * SHARE)
    )


def packed_columns():
    src = []
    for group in range(6):
        if group < 4:
            member, half = group // 2, group % 2
            for g in range(KH):
                head = 2 * g + member
                src += [head * HD + half * HALF + t for t in range(HALF)]
        else:
            half = group - 4
            for g in range(KH):
                src += [QH * HD + g * HD + half * HALF + t for t in range(HALF)]
        src += [(QH + KH) * HD + group * 32 + t for t in range(32)]
    return np.array(src, np.int32)


def pack_matrix():
    n = (QH + 2 * KH) * HD
    src = jnp.asarray(packed_columns())
    return (lax.broadcasted_iota(jnp.int32, (n, n), 0) == src[None, :]).astype(BF)


def rms_rows(x):
    return x * lax.rsqrt(jnp.mean(x * x, axis=-1, keepdims=True) + EPSILON)


def qkv_kernel(c_ref, x0, x1, x2, x3, w, cos, sin, normed, q, k, v, xs):
    for d, ref in enumerate((x0, x1, x2, x3)):

        @pl.when(pl.program_id(0) == d)
        def _():
            xs[...] = ref[0]

    n = rms_rows(xs[...].astype(F32)).astype(BF)
    normed[...] = n
    t = dot_nn(n, w[...])
    y = [t[:, LANES * p : LANES * (p + 1)] for p in range(6)]
    c, s = cos[...], sin[...]
    rot = []
    for p in range(0, 6, 2):
        rot += [y[p] * c - y[p + 1] * s, y[p + 1] * c + y[p] * s]
    for p in range(4):
        q[:, LANES * p : LANES * (p + 1)] = rot[p].astype(BF)
    for p in range(2):
        k[:, LANES * p : LANES * (p + 1)] = rot[4 + p].astype(BF)
    quarter = lane_iota(y[0].shape[0], LANES) // 32

    def place(parts):
        out = jnp.ones_like(y[0])
        for dst, p in parts:
            piece = y[p] if dst == 3 else pltpu.roll(y[p], 32 * (dst + 1), 1)
            out = jnp.where(quarter == dst, piece, out)
        return out.astype(BF)

    v[:, 0:128] = place(((0, 0), (1, 1), (2, 2), (3, 0)))
    v[:, 128:256] = place(((0, 1), (1, 2)))
    v[:, 256:384] = place(((2, 3), (3, 4)))
    v[:, 384:512] = place(((0, 5), (1, 3), (2, 4), (3, 5)))


def qkv_call(c, xs, w, cos, sin):
    seqs, tok, width = xs[0].shape
    total = seqs * CTX * tok
    cols = 768

    def own(d):
        return pl.BlockSpec(
            (1, tok, width),
            lambda i, s, c: (jnp.where(i == d, s, jnp.where(i < d, 0, seqs - 1)), 0, 0),
        )

    def rows(n):
        return pl.BlockSpec((tok, n), lambda i, s, c: (s * CTX + (i ^ c[0]), 0))

    return pl.pallas_call(
        qkv_kernel,
        grid_spec=pltpu.PrefetchScalarGridSpec(
            num_scalar_prefetch=1,
            grid=(CTX, seqs),
            in_specs=[
                own(0),
                own(1),
                own(2),
                own(3),
                pl.BlockSpec((width, cols), lambda i, s, c: (0, 0)),
                rows(LANES),
                rows(LANES),
            ],
            out_specs=[rows(width), rows(512), rows(256), rows(512)],
            scratch_shapes=[pltpu.VMEM((tok, width), BF)],
        ),
        out_shape=[
            jax.ShapeDtypeStruct((total, width), BF),
            jax.ShapeDtypeStruct((total, 512), BF),
            jax.ShapeDtypeStruct((total, 256), BF),
            jax.ShapeDtypeStruct((total, 512), BF),
        ],
        compiler_params=params(40, ("arbitrary", "arbitrary")),
        cost_estimate=cost(2 * total * width * 768, total * width * 4 + width * 768 * 2 + total * 3584),
        name="qkv",
    )(c, *xs, w, cos, sin)


def head_masks(rows):
    lane = lane_iota(rows, 256)
    inner_lane = lane % LANES
    by_kv = [inner_lane < HALF, (inner_lane >= HALF) & (inner_lane < HD)]
    in_mixed = [
        lane < HD,
        (lane >= HD) & (lane < 2 * HD),
        (lane >= 64) & (lane < 64 + HD),
        lane >= 64 + HD,
    ]
    return lane, by_kv, in_mixed


def attend_kernel(js_ref, c_ref, q, k, v, start, mixed, lse, vt_s, m_s, o_s):
    s_id, i = pl.program_id(0), pl.program_id(1)
    blocks = k.shape[0] // BLK
    lane, by_kv, in_mixed = head_masks(BLK)
    sub = lax.broadcasted_iota(jnp.int32, (256, BLK), 0)
    take_a = (sub < HD) | ((sub >= 192) & (sub < 224))
    take_b = ((sub >= 64) & (sub < 64 + HD)) | (sub < 32)
    zero = jnp.zeros((BLK, 256), BF)

    @pl.when(i == 0)
    def _():
        for b in range(blocks):
            vt_s[b] = jnp.transpose(v[b * BLK : (b + 1) * BLK, :])

    m_s[...] = jnp.full_like(m_s, -jnp.inf)
    o_s[...] = jnp.zeros_like(o_s)
    col = i * BLK + lax.broadcasted_iota(jnp.int32, (BLK, BLK), 1)
    first = start[0, 0]
    low = js_ref[s_id * CTX + i]

    def step(t, _):
        j = i - t
        kb = k[pl.ds(pl.multiple_of(j * BLK, BLK), BLK), :]
        row = j * BLK + lax.broadcasted_iota(jnp.int32, (BLK, BLK), 0)
        bias = jnp.where((row >= first) & (row <= col), 0.0, NEG)
        for win, take in enumerate((take_a, take_b)):
            vt = vt_s[j, 256 * win : 256 * (win + 1), :]
            outs, alphas = [], []
            for m in range(2):
                h = 2 * win + m
                qh = jnp.where(by_kv[win], q[:, 256 * m : 256 * (m + 1)], zero)
                sc = dot_nt(kb, qh) * SCALE_LOG2 + bias
                m_old = m_s[h : h + 1, :]
                m_new = jnp.maximum(m_old, jnp.max(sc, axis=0, keepdims=True))
                p = jnp.exp2(sc - m_new)
                alphas.append(jnp.exp2(m_old - m_new))
                m_s[h : h + 1, :] = m_new
                outs.append(dot_nn(vt, p.astype(BF)))
            o_s[win] = o_s[win] * jnp.where(take, alphas[0], alphas[1]) + jnp.where(take, outs[0], outs[1])
        return 0

    lax.fori_loop(0, i - low + 1, step, 0)
    sums = [o_s[0, 192:193, :], o_s[0, 224:225, :], o_s[1, 0:1, :], o_s[1, 32:33, :]]
    inv = [1.0 / x for x in sums]
    a = jnp.transpose(o_s[0] * jnp.where(take_a, inv[0], inv[1]))
    b = jnp.transpose(o_s[1] * jnp.where(take_b, inv[2], inv[3]))
    mixed[0, 0, :, 0:128] = a[:, 0:128].astype(BF)
    mixed[0, 0, :, 128:256] = jnp.where(lane[:, :LANES] < 64, a[:, 128:256], b[:, 0:128]).astype(BF)
    mixed[0, 0, :, 256:384] = b[:, 128:256].astype(BF)
    lse[0, 0] = jnp.zeros_like(lse[0, 0])
    for h in range(QH):
        lse[0, 0, h : h + 1, :] = m_s[h : h + 1, :] + jnp.log2(sums[h])


def attend_call(c, js, q, k, v, start, seqs, length):
    blocks = length // BLK
    return pl.pallas_call(
        attend_kernel,
        grid_spec=pltpu.PrefetchScalarGridSpec(
            num_scalar_prefetch=2,
            grid=(seqs, blocks),
            in_specs=[
                pl.BlockSpec((BLK, 512), lambda s, i, js, c: (s * CTX + i, 0)),
                pl.BlockSpec((length, 256), lambda s, i, js, c: (s, 0)),
                pl.BlockSpec((length, 512), lambda s, i, js, c: (s, 0)),
                pl.BlockSpec((1, 1, 1, BLK), lambda s, i, js, c: (s, i, 0, 0)),
            ],
            out_specs=[
                pl.BlockSpec((1, 1, BLK, QH * HD), lambda s, i, js, c: (i ^ c[0], s, 0, 0)),
                pl.BlockSpec((1, 1, 8, BLK), lambda s, i, js, c: (s, i, 0, 0)),
            ],
            scratch_shapes=[
                pltpu.VMEM((blocks, 512, BLK), BF),
                pltpu.VMEM((8, BLK), F32),
                pltpu.VMEM((2, 256, BLK), F32),
            ],
        ),
        out_shape=[
            jax.ShapeDtypeStruct((CTX, seqs, BLK, QH * HD), BF),
            jax.ShapeDtypeStruct((seqs, blocks, 8, BLK), F32),
        ],
        compiler_params=params(40, ("arbitrary", "arbitrary")),
        cost_estimate=cost(6e9, 8e6, 4e6),
        name="attend",
    )(js, c, q, k, v, start)


def attend_back_kernel(
    js_ref, c_ref, q, k, v, o, d0, d1, d23, lse, start, cos, sin, out, do_s, dl_s, kt_s, dq_s, dk_s, dv_s
):
    s_id = pl.program_id(0)
    c = c_ref[0]
    blocks = q.shape[0] // BLK
    lane, by_kv, in_mixed = head_masks(BLK)
    zero = jnp.zeros((BLK, 256), BF)
    mixed_lane = lane_iota(8, QH * HD)
    mixed_row = lax.broadcasted_iota(jnp.int32, (8, QH * HD), 0)
    picks = (mixed_lane // HD == mixed_row).astype(F32)
    for d in range(CTX):
        b = d ^ c
        rows = pl.ds(pl.multiple_of(b * BLK, BLK), BLK)
        g = d0[0, 0] if d == 0 else d1[0] if d == 1 else d23[d - 2, 0]
        do_s[rows, :] = g
        prod = g.astype(F32) * o[d, 0].astype(F32)
        dl_s[b] = lax.dot_general(
            picks, prod, NT, preferred_element_type=F32, precision=lax.Precision.HIGHEST
        )
    for b in range(blocks):
        kt_s[b] = jnp.transpose(k[b * BLK : (b + 1) * BLK, :])
    sub_in = lax.broadcasted_iota(jnp.int32, (256, BLK), 0) % LANES
    sub_kv = [sub_in < HALF, (sub_in >= HALF) & (sub_in < HD)]
    dq_s[...] = jnp.zeros_like(dq_s)
    dk_s[...] = jnp.zeros_like(dk_s)
    dv_s[...] = jnp.zeros_like(dv_s)

    def outer(i, _):
        qs = pl.ds(pl.multiple_of(i * BLK, BLK), BLK)
        col = i * BLK + lax.broadcasted_iota(jnp.int32, (BLK, BLK), 1)
        first = start[0, i]
        delta = dl_s[i]
        logs = lse[0, i]

        def step(t, _):
            j = i - t
            ks = pl.ds(pl.multiple_of(j * BLK, BLK), BLK)
            kb = k[ks, :]
            kt = kt_s[j]
            row = j * BLK + lax.broadcasted_iota(jnp.int32, (BLK, BLK), 0)
            bias = jnp.where((row >= first) & (row <= col), 0.0, NEG)
            dk = jnp.zeros((BLK, 256), F32)
            dq = [jnp.zeros((256, BLK), F32) for _ in range(2)]
            for win in range(KH):
                vb = v[ks, 256 * win : 256 * (win + 1)]
                kg = jnp.where(sub_kv[win], kt, zero)
                dv = jnp.zeros((BLK, 256), F32)
                for m in range(2):
                    h = 2 * win + m
                    qh = jnp.where(by_kv[win], q[qs, 256 * m : 256 * (m + 1)], zero)
                    do = jnp.where(in_mixed[h], do_s[qs, LANES * win : LANES * win + 256], zero)
                    sc = dot_nt(kb, qh) * SCALE_LOG2 + bias
                    p = jnp.exp2(sc - logs[h : h + 1, :])
                    dp = dot_nt(vb, do)
                    ds = (p * (dp - delta[h : h + 1, :])).astype(BF)
                    dv = dv + dot_nn(p.astype(BF), do)
                    dk = dk + dot_nn(ds, qh)
                    dq[m] = dq[m] + dot_nn(kg, ds)
                dv_s[ks, 256 * win : 256 * (win + 1)] += dv
            dk_s[ks, :] += dk
            for m in range(2):
                dq_s[i, m] += dq[m]
            return 0

        lax.fori_loop(0, i - js_ref[s_id * CTX + i] + 1, step, 0)
        return 0

    lax.fori_loop(0, blocks, outer, 0)
    head_lane = lane[:, :LANES] < HD

    def finish(i, _):
        rows = pl.ds(pl.multiple_of(i * BLK, BLK), BLK)
        cs, sn = cos[rows, :] * SCALE, sin[rows, :] * SCALE
        a0, a1 = dv_s[rows, 0:128], dv_s[rows, 128:256]
        b0, b1 = dv_s[rows, 256:384], dv_s[rows, 384:512]

        def r(x, n):
            return pltpu.roll(x, n, 1)

        pieces = [
            r(a0, 96) + a0,
            r(a0, 64) + r(a1, 96),
            r(a0, 32) + r(a1, 64),
            r(b0, 32) + r(b1, 64),
            b0 + r(b1, 32),
            r(b1, 96) + b1,
        ]
        grads = []
        for m in range(2):
            dq = jnp.transpose(dq_s[i, m])
            grads += [dq[:, 0:128], dq[:, 128:256]]
        grads += [dk_s[rows, 0:128], dk_s[rows, 128:256]]
        for p in range(0, 6, 2):
            first_half = grads[p] * cs + grads[p + 1] * sn
            second_half = grads[p + 1] * cs - grads[p] * sn
            out[rows, LANES * p : LANES * (p + 1)] = jnp.where(head_lane, first_half, pieces[p]).astype(BF)
            out[rows, LANES * (p + 1) : LANES * (p + 2)] = jnp.where(
                head_lane, second_half, pieces[p + 1]
            ).astype(BF)
        return 0

    lax.fori_loop(0, blocks, finish, 0)


def attend_back_call(c, js, q, k, v, o, d0, d1, d23, lse, start, cos, sin, seqs, length):
    blocks = length // BLK
    width = QH * HD
    return pl.pallas_call(
        attend_back_kernel,
        grid_spec=pltpu.PrefetchScalarGridSpec(
            num_scalar_prefetch=2,
            grid=(seqs,),
            in_specs=[
                pl.BlockSpec((length, 512), lambda s, js, c: (s, 0)),
                pl.BlockSpec((length, 256), lambda s, js, c: (s, 0)),
                pl.BlockSpec((length, 512), lambda s, js, c: (s, 0)),
                pl.BlockSpec((CTX, 1, BLK, width), lambda s, js, c: (0, s, 0, 0)),
                pl.BlockSpec((1, 1, BLK, width), lambda s, js, c: (0, s, 0, 0)),
                pl.BlockSpec((1, BLK, width), lambda s, js, c: (s, 0, 0)),
                pl.BlockSpec((2, 1, BLK, width), lambda s, js, c: (0, s, 0, 0)),
                pl.BlockSpec((1, blocks, 8, BLK), lambda s, js, c: (s, 0, 0, 0)),
                pl.BlockSpec((1, blocks, 1, BLK), lambda s, js, c: (s, 0, 0, 0)),
                pl.BlockSpec((length, LANES), lambda s, js, c: (s, 0)),
                pl.BlockSpec((length, LANES), lambda s, js, c: (s, 0)),
            ],
            out_specs=pl.BlockSpec((length, 768), lambda s, js, c: (s, 0)),
            scratch_shapes=[
                pltpu.VMEM((length, width), BF),
                pltpu.VMEM((blocks, 8, BLK), F32),
                pltpu.VMEM((blocks, 256, BLK), BF),
                pltpu.VMEM((blocks, 2, 256, BLK), F32),
                pltpu.VMEM((length, 256), F32),
                pltpu.VMEM((length, 512), F32),
            ],
        ),
        out_shape=jax.ShapeDtypeStruct((seqs * length, 768), BF),
        compiler_params=params(48, ("arbitrary",)),
        cost_estimate=cost(2e10, 1.2e7, 4e6),
        name="attend_back",
    )(js, c, q, k, v, o, d0, d1, d23, lse, start, cos, sin)


def assemble_kernel(c_ref, f_ref, p0, p1, p2, p3, out):
    quarter = p0.shape[-1]
    for b in range(CTX):
        for d, ref in enumerate((p0, p1, p2, p3)):

            @pl.when((b ^ c_ref[0]) == d)
            def _():
                out[:, b * quarter : (b + 1) * quarter] = ref[0]


def assemble_call(c, f, parts):
    count, rows, quarter = parts[0].shape
    part = pl.BlockSpec((1, rows, quarter), lambda b, c, f: (b ^ f[0], 0, 0))
    return pl.pallas_call(
        assemble_kernel,
        grid_spec=pltpu.PrefetchScalarGridSpec(
            num_scalar_prefetch=2,
            grid=(count,),
            in_specs=[part] * CTX,
            out_specs=pl.BlockSpec((rows, CTX * quarter), lambda b, c, f: (b, 0)),
        ),
        out_shape=jax.ShapeDtypeStruct((count * rows, CTX * quarter), BF),
        compiler_params=params(20, ("arbitrary",)),
        cost_estimate=cost(0, count * rows * quarter * 16),
        name="assemble",
    )(c, f, *parts)


def out_kernel(c_ref, x, m0, m1, m2, m3, w, resid, normed):
    c = c_ref[0]
    acc = x[0].astype(F32)
    for d, ref in enumerate((m0, m1, m2, m3)):
        rows = pl.ds(pl.multiple_of((d ^ c) * (QH * HD), QH * HD), QH * HD)
        acc = acc + dot_nn(ref[0, 0], w[rows, :])
    resid[0] = acc
    normed[0] = rms_rows(acc).astype(BF)


def out_call(c, x, mixed, r1, r2, w):
    seqs, tok, width = x.shape
    inner_w = QH * HD

    def slot(n):
        return pl.BlockSpec((1, 1, tok, inner_w), lambda s, c: (n, s, 0, 0))

    tile = pl.BlockSpec((1, tok, width), lambda s, c: (s, 0, 0))
    return pl.pallas_call(
        out_kernel,
        grid_spec=pltpu.PrefetchScalarGridSpec(
            num_scalar_prefetch=1,
            grid=(seqs,),
            in_specs=[
                tile,
                slot(0),
                slot(0),
                slot(0),
                slot(1),
                pl.BlockSpec((H * HD, width), lambda s, c: (0, 0)),
            ],
            out_specs=[tile, tile],
        ),
        out_shape=[
            jax.ShapeDtypeStruct((seqs, tok, width), F32),
            jax.ShapeDtypeStruct((seqs, tok, width), BF),
        ],
        compiler_params=params(48, ("arbitrary",)),
        cost_estimate=cost(2 * seqs * tok * width * width, width * width * 2 + seqs * tok * width * 10),
        name="out_proj",
    )(c, x, mixed, r1, r2, r2, w)


def rms_back(v, dyg):
    r = lax.rsqrt(jnp.mean(v * v, axis=-1, keepdims=True) + EPSILON)
    return r * dyg - v * (r * r * r * jnp.mean(dyg * v, axis=-1, keepdims=True))


def out_back_kernel(c_ref, part_a, part_b, resid, dy, w, dresid, dattn, dmixed):
    c = c_ref[0]
    dn = part_a[0].astype(F32) + part_b[0].astype(F32)
    total = dy[0].astype(F32) + rms_back(resid[0], dn)
    dresid[0] = total
    low = total.astype(BF)
    dattn[0] = low
    for d in range(CTX):
        rows = pl.ds(pl.multiple_of((d ^ c) * (QH * HD), QH * HD), QH * HD)
        dmixed[d, 0] = dot_nt(low, w[rows, :]).astype(BF)


def out_back_call(c, part_a, part_b, resid, dy, w):
    seqs, tok, width = dy.shape
    inner_w = QH * HD
    tile = pl.BlockSpec((1, tok, width), lambda s, c: (s, 0, 0))
    return pl.pallas_call(
        out_back_kernel,
        grid_spec=pltpu.PrefetchScalarGridSpec(
            num_scalar_prefetch=1,
            grid=(seqs,),
            in_specs=[
                tile,
                tile,
                tile,
                tile,
                pl.BlockSpec((H * HD, width), lambda s, c: (0, 0)),
            ],
            out_specs=[
                tile,
                tile,
                pl.BlockSpec((CTX, 1, tok, inner_w), lambda s, c: (0, s, 0, 0)),
            ],
        ),
        out_shape=[
            jax.ShapeDtypeStruct((seqs, tok, width), F32),
            jax.ShapeDtypeStruct((seqs, tok, width), BF),
            jax.ShapeDtypeStruct((CTX, seqs, tok, inner_w), BF),
        ],
        compiler_params=params(56, ("arbitrary",)),
        cost_estimate=cost(2 * seqs * tok * width * width, width * width * 2 + seqs * tok * width * 20),
        name="out_back",
    )(c, part_a, part_b, resid, dy, w)


def mlp_kernel(n2, dy, wg, wu, wd, hidden, grads):
    n, g_out = n2[...], dy[...]
    gate = dot_nn(n, wg[...])
    up = dot_nn(n, wu[...])
    dh = dot_nn(g_out, wd[...])
    sig = 1.0 / (1.0 + jnp.exp(-gate))
    act = gate * sig
    hidden[...] = (act * up).astype(BF)
    cols = wg.shape[1]
    grads[0] = (dh * up * (sig + act * (1.0 - sig))).astype(BF)
    grads[1] = (dh * act).astype(BF)


def mlp_call(n2, dy, w):
    rows, width = n2.shape
    ff = w.shape[1] // 3
    tile = BLK
    steps = ff // tile
    full = pl.BlockSpec((rows, width), lambda j: (0, 0))
    return pl.pallas_call(
        mlp_kernel,
        grid=(steps,),
        in_specs=[
            full,
            full,
            pl.BlockSpec((width, tile), lambda j: (0, j)),
            pl.BlockSpec((width, tile), lambda j: (0, j + steps)),
            pl.BlockSpec((width, tile), lambda j: (0, j + 2 * steps)),
        ],
        out_specs=[
            pl.BlockSpec((rows, tile), lambda j: (0, j)),
            pl.BlockSpec((2, rows, tile), lambda j: (0, 0, j)),
        ],
        out_shape=[
            jax.ShapeDtypeStruct((rows, ff), BF),
            jax.ShapeDtypeStruct((2, rows, ff), BF),
        ],
        compiler_params=params(40, ("arbitrary",)),
        cost_estimate=cost(6 * rows * width * ff, width * ff * 6 + rows * width * 4 + rows * ff * 6, rows * ff),
        name="mlp",
    )(n2, dy, w, w, w)


def sum_nt_kernel(slots, *refs):
    count = len(slots)
    out = refs[-1]
    acc = None
    for n in range(count):
        left = refs[n]
        part = dot_nt(left[0] if len(left.shape) == 3 else left[...], refs[count + n][...])
        acc = part if acc is None else acc + part
    out[...] = acc.astype(out.dtype)


def sum_nt_call(terms, tile):
    rows, k = terms[0][0].shape[-2:]
    n = terms[0][2].shape[0]
    lefts, rights = [], []
    for array, slot, weight, window in terms:
        if slot is None:
            lefts.append(pl.BlockSpec((rows, k), lambda j: (0, 0)))
        else:
            lefts.append(pl.BlockSpec((1, rows, k), functools.partial(lambda slot, j: (slot, 0, 0), slot)))
        rights.append(pl.BlockSpec((tile, k), functools.partial(lambda window, j: (j, window), window)))
    count = len(terms)
    return pl.pallas_call(
        functools.partial(sum_nt_kernel, tuple(t[1] for t in terms)),
        grid=(n // tile,),
        in_specs=lefts + rights,
        out_specs=pl.BlockSpec((rows, tile), lambda j: (0, j)),
        out_shape=jax.ShapeDtypeStruct((rows, n), BF),
        compiler_params=params(40, ("arbitrary",)),
        cost_estimate=cost(2 * rows * k * n * count, 2 * count * (rows * k + n * k) + 2 * rows * n),
        name="sum_nt",
    )(*[t[0] for t in terms], *[t[2] for t in terms])


def mlp_gram_kernel(count, *refs):
    dys, n2s = refs[:count], refs[count : 2 * count]
    hid, gu = refs[2 * count : 3 * count], refs[3 * count : 4 * count]
    out = refs[-1]

    @pl.when(pl.program_id(0) == 0)
    def _():
        acc = dot_tn(dys[0][...], hid[0][...])
        for n in range(1, count):
            acc = acc + dot_tn(dys[n][...], hid[n][...])
        out[...] = acc.astype(out.dtype)

    @pl.when(pl.program_id(0) != 0)
    def _():
        acc = dot_tn(n2s[0][...], gu[0][0])
        for n in range(1, count):
            acc = acc + dot_tn(n2s[n][...], gu[n][0])
        out[...] = acc.astype(out.dtype)


def mlp_gram_call(dys, n2s, hid, gu, tile_m):
    rows, m = dys[0].shape
    k = hid[0].shape[1]
    count = len(dys)
    return pl.pallas_call(
        functools.partial(mlp_gram_kernel, count),
        grid=(3, m // tile_m),
        in_specs=[pl.BlockSpec((rows, tile_m), lambda j, i: (0, jnp.where(j == 0, i, m // tile_m - 1)))] * count
        + [pl.BlockSpec((rows, tile_m), lambda j, i: (0, jnp.where(j == 0, 0, i)))] * count
        + [pl.BlockSpec((rows, k), lambda j, i: (0, 0))] * count
        + [pl.BlockSpec((1, rows, k), lambda j, i: (jnp.maximum(j - 1, 0), 0, 0))] * count,
        out_specs=pl.BlockSpec((tile_m, k), lambda j, i: (i, j)),
        out_shape=jax.ShapeDtypeStruct((m, 3 * k), BF),
        compiler_params=params(56, ("arbitrary", "arbitrary")),
        cost_estimate=cost(6 * rows * m * k * count, count * rows * (2 * m + 3 * k) * 2 + m * 3 * k * 2),
        name="mlp_gram",
    )(*dys, *n2s, *hid, *gu)


def gram_kernel(left, right, out):
    out[...] = dot_tn(left[...], right[...]).astype(out.dtype)


def gram_call(left, right, tile_m, tile_n):
    rows, m = left.shape
    n = right.shape[1]
    return pl.pallas_call(
        gram_kernel,
        grid=(n // tile_n, m // tile_m),
        in_specs=[
            pl.BlockSpec((rows, tile_m), lambda j, i: (0, i)),
            pl.BlockSpec((rows, tile_n), lambda j, i: (0, j)),
        ],
        out_specs=pl.BlockSpec((tile_m, tile_n), lambda j, i: (i, j)),
        out_shape=jax.ShapeDtypeStruct((m, n), BF),
        compiler_params=params(40, ("arbitrary", "arbitrary")),
        cost_estimate=cost(2 * rows * m * n, rows * (m + n) * 2 + m * n * 2),
        name="gram",
    )(left, right)


def out_gram_kernel(c_ref, f_ref, m0, m1, m2, m3, dattn, out):
    side = f_ref[0] % 2
    rows = out.shape[3]
    for d, ref in enumerate((m0, m1, m2, m3)):

        @pl.when(pl.program_id(0) == d)
        def _():
            tok = ref.shape[1] * ref.shape[2]
            acc = dot_tn(ref[0].reshape(tok, ref.shape[3]), dattn[...]).astype(BF)

            @pl.when(side == 0)
            def _():
                out[0, 0, 0] = acc[:rows]
                out[0, 1, 0] = acc[rows:]

            @pl.when(side != 0)
            def _():
                out[0, 0, 0] = acc[rows:]
                out[0, 1, 0] = acc[:rows]


def out_gram_call(c, f, mixed, r1, r2, dattn):
    seqs, tok, inner_w = mixed.shape[1:]
    rows, width = dattn.shape
    quarter = width // CTX

    def slot(n):
        return pl.BlockSpec((1, seqs, tok, inner_w), lambda d, e, c, f: (n, 0, 0, 0))

    return pl.pallas_call(
        out_gram_kernel,
        grid_spec=pltpu.PrefetchScalarGridSpec(
            num_scalar_prefetch=2,
            grid=(CTX, CTX),
            in_specs=[
                slot(0),
                slot(0),
                slot(0),
                slot(1),
                pl.BlockSpec((rows, quarter), lambda d, e, c, f: (0, e ^ c[0])),
            ],
            out_specs=pl.BlockSpec(
                (1, 2, 1, inner_w // 2, quarter), lambda d, e, c, f: (e, 0, d ^ c[0] ^ (f[0] // 2), 0, 0)
            ),
        ),
        out_shape=jax.ShapeDtypeStruct((CTX, 2, 4, inner_w // 2, quarter), BF),
        compiler_params=params(40, ("arbitrary", "arbitrary")),
        cost_estimate=cost(2 * rows * width * width, width * width * 2 + rows * width * 4),
        name="out_gram",
    )(c, f, mixed, r1, r2, r2, dattn)


def unpack_kernel(c_ref, s0, s1, s2, s3, perm, o0, o1, o2, o3, wq, wk, wv, gain, gq, gk, gv, gg, gm, go):
    c = c_ref[0]
    qw, kw = QH * HD, KH * HD
    n = perm.shape[0]
    g = gain[...]
    for b in range(CTX):
        for d, (ref, out) in enumerate(((s0, o0), (s1, o1), (s2, o2), (s3, o3))):

            @pl.when((b ^ c) == d)
            def _():
                flat = dot_nt(ref[:, :n], perm[...])
                gq[:, b * qw : (b + 1) * qw] = flat[:, :qw]
                gk[:, b * kw : (b + 1) * kw] = flat[:, qw : qw + kw]
                gv[:, b * kw : (b + 1) * kw] = flat[:, qw + kw :]
                go[:, b * qw : (b + 1) * qw] = out[...].astype(F32)

    total = jnp.zeros_like(g)
    for grad, w in ((gq, wq), (gk, wk), (gv, wv)):
        total = total + jnp.sum(grad[...] * w[...].astype(F32), axis=-1, keepdims=True)
        grad[...] = grad[...] * g
    gg[...] = total
    gm[...] = (
        s0[:, n:].astype(F32) + s1[:, n:].astype(F32) + s2[:, n:].astype(F32) + s3[:, n:].astype(F32)
    )[:, 0:1]


def unpack_call(c, parts, perm, outs, wq, wk, wv, gain):
    rows = parts[0].shape[0]
    vm = pl.BlockSpec(memory_space=pltpu.VMEM)
    return pl.pallas_call(
        unpack_kernel,
        in_specs=[pl.BlockSpec(memory_space=pltpu.SMEM)] + [vm] * 13,
        out_specs=[vm] * 6,
        out_shape=[
            jax.ShapeDtypeStruct((rows, H * HD), F32),
            jax.ShapeDtypeStruct((rows, KVH * HD), F32),
            jax.ShapeDtypeStruct((rows, KVH * HD), F32),
            jax.ShapeDtypeStruct((rows, 1), F32),
            jax.ShapeDtypeStruct((rows, 1), F32),
            jax.ShapeDtypeStruct((rows, CTX * outs[0].shape[1]), F32),
        ],
        compiler_params=pltpu.CompilerParams(vmem_limit_bytes=40 << 20),
        cost_estimate=cost(1e9, 1e7),
        name="unpack",
    )(c, *parts, perm, *outs, wq, wk, wv, gain)


def qkv_back_kernel(c_ref, g, w, out):
    out[0, 0] = dot_nt(g[...], w[...]).astype(BF)


def qkv_back_call(c, grads, w, seqs, base):
    width = w.shape[0]
    return pl.pallas_call(
        qkv_back_kernel,
        grid_spec=pltpu.PrefetchScalarGridSpec(
            num_scalar_prefetch=1,
            grid=(2, seqs),
            in_specs=[
                pl.BlockSpec((BLK, 768), lambda d, s, c: (s * CTX + ((d + base) ^ c[0]), 0)),
                pl.BlockSpec((width, 768), lambda d, s, c: (0, 0)),
            ],
            out_specs=pl.BlockSpec((1, 1, BLK, width), lambda d, s, c: (d, s, 0, 0)),
        ),
        out_shape=jax.ShapeDtypeStruct((2, seqs, BLK, width), BF),
        compiler_params=params(40, ("arbitrary", "arbitrary")),
        cost_estimate=cost(4 * seqs * BLK * 768 * width, width * 768 * 2 + 2 * seqs * BLK * (width + 768) * 2),
        name="qkv_back",
    )(c, grads, w)


def final_kernel(part_a, part_b, x, dresid, out):
    dn = part_a[0].astype(F32) + part_b[0].astype(F32)
    out[0] = dresid[0] + rms_back(x[0].astype(F32), dn)


def final_call(part_a, part_b, x, dresid):
    seqs, tok, width = x.shape
    tile = pl.BlockSpec((1, tok, width), lambda s: (s, 0, 0))
    return pl.pallas_call(
        final_kernel,
        grid=(seqs,),
        in_specs=[tile] * 4,
        out_specs=tile,
        out_shape=jax.ShapeDtypeStruct((seqs, tok, width), F32),
        compiler_params=params(40, ("arbitrary",)),
        cost_estimate=cost(20 * seqs * tok * width, 14 * seqs * tok * width),
        name="final",
    )(part_a, part_b, x, dresid)


CORE = [(i, i ^ 1) for i in range(CTX)]
ROW = [(i, i ^ 2) for i in range(CTX)]


def swap_core(x):
    return lax.ppermute(x, "context", CORE)


def swap_row(x):
    return lax.ppermute(x, "context", ROW)


def gather_blocks(x):
    far = swap_row(x)
    near = swap_core(x)
    return [x, near, far, swap_core(far)]


def after(x, *first):
    return lax.optimization_barrier((x,) + first)[0]


def swap_fsdp(x, bit):
    size = lax.axis_size("fsdp")
    return lax.ppermute(x, "fsdp", [(i, i ^ bit) for i in range(size)])


def gather_fsdp(x):
    near = swap_fsdp(x, 2)
    side = swap_fsdp(x, 1)
    far = swap_fsdp(jnp.stack([x, near]), 4)
    near_side = swap_fsdp(near, 1)
    far_side = swap_fsdp(far, 1)
    return jnp.stack([x, side, near, near_side, far[0], far_side[0], far[1], far_side[1]])


def reduce_fsdp(mine, theirs):
    a = add_low(mine, swap_fsdp(theirs, 1))
    b = add_low(a[0:2], swap_fsdp(a[2:4], 4))
    return add_low(b[0], swap_fsdp(b[1], 2))


def add_low(a, b):
    return (a.astype(F32) + b.astype(F32)).astype(BF)


def on_device(
    tokens,
    segments,
    w_query,
    w_key,
    w_value,
    w_out,
    w_gate,
    w_up,
    w_down,
    gain_attn,
    gain_mlp,
    cotangent,
):
    seqs, tok, width = tokens.shape
    rows = seqs * tok
    length = tok * CTX
    qkv_w = (QH + 2 * KH) * HD
    ctx = lax.axis_index("context")
    core = ctx % 2
    c = ctx.astype(jnp.int32).reshape(1)

    segs = gather_blocks(segments)
    xs = gather_blocks(tokens)

    perm = pack_matrix()
    fsdp = lax.axis_index("fsdp").astype(jnp.int32).reshape(1)
    col_a, col_m = gain_attn.astype(F32)[:, None], gain_mlp.astype(F32)[:, None]
    shard = jnp.concatenate(
        [
            lax.dynamic_slice_in_dim(w_query, ctx * (QH * HD), QH * HD, 1),
            lax.dynamic_slice_in_dim(w_key, ctx * (KH * HD), KH * HD, 1),
            lax.dynamic_slice_in_dim(w_value, ctx * (KH * HD), KH * HD, 1),
        ],
        axis=1,
    )
    shard = jnp.dot(shard, perm, preferred_element_type=F32)
    shard = (shard * col_a).astype(BF)
    w_qkv = lax.all_gather(shard, "fsdp", axis=0, tiled=True)
    quarter = width // CTX
    out_part = gather_fsdp(lax.dynamic_slice_in_dim(w_out, ctx * quarter, quarter, 1))
    dys = gather_blocks(after(cotangent, xs[2]))
    out_parts = gather_blocks(out_part)
    w_out_full = assemble_call(c, fsdp, out_parts)
    down_t = jnp.transpose(w_down)
    ff = w_gate.shape[1] // 2
    w_parts = []
    for n in range(2):
        cols = slice(n * ff, (n + 1) * ff)
        part = jnp.concatenate(
            [
                (w_gate[:, cols].astype(F32) * col_m).astype(BF),
                (w_up[:, cols].astype(F32) * col_m).astype(BF),
                down_t[:, cols],
            ],
            axis=1,
        )
        part = after(part, *(segs if n else [shard]))
        w_parts.append(lax.all_gather(part, "fsdp", axis=0, tiled=True))

    seg_blocks = jnp.stack(segs)
    whole_seg = jnp.concatenate(
        [lax.dynamic_index_in_dim(seg_blocks, b ^ ctx, 0, keepdims=False) for b in range(CTX)], axis=1
    )
    index = jnp.arange(length, dtype=jnp.int32)
    starts = jnp.concatenate(
        [jnp.ones((seqs, 1), dtype=bool), whole_seg[:, 1:] != whole_seg[:, :-1]], axis=1
    )
    first = lax.cummax(jnp.where(starts, index[None, :], 0), axis=1)
    positions = (index[None, :] - first).astype(F32).reshape(seqs * length, 1)
    freq = np.zeros((LANES,), np.float32)
    base = (THETA ** -(np.arange(HALF, dtype=np.float64) * 2.0 / HD)).astype(np.float32)
    for g in range(KH):
        freq[g * HALF : (g + 1) * HALF] = base
    angles = positions * jnp.asarray(freq)[None, :]
    cos, sin = jnp.cos(angles), jnp.sin(angles)
    low_block = (first[:, ::BLK] // BLK).reshape(seqs * CTX).astype(jnp.int32)
    first_rows = first.reshape(seqs, CTX, 1, BLK)

    normed, q, k, v = qkv_call(c, xs, w_qkv, cos, sin)
    mixed, lse = attend_call(c, low_block, after(q, dys[2]), k, v, first_rows, seqs, length)
    r1 = swap_core(jnp.stack([mixed[1], mixed[3]]))
    r2 = swap_row(jnp.stack([mixed[2], r1[1]]))
    resid, normed_two = out_call(c, tokens, mixed, r1, r2, w_out_full)

    n2s = [n.reshape(rows, width) for n in gather_blocks(normed_two)]
    dys = [d.reshape(rows, width) for d in dys]
    first_pairs = [mlp_call(n2s[d], dys[d], w_parts[0]) for d in (0, 1)]
    n2s[2] = after(n2s[2], first_pairs[0][0], first_pairs[1][0])
    n2s[3] = after(n2s[3], first_pairs[0][0], first_pairs[1][0])
    first_pairs += [mlp_call(n2s[d], dys[d], w_parts[0]) for d in (2, 3)]
    share_one = mlp_gram_call(dys, n2s, [p[0] for p in first_pairs], [p[1] for p in first_pairs], 768)
    s_one = lax.psum_scatter(share_one, "fsdp", scatter_dimension=0, tiled=True)
    second_pairs = [None] * CTX

    def back_rows(d):
        terms = [(pairs[d][1], slot, w, slot) for pairs, w in zip((first_pairs, second_pairs), w_parts) for slot in range(2)]
        return sum_nt_call(terms, 512)

    def down_rows(d, dep):
        halves = (after(first_pairs[d][0], dep), second_pairs[d][0])
        return sum_nt_call([(h, None, w, 2) for h, w in zip(halves, w_parts)], 512)

    n2_gate = after(n2s[3], share_one)
    for d in (3, 2):
        second_pairs[d] = mlp_call(n2_gate if d == 3 else n2s[d], dys[d], w_parts[1])
    dn2 = add_low(back_rows(2), swap_core(back_rows(3)))
    dn_b = swap_row(dn2)
    for d in (1, 0):
        second_pairs[d] = mlp_call(after(n2s[d], dn2), dys[d], w_parts[1])
    dn_a = add_low(back_rows(0), swap_core(back_rows(1)))
    share_two = mlp_gram_call(dys, n2s, [p[0] for p in second_pairs], [p[1] for p in second_pairs], 768)
    s_two = lax.psum_scatter(share_two, "fsdp", scatter_dimension=0, tiled=True)
    dn_b = after(dn_b, dn_a, share_two)
    dresid, dattn, dmixed = out_back_call(
        c, dn_a.reshape(tokens.shape), dn_b.reshape(tokens.shape), resid, cotangent, w_out_full
    )

    b1 = swap_core(jnp.stack([dmixed[1], dmixed[3]]))
    b2_send = jnp.stack([dmixed[2], b1[1]])
    b2 = swap_row(b2_send)
    g_out = out_gram_call(c, fsdp, mixed, r1, r2, after(dattn, b2_send).reshape(rows, width))
    got = swap_core(jnp.stack([g_out[1], g_out[3]]))
    g_send = add_low(g_out[2], got[1])
    got_row = swap_row(g_send)
    b2 = after(b2, g_send, s_one)
    dqkv = attend_back_call(
        c, low_block, q, k, v, mixed, dmixed, b1[0], b2, lse, first_rows, cos, sin, seqs, length
    )

    g_qkv = gram_call(normed, dqkv, 768, 768)
    dqkv_b = after(dqkv, g_qkv)
    far = qkv_back_call(c, dqkv_b, w_qkv, seqs, 2)
    dx2 = add_low(far[0], swap_core(far[1]))
    dx_b = swap_row(dx2)
    near = qkv_back_call(c, dqkv_b, w_qkv, seqs, 0)
    dx_a = add_low(near[0], swap_core(near[1]))
    g_out = add_low(add_low(g_out[0], got[0]), after(got_row, dx2))
    s_out = reduce_fsdp(g_out[0], g_out[1])
    downs = [down_rows(d, dx2) for d in range(CTX)]
    down2 = add_low(downs[2], swap_core(downs[3]))
    down_b = swap_row(down2)
    down_a = add_low(downs[0], swap_core(downs[1]))
    output = (
        resid + down_a.astype(F32).reshape(resid.shape) + down_b.astype(F32).reshape(resid.shape)
    ).astype(BF)
    grad_tokens = final_call(dx_a, after(dx_b, s_two), tokens, dresid)
    s_qkv = lax.psum_scatter(g_qkv, "fsdp", scatter_dimension=0, tiled=True)
    s_down, s_gate, s_up = [
        jnp.concatenate([s[:, n * ff : (n + 1) * ff] for s in (s_one, s_two)], axis=1).astype(F32)
        for n in range(3)
    ]
    part_m = jnp.sum(s_gate * w_gate.astype(F32) + s_up * w_up.astype(F32), axis=1, keepdims=True)
    part_m = jnp.broadcast_to(part_m, (part_m.shape[0], LANES)).astype(BF)
    g_query, g_key, g_value, g_gain_a, g_gain_m, g_w_out = unpack_call(
        c,
        gather_blocks(jnp.concatenate([s_qkv, part_m], axis=1)),
        perm,
        gather_blocks(s_out),
        w_query,
        w_key,
        w_value,
        col_a,
    )
    return (
        output,
        grad_tokens,
        g_query,
        g_key,
        g_value,
        g_w_out,
        s_gate * col_m,
        s_up * col_m,
        jnp.transpose(s_down),
        g_gain_a[:, 0],
        g_gain_m[:, 0],
    )


def solution(mesh):
    split_heads = mesh.shape["context"] == CTX
    return jax.shard_map(
        on_device if split_heads else on_device_general,
        mesh=mesh,
        in_specs=(
            P("fsdp", "context", None),
            P("fsdp", "context"),
            P("fsdp", None),
            P("fsdp", None),
            P("fsdp", None),
            P("fsdp", None),
            P("fsdp", "context"),
            P("fsdp", "context"),
            P("context", "fsdp"),
            P("fsdp"),
            P("fsdp"),
            P("fsdp", "context", None),
        ),
        out_specs=(
            P("fsdp", "context", None),
            P("fsdp", "context", None),
            P("fsdp", None),
            P("fsdp", None),
            P("fsdp", None),
            P("fsdp", None),
            P("fsdp", "context"),
            P("fsdp", "context"),
            P("context", "fsdp"),
            P("fsdp"),
            P("fsdp"),
        ),
        check_vma=False,
    )
```

```python
import functools
import math

import jax
import jax.numpy as jnp
import numpy as np
from jax import lax
from jax.experimental import pallas as pl
from jax.experimental.pallas import tpu as pltpu
from jax.sharding import PartitionSpec as P

H = 16
KVH = 8
HD = 96


EPSILON = 1e-05
THETA = 100000.0


def rms_scale(values, gain):
    return values * lax.rsqrt(jnp.mean(values * values, axis=-1, keepdims=True) + EPSILON) * gain


def rotate(values, cosines, sines):
    half_width = values.shape[-1] // 2
    leading = values[..., :half_width]
    trailing = values[..., half_width:]
    return jnp.concatenate(
        [leading * cosines - trailing * sines, trailing * cosines + leading * sines], axis=-1
    )


def gated(gate_act, up_act):
    return jax.nn.silu(gate_act) * up_act


def inner(left, right):
    return jnp.einsum("ti,tj->ij", left, right, preferred_element_type=jnp.float32)


def outer_back(grad_rows, weight):
    return jnp.einsum("ti,ji->tj", grad_rows, weight, preferred_element_type=jnp.float32)


def reduce_grads(parts):
    shares = (
        lax.psum_scatter(
            parts[0].astype(jnp.bfloat16), "fsdp", scatter_dimension=0, tiled=True
        ).astype(jnp.float32),
        lax.psum_scatter(
            parts[1].astype(jnp.bfloat16), "fsdp", scatter_dimension=0, tiled=True
        ).astype(jnp.float32),
        lax.psum_scatter(
            parts[2].astype(jnp.bfloat16), "fsdp", scatter_dimension=0, tiled=True
        ).astype(jnp.float32),
        lax.psum_scatter(
            parts[3].astype(jnp.bfloat16), "fsdp", scatter_dimension=0, tiled=True
        ).astype(jnp.float32),
        lax.psum_scatter(
            parts[4].astype(jnp.bfloat16), "fsdp", scatter_dimension=0, tiled=True
        ).astype(jnp.float32),
        lax.psum_scatter(
            parts[5].astype(jnp.bfloat16), "fsdp", scatter_dimension=0, tiled=True
        ).astype(jnp.float32),
    )
    result = (
        lax.psum(shares[0].astype(jnp.bfloat16), "context").astype(jnp.float32),
        lax.psum(shares[1].astype(jnp.bfloat16), "context").astype(jnp.float32),
        lax.psum(shares[2].astype(jnp.bfloat16), "context").astype(jnp.float32),
        lax.psum(shares[3].astype(jnp.bfloat16), "context").astype(jnp.float32),
        lax.psum(shares[4].astype(jnp.bfloat16), "context").astype(jnp.float32),
        lax.psum(shares[5].astype(jnp.bfloat16), "context").astype(jnp.float32),
    )
    return result


def gather_attention(shard_query, shard_key, shard_value, shard_out, shard_gain_a, shard_gain_m):
    return (
        lax.all_gather(shard_query, "fsdp", axis=0, tiled=True),
        lax.all_gather(shard_key, "fsdp", axis=0, tiled=True),
        lax.all_gather(shard_value, "fsdp", axis=0, tiled=True),
        lax.all_gather(shard_out, "fsdp", axis=0, tiled=True),
        lax.all_gather(shard_gain_a, "fsdp", axis=0, tiled=True),
        lax.all_gather(shard_gain_m, "fsdp", axis=0, tiled=True),
    )


def gather_mlp(shard_gate, shard_up, shard_down):
    return (
        lax.all_gather(shard_gate, "fsdp", axis=0, tiled=True),
        lax.all_gather(shard_up, "fsdp", axis=0, tiled=True),
        lax.all_gather(shard_down, "fsdp", axis=1, tiled=True),
    )


def on_device_general(
    tokens,
    segments,
    w_query,
    w_key,
    w_value,
    w_out,
    w_gate,
    w_up,
    w_down,
    gain_attn,
    gain_mlp,
    cotangent,
):
    seq_count, tok_local, model_width = tokens.shape
    row_count = seq_count * tok_local
    groups = H // KVH
    kv_width = KVH * HD
    logit_scale = 1.0 / math.sqrt(HD)
    whole_seg = lax.all_gather(segments, "context", axis=1, tiled=True)
    length = whole_seg.shape[1]
    all_rows = seq_count * length
    offset = lax.axis_index("context") * tok_local
    key_index = jnp.arange(length, dtype=jnp.int32)
    query_index = offset + jnp.arange(tok_local, dtype=jnp.int32)
    starts = jnp.concatenate(
        [jnp.ones((seq_count, 1), dtype=bool), whole_seg[:, 1:] != whole_seg[:, :-1]], axis=1
    )
    first_index = lax.cummax(jnp.where(starts, key_index[None, :], 0), axis=1)
    positions = lax.dynamic_slice_in_dim(key_index[None, :] - first_index, offset, tok_local, 1)
    frequency = jnp.power(THETA, -(jnp.arange(HD // 2, dtype=jnp.float32) * 2.0 / HD))
    angles = positions.astype(jnp.float32)[:, :, None] * frequency[None, None, :]
    cosines = jnp.cos(angles).reshape(row_count, 1, HD // 2)
    sines = jnp.sin(angles).reshape(row_count, 1, HD // 2)
    x_flat = tokens.reshape(row_count, model_width).astype(jnp.float32)

    def masked_scores(query_sequence, k_seq, q_seg, k_seg):
        unscaled_scores = (
            jnp.einsum(
                "wxif,axf->xiwa",
                query_sequence,
                k_seq.reshape(length, KVH, HD),
                preferred_element_type=jnp.float32,
            )
            * logit_scale
        )
        allowed = (q_seg[:, None] == k_seg[None, :]) & (key_index[None, :] <= query_index[:, None])
        return jnp.where(allowed[None, None], unscaled_scores, -1e30)

    def attend(items):
        query_sequence, k_seq, v_seq, q_seg, k_seg = items
        scores = masked_scores(query_sequence, k_seq, q_seg, k_seg)
        top_score = jnp.max(scores, axis=-1, keepdims=True)
        weights = jnp.exp(scores - top_score)
        total = jnp.sum(weights, axis=-1, keepdims=True)
        attention_probabilities = (weights / total).astype(jnp.bfloat16)
        mixed_seq = jnp.einsum(
            "uvqe,eua->quva",
            attention_probabilities,
            v_seq.reshape(length, KVH, HD),
            preferred_element_type=jnp.float32,
        ).astype(jnp.bfloat16)
        return (mixed_seq, top_score + jnp.log(total))

    def forward(attn_weights, mlp_weights):
        full_query, full_key, full_value, full_out, full_gain_a, full_gain_m = attn_weights
        normed = rms_scale(x_flat, full_gain_a.astype(jnp.float32)).astype(jnp.bfloat16)
        queries = jnp.dot(normed, full_query, preferred_element_type=jnp.float32).reshape(
            row_count, H, HD
        )
        key_rows = jnp.dot(normed, full_key, preferred_element_type=jnp.float32).reshape(
            row_count, KVH, HD
        )
        value_matrix_rows = jnp.dot(normed, full_value, preferred_element_type=jnp.float32).astype(
            jnp.bfloat16
        )
        qrot = (
            rotate(queries, cosines, sines)
            .astype(jnp.bfloat16)
            .reshape(seq_count, tok_local, KVH, groups, HD)
        )
        rotary_keys = (
            rotate(key_rows, cosines, sines)
            .astype(jnp.bfloat16)
            .reshape(seq_count, tok_local, kv_width)
        )
        all_keys, all_values = (
            lax.all_gather(rotary_keys, "context", axis=1, tiled=True),
            lax.all_gather(
                value_matrix_rows.reshape(seq_count, tok_local, kv_width),
                "context",
                axis=1,
                tiled=True,
            ),
        )
        mixed, log_totals = lax.map(attend, (qrot, all_keys, all_values, segments, whole_seg))
        mixed_flat = mixed.reshape(row_count, H * HD)
        resid = x_flat + jnp.dot(mixed_flat, full_out, preferred_element_type=jnp.float32)
        full_gate, full_up, full_down = mlp_weights
        normed_two = rms_scale(resid, full_gain_m.astype(jnp.float32)).astype(jnp.bfloat16)
        all_normed_two = lax.all_gather(
            normed_two.reshape(seq_count, tok_local, model_width), "context", axis=1, tiled=True
        ).reshape(all_rows, model_width)
        gate_act = jnp.dot(all_normed_two, full_gate, preferred_element_type=jnp.float32)
        up_act = jnp.dot(all_normed_two, full_up, preferred_element_type=jnp.float32)
        hidden = gated(gate_act, up_act).astype(jnp.bfloat16)
        partial_down = jnp.dot(hidden, full_down, preferred_element_type=jnp.float32)
        down_sum = (
            lax.psum_scatter(
                partial_down.reshape(seq_count, length, model_width).astype(jnp.bfloat16),
                "context",
                scatter_dimension=1,
                tiled=True,
            )
            .astype(jnp.float32)
            .reshape(row_count, model_width)
        )
        final = resid + down_sum
        return (
            final,
            normed,
            qrot,
            all_keys,
            all_values,
            mixed,
            log_totals,
            resid,
            all_normed_two,
            gate_act,
            up_act,
            hidden,
        )

    attn_weights = gather_attention(w_query, w_key, w_value, w_out, gain_attn, gain_mlp)
    mlp_weights = gather_mlp(w_gate, w_up, w_down)
    state = forward(attn_weights, mlp_weights)
    output = state[0].astype(jnp.bfloat16).reshape(seq_count, tok_local, model_width)
    (
        final,
        normed,
        qrot,
        all_keys,
        all_values,
        mixed,
        log_totals,
        resid,
        all_normed_two,
        gate_act,
        up_act,
        hidden,
    ) = state
    full_query, full_key, full_value, full_out, full_gain_a, full_gain_m = attn_weights
    full_gate, full_up, full_down = mlp_weights
    grad_out = cotangent.reshape(row_count, model_width)
    all_grad_out = lax.all_gather(cotangent, "context", axis=1, tiled=True).reshape(
        all_rows, model_width
    )
    grad_down_t = inner(all_grad_out, hidden)
    grad_hidden = outer_back(all_grad_out, full_down)
    gate_pull = jax.vjp(gated, gate_act, up_act)[1]
    grad_gate_f, grad_up_f = gate_pull(grad_hidden)
    grad_gate_act = grad_gate_f.astype(jnp.bfloat16)
    grad_up_act = grad_up_f.astype(jnp.bfloat16)
    grad_gate = inner(all_normed_two, grad_gate_act)
    grad_up = inner(all_normed_two, grad_up_act)
    part_normed_two = outer_back(grad_gate_act, full_gate) + outer_back(grad_up_act, full_up)
    grad_normed_two = lax.psum_scatter(
        part_normed_two.reshape(seq_count, length, model_width),
        "context",
        scatter_dimension=1,
        tiled=True,
    ).reshape(row_count, model_width)
    norm_pull = jax.vjp(rms_scale, resid, full_gain_m.astype(jnp.float32))[1]
    back_resid, grad_gain_m = norm_pull(grad_normed_two)
    mlp_shares = (
        lax.psum_scatter(
            grad_gate.astype(jnp.bfloat16), "fsdp", scatter_dimension=0, tiled=True
        ).astype(jnp.float32),
        lax.psum_scatter(
            grad_up.astype(jnp.bfloat16), "fsdp", scatter_dimension=0, tiled=True
        ).astype(jnp.float32),
        lax.psum_scatter(
            grad_down_t.astype(jnp.bfloat16), "fsdp", scatter_dimension=0, tiled=True
        ).astype(jnp.float32),
    )
    grad_resid = grad_out.astype(jnp.float32) + back_resid
    grad_attn = grad_resid.astype(jnp.bfloat16)
    mixed_flat = mixed.reshape(row_count, H * HD)
    grad_out_w = inner(mixed_flat, grad_attn)
    grad_mixed = (
        outer_back(grad_attn, full_out)
        .astype(jnp.bfloat16)
        .reshape(seq_count, tok_local, KVH, groups, HD)
    )

    def attend_back(items):
        query_sequence, k_seq, v_seq, q_seg, k_seg, log_total, grad_seq = items
        scores = masked_scores(query_sequence, k_seq, q_seg, k_seg)
        attention_probabilities = jnp.exp(scores - log_total)
        grad_probs = jnp.einsum(
            "wxif,axf->xiwa",
            grad_seq,
            v_seq.reshape(length, KVH, HD),
            preferred_element_type=jnp.float32,
        )
        weighted = jnp.sum(attention_probabilities * grad_probs, axis=-1, keepdims=True)
        score_gradient = (attention_probabilities * (grad_probs - weighted)).astype(jnp.bfloat16)
        grad_q = (
            jnp.einsum(
                "uvqe,eua->quva",
                score_gradient,
                k_seq.reshape(length, KVH, HD),
                preferred_element_type=jnp.float32,
            )
            * logit_scale
        )
        grad_k = (
            jnp.einsum(
                "jnbp,bjny->pjy", score_gradient, query_sequence, preferred_element_type=jnp.float32
            )
            * logit_scale
        )
        grad_v = jnp.einsum(
            "jnbp,bjny->pjy",
            attention_probabilities.astype(jnp.bfloat16),
            grad_seq,
            preferred_element_type=jnp.float32,
        )
        return (grad_q, grad_k.reshape(length, kv_width), grad_v.reshape(length, kv_width))

    grad_qrot, part_keys, part_values = lax.map(
        attend_back, (qrot, all_keys, all_values, segments, whole_seg, log_totals, grad_mixed)
    )
    grad_krot, grad_vals = (
        lax.psum_scatter(
            part_keys.astype(jnp.bfloat16), "context", scatter_dimension=1, tiled=True
        ).astype(jnp.float32),
        lax.psum_scatter(
            part_values.astype(jnp.bfloat16), "context", scatter_dimension=1, tiled=True
        ).astype(jnp.float32),
    )
    grad_queries = (
        rotate(grad_qrot.reshape(row_count, H, HD), cosines, -sines)
        .astype(jnp.bfloat16)
        .reshape(row_count, H * HD)
    )
    grad_keys = (
        rotate(grad_krot.reshape(row_count, KVH, HD), cosines, -sines)
        .astype(jnp.bfloat16)
        .reshape(row_count, kv_width)
    )
    grad_values = grad_vals.reshape(row_count, kv_width).astype(jnp.bfloat16)
    grad_query_w = inner(normed, grad_queries)
    grad_key_w = inner(normed, grad_keys)
    grad_value_w = inner(normed, grad_values)
    grad_normed = (
        outer_back(grad_queries, full_query)
        + outer_back(grad_keys, full_key)
        + outer_back(grad_values, full_value)
    )
    first_pull = jax.vjp(rms_scale, x_flat, full_gain_a.astype(jnp.float32))[1]
    back_input, grad_gain_a = first_pull(grad_normed)
    attn_grads = reduce_grads(
        (grad_query_w, grad_key_w, grad_value_w, grad_out_w, grad_gain_a, grad_gain_m)
    )
    grad_input = (grad_resid + back_input).reshape(seq_count, tok_local, model_width)
    return (
        output,
        grad_input,
        attn_grads[0],
        attn_grads[1],
        attn_grads[2],
        attn_grads[3],
        mlp_shares[0],
        mlp_shares[1],
        jnp.transpose(mlp_shares[2]),
        attn_grads[4],
        attn_grads[5],
    )


BF = jnp.bfloat16
F32 = jnp.float32
LANES = 128
HALF = HD // 2
NEG = -1e30
SCALE = 1.0 / math.sqrt(HD)
SCALE_LOG2 = SCALE * math.log2(math.e)
CTX = 4
QH = H // CTX
KH = KVH // CTX
BLK = 256
SHARE = 0.25
NT = (((1,), (1,)), ((), ()))
TN = (((0,), (0,)), ((), ()))


def dot_nt(a, b):
    return lax.dot_general(a, b, NT, preferred_element_type=F32)


def dot_tn(a, b):
    return lax.dot_general(a, b, TN, preferred_element_type=F32)


def dot_nn(a, b):
    return jnp.dot(a, b, preferred_element_type=F32)


def lane_iota(rows, width):
    return lax.broadcasted_iota(jnp.int32, (rows, width), 1)


def params(mb, sem):
    return pltpu.CompilerParams(vmem_limit_bytes=mb << 20, dimension_semantics=sem)


def cost(micros):
    return pl.CostEstimate(flops=int(micros * SHARE * 1.15e9), bytes_accessed=0, transcendentals=0)


def packed_columns():
    src = []
    for group in range(6):
        if group < 4:
            member, half = group // 2, group % 2
            for g in range(KH):
                head = 2 * g + member
                src += [head * HD + half * HALF + t for t in range(HALF)]
        else:
            half = group - 4
            for g in range(KH):
                src += [QH * HD + g * HD + half * HALF + t for t in range(HALF)]
        src += [(QH + KH) * HD + group * 32 + t for t in range(32)]
    return np.array(src, np.int32)


def pack_matrix():
    n = (QH + 2 * KH) * HD
    src = jnp.asarray(packed_columns())
    return (lax.broadcasted_iota(jnp.int32, (n, n), 0) == src[None, :]).astype(BF)


def rms_rows(x):
    return x * lax.rsqrt(jnp.mean(x * x, axis=-1, keepdims=True) + EPSILON)


def qkv_kernel(c_ref, x0, x1, x2, x3, w, cos, sin, normed, q, k, v, xs):
    for d, ref in enumerate((x0, x1, x2, x3)):

        @pl.when(pl.program_id(0) == d)
        def _():
            xs[...] = ref[0]

    n = rms_rows(xs[...].astype(F32)).astype(BF)
    normed[...] = n
    t = dot_nn(n, w[...])
    y = [t[:, LANES * p : LANES * (p + 1)] for p in range(6)]
    c, s = cos[...], sin[...]
    rot = []
    for p in range(0, 6, 2):
        rot += [y[p] * c - y[p + 1] * s, y[p + 1] * c + y[p] * s]
    for p in range(4):
        q[:, LANES * p : LANES * (p + 1)] = rot[p].astype(BF)
    for p in range(2):
        k[:, LANES * p : LANES * (p + 1)] = rot[4 + p].astype(BF)
    quarter = lane_iota(y[0].shape[0], LANES) // 32

    def place(parts):
        out = jnp.ones_like(y[0])
        for dst, p in parts:
            piece = y[p] if dst == 3 else pltpu.roll(y[p], 32 * (dst + 1), 1)
            out = jnp.where(quarter == dst, piece, out)
        return out.astype(BF)

    v[:, 0:128] = place(((0, 0), (1, 1), (2, 2), (3, 0)))
    v[:, 128:256] = place(((0, 1), (1, 2)))
    v[:, 256:384] = place(((2, 3), (3, 4)))
    v[:, 384:512] = place(((0, 5), (1, 3), (2, 4), (3, 5)))


def qkv_call(c, xs, w, cos, sin):
    seqs, tok, width = xs[0].shape
    total = seqs * CTX * tok
    cols = 768

    def own(d):
        return pl.BlockSpec(
            (1, tok, width),
            lambda i, s, c: (jnp.where(i == d, s, jnp.where(i < d, 0, seqs - 1)), 0, 0),
        )

    def rows(n):
        return pl.BlockSpec((tok, n), lambda i, s, c: (s * CTX + (i ^ c[0]), 0))

    return pl.pallas_call(
        qkv_kernel,
        grid_spec=pltpu.PrefetchScalarGridSpec(
            num_scalar_prefetch=1,
            grid=(CTX, seqs),
            in_specs=[
                own(0),
                own(1),
                own(2),
                own(3),
                pl.BlockSpec((width, cols), lambda i, s, c: (0, 0)),
                rows(LANES),
                rows(LANES),
            ],
            out_specs=[rows(width), rows(512), rows(256), rows(512)],
            scratch_shapes=[pltpu.VMEM((tok, width), BF)],
        ),
        out_shape=[
            jax.ShapeDtypeStruct((total, width), BF),
            jax.ShapeDtypeStruct((total, 512), BF),
            jax.ShapeDtypeStruct((total, 256), BF),
            jax.ShapeDtypeStruct((total, 512), BF),
        ],
        compiler_params=params(40, ("arbitrary", "arbitrary")),
        cost_estimate=cost(13),
        name="qkv",
    )(c, *xs, w, cos, sin)


def head_masks(rows):
    lane = lane_iota(rows, 256)
    inner_lane = lane % LANES
    by_kv = [inner_lane < HALF, (inner_lane >= HALF) & (inner_lane < HD)]
    in_mixed = [
        lane < HD,
        (lane >= HD) & (lane < 2 * HD),
        (lane >= 64) & (lane < 64 + HD),
        lane >= 64 + HD,
    ]
    return lane, by_kv, in_mixed


def attend_kernel(js_ref, c_ref, q, k, v, start, mixed, lse, vt_s, m_s, o_s):
    s_id, i = pl.program_id(0), pl.program_id(1)
    blocks = k.shape[0] // BLK
    lane, by_kv, in_mixed = head_masks(BLK)
    sub = lax.broadcasted_iota(jnp.int32, (256, BLK), 0)
    take_a = (sub < HD) | ((sub >= 192) & (sub < 224))
    take_b = ((sub >= 64) & (sub < 64 + HD)) | (sub < 32)
    zero = jnp.zeros((BLK, 256), BF)

    @pl.when(i == 0)
    def _():
        for b in range(blocks):
            vt_s[b] = jnp.transpose(v[b * BLK : (b + 1) * BLK, :])

    m_s[...] = jnp.full_like(m_s, -jnp.inf)
    o_s[...] = jnp.zeros_like(o_s)
    col = i * BLK + lax.broadcasted_iota(jnp.int32, (BLK, BLK), 1)
    first = start[0, 0]
    low = js_ref[s_id * CTX + i]

    def step(t, _):
        j = i - t
        kb = k[pl.ds(pl.multiple_of(j * BLK, BLK), BLK), :]
        row = j * BLK + lax.broadcasted_iota(jnp.int32, (BLK, BLK), 0)
        bias = jnp.where((row >= first) & (row <= col), 0.0, NEG)
        for win, take in enumerate((take_a, take_b)):
            vt = vt_s[j, 256 * win : 256 * (win + 1), :]
            outs, alphas = [], []
            for m in range(2):
                h = 2 * win + m
                qh = jnp.where(by_kv[win], q[:, 256 * m : 256 * (m + 1)], zero)
                sc = dot_nt(kb, qh) * SCALE_LOG2 + bias
                m_old = m_s[h : h + 1, :]
                m_new = jnp.maximum(m_old, jnp.max(sc, axis=0, keepdims=True))
                p = jnp.exp2(sc - m_new)
                alphas.append(jnp.exp2(m_old - m_new))
                m_s[h : h + 1, :] = m_new
                outs.append(dot_nn(vt, p.astype(BF)))
            o_s[win] = o_s[win] * jnp.where(take, alphas[0], alphas[1]) + jnp.where(take, outs[0], outs[1])
        return 0

    lax.fori_loop(0, i - low + 1, step, 0)
    sums = [o_s[0, 192:193, :], o_s[0, 224:225, :], o_s[1, 0:1, :], o_s[1, 32:33, :]]
    inv = [1.0 / x for x in sums]
    a = jnp.transpose(o_s[0] * jnp.where(take_a, inv[0], inv[1]))
    b = jnp.transpose(o_s[1] * jnp.where(take_b, inv[2], inv[3]))
    mixed[0, 0, :, 0:128] = a[:, 0:128].astype(BF)
    mixed[0, 0, :, 128:256] = jnp.where(lane[:, :LANES] < 64, a[:, 128:256], b[:, 0:128]).astype(BF)
    mixed[0, 0, :, 256:384] = b[:, 128:256].astype(BF)
    lse[0, 0] = jnp.zeros_like(lse[0, 0])
    for h in range(QH):
        lse[0, 0, h : h + 1, :] = m_s[h : h + 1, :] + jnp.log2(sums[h])


def attend_call(c, js, q, k, v, start, seqs, length):
    blocks = length // BLK
    return pl.pallas_call(
        attend_kernel,
        grid_spec=pltpu.PrefetchScalarGridSpec(
            num_scalar_prefetch=2,
            grid=(seqs, blocks),
            in_specs=[
                pl.BlockSpec((BLK, 512), lambda s, i, js, c: (s * CTX + i, 0)),
                pl.BlockSpec((length, 256), lambda s, i, js, c: (s, 0)),
                pl.BlockSpec((length, 512), lambda s, i, js, c: (s, 0)),
                pl.BlockSpec((1, 1, 1, BLK), lambda s, i, js, c: (s, i, 0, 0)),
            ],
            out_specs=[
                pl.BlockSpec((1, 1, BLK, QH * HD), lambda s, i, js, c: (i ^ c[0], s, 0, 0)),
                pl.BlockSpec((1, 1, 8, BLK), lambda s, i, js, c: (s, i, 0, 0)),
            ],
            scratch_shapes=[
                pltpu.VMEM((blocks, 512, BLK), BF),
                pltpu.VMEM((8, BLK), F32),
                pltpu.VMEM((2, 256, BLK), F32),
            ],
        ),
        out_shape=[
            jax.ShapeDtypeStruct((CTX, seqs, BLK, QH * HD), BF),
            jax.ShapeDtypeStruct((seqs, blocks, 8, BLK), F32),
        ],
        compiler_params=params(40, ("arbitrary", "arbitrary")),
        cost_estimate=cost(18),
        name="attend",
    )(js, c, q, k, v, start)


def attend_back_kernel(
    js_ref, c_ref, q, k, v, o, d0, d1, d23, lse, start, cos, sin, out, do_s, dl_s, kt_s, dq_s, dk_s, dv_s
):
    s_id = pl.program_id(0)
    c = c_ref[0]
    blocks = q.shape[0] // BLK
    lane, by_kv, in_mixed = head_masks(BLK)
    zero = jnp.zeros((BLK, 256), BF)
    mixed_lane = lane_iota(8, QH * HD)
    mixed_row = lax.broadcasted_iota(jnp.int32, (8, QH * HD), 0)
    picks = (mixed_lane // HD == mixed_row).astype(F32)
    for d in range(CTX):
        b = d ^ c
        rows = pl.ds(pl.multiple_of(b * BLK, BLK), BLK)
        g = d0[0, 0] if d == 0 else d1[0] if d == 1 else d23[d - 2, 0]
        do_s[rows, :] = g
        prod = g.astype(F32) * o[d, 0].astype(F32)
        dl_s[b] = lax.dot_general(
            picks, prod, NT, preferred_element_type=F32, precision=lax.Precision.HIGHEST
        )
    for b in range(blocks):
        kt_s[b] = jnp.transpose(k[b * BLK : (b + 1) * BLK, :])
    sub_in = lax.broadcasted_iota(jnp.int32, (256, BLK), 0) % LANES
    sub_kv = [sub_in < HALF, (sub_in >= HALF) & (sub_in < HD)]
    dq_s[...] = jnp.zeros_like(dq_s)
    dk_s[...] = jnp.zeros_like(dk_s)
    dv_s[...] = jnp.zeros_like(dv_s)

    def outer(i, _):
        qs = pl.ds(pl.multiple_of(i * BLK, BLK), BLK)
        col = i * BLK + lax.broadcasted_iota(jnp.int32, (BLK, BLK), 1)
        first = start[0, i]
        delta = dl_s[i]
        logs = lse[0, i]

        def step(t, _):
            j = i - t
            ks = pl.ds(pl.multiple_of(j * BLK, BLK), BLK)
            kb = k[ks, :]
            kt = kt_s[j]
            row = j * BLK + lax.broadcasted_iota(jnp.int32, (BLK, BLK), 0)
            bias = jnp.where((row >= first) & (row <= col), 0.0, NEG)
            dk = jnp.zeros((BLK, 256), F32)
            dq = [jnp.zeros((256, BLK), F32) for _ in range(2)]
            for win in range(KH):
                vb = v[ks, 256 * win : 256 * (win + 1)]
                kg = jnp.where(sub_kv[win], kt, zero)
                dv = jnp.zeros((BLK, 256), F32)
                for m in range(2):
                    h = 2 * win + m
                    qh = jnp.where(by_kv[win], q[qs, 256 * m : 256 * (m + 1)], zero)
                    do = jnp.where(in_mixed[h], do_s[qs, LANES * win : LANES * win + 256], zero)
                    sc = dot_nt(kb, qh) * SCALE_LOG2 + bias
                    p = jnp.exp2(sc - logs[h : h + 1, :])
                    dp = dot_nt(vb, do)
                    ds = (p * (dp - delta[h : h + 1, :])).astype(BF)
                    dv = dv + dot_nn(p.astype(BF), do)
                    dk = dk + dot_nn(ds, qh)
                    dq[m] = dq[m] + dot_nn(kg, ds)
                dv_s[ks, 256 * win : 256 * (win + 1)] += dv
            dk_s[ks, :] += dk
            for m in range(2):
                dq_s[i, m] += dq[m]
            return 0

        lax.fori_loop(0, i - js_ref[s_id * CTX + i] + 1, step, 0)
        return 0

    lax.fori_loop(0, blocks, outer, 0)
    head_lane = lane[:, :LANES] < HD

    def finish(i, _):
        rows = pl.ds(pl.multiple_of(i * BLK, BLK), BLK)
        cs, sn = cos[rows, :] * SCALE, sin[rows, :] * SCALE
        a0, a1 = dv_s[rows, 0:128], dv_s[rows, 128:256]
        b0, b1 = dv_s[rows, 256:384], dv_s[rows, 384:512]

        def r(x, n):
            return pltpu.roll(x, n, 1)

        pieces = [
            r(a0, 96) + a0,
            r(a0, 64) + r(a1, 96),
            r(a0, 32) + r(a1, 64),
            r(b0, 32) + r(b1, 64),
            b0 + r(b1, 32),
            r(b1, 96) + b1,
        ]
        grads = []
        for m in range(2):
            dq = jnp.transpose(dq_s[i, m])
            grads += [dq[:, 0:128], dq[:, 128:256]]
        grads += [dk_s[rows, 0:128], dk_s[rows, 128:256]]
        for p in range(0, 6, 2):
            first_half = grads[p] * cs + grads[p + 1] * sn
            second_half = grads[p + 1] * cs - grads[p] * sn
            out[rows, LANES * p : LANES * (p + 1)] = jnp.where(head_lane, first_half, pieces[p]).astype(BF)
            out[rows, LANES * (p + 1) : LANES * (p + 2)] = jnp.where(
                head_lane, second_half, pieces[p + 1]
            ).astype(BF)
        return 0

    lax.fori_loop(0, blocks, finish, 0)


def attend_back_call(c, js, q, k, v, o, d0, d1, d23, lse, start, cos, sin, seqs, length):
    blocks = length // BLK
    width = QH * HD
    return pl.pallas_call(
        attend_back_kernel,
        grid_spec=pltpu.PrefetchScalarGridSpec(
            num_scalar_prefetch=2,
            grid=(seqs,),
            in_specs=[
                pl.BlockSpec((length, 512), lambda s, js, c: (s, 0)),
                pl.BlockSpec((length, 256), lambda s, js, c: (s, 0)),
                pl.BlockSpec((length, 512), lambda s, js, c: (s, 0)),
                pl.BlockSpec((CTX, 1, BLK, width), lambda s, js, c: (0, s, 0, 0)),
                pl.BlockSpec((1, 1, BLK, width), lambda s, js, c: (0, s, 0, 0)),
                pl.BlockSpec((1, BLK, width), lambda s, js, c: (s, 0, 0)),
                pl.BlockSpec((2, 1, BLK, width), lambda s, js, c: (0, s, 0, 0)),
                pl.BlockSpec((1, blocks, 8, BLK), lambda s, js, c: (s, 0, 0, 0)),
                pl.BlockSpec((1, blocks, 1, BLK), lambda s, js, c: (s, 0, 0, 0)),
                pl.BlockSpec((length, LANES), lambda s, js, c: (s, 0)),
                pl.BlockSpec((length, LANES), lambda s, js, c: (s, 0)),
            ],
            out_specs=pl.BlockSpec((length, 768), lambda s, js, c: (s, 0)),
            scratch_shapes=[
                pltpu.VMEM((length, width), BF),
                pltpu.VMEM((blocks, 8, BLK), F32),
                pltpu.VMEM((blocks, 256, BLK), BF),
                pltpu.VMEM((blocks, 2, 256, BLK), F32),
                pltpu.VMEM((length, 256), F32),
                pltpu.VMEM((length, 512), F32),
            ],
        ),
        out_shape=jax.ShapeDtypeStruct((seqs * length, 768), BF),
        compiler_params=params(48, ("arbitrary",)),
        cost_estimate=cost(31),
        name="attend_back",
    )(js, c, q, k, v, o, d0, d1, d23, lse, start, cos, sin)


def assemble_kernel(c_ref, f_ref, p0, p1, p2, p3, out):
    quarter = p0.shape[-1]
    for b in range(CTX):
        for d, ref in enumerate((p0, p1, p2, p3)):

            @pl.when((b ^ c_ref[0]) == d)
            def _():
                out[:, b * quarter : (b + 1) * quarter] = ref[0]


def assemble_call(c, f, parts):
    count, rows, quarter = parts[0].shape
    part = pl.BlockSpec((1, rows, quarter), lambda b, c, f: (b ^ f[0], 0, 0))
    return pl.pallas_call(
        assemble_kernel,
        grid_spec=pltpu.PrefetchScalarGridSpec(
            num_scalar_prefetch=2,
            grid=(count,),
            in_specs=[part] * CTX,
            out_specs=pl.BlockSpec((rows, CTX * quarter), lambda b, c, f: (b, 0)),
        ),
        out_shape=jax.ShapeDtypeStruct((count * rows, CTX * quarter), BF),
        compiler_params=params(20, ("arbitrary",)),
        cost_estimate=cost(5),
        name="assemble",
    )(c, f, *parts)


def out_kernel(c_ref, x, m0, m1, m2, m3, w, resid, normed):
    c = c_ref[0]
    acc = x[0].astype(F32)
    for d, ref in enumerate((m0, m1, m2, m3)):
        rows = pl.ds(pl.multiple_of((d ^ c) * (QH * HD), QH * HD), QH * HD)
        acc = acc + dot_nn(ref[0, 0], w[rows, :])
    resid[0] = acc
    normed[0] = rms_rows(acc).astype(BF)


def out_call(c, x, mixed, r1, r2, w):
    seqs, tok, width = x.shape
    inner_w = QH * HD

    def slot(n):
        return pl.BlockSpec((1, 1, tok, inner_w), lambda s, c: (n, s, 0, 0))

    tile = pl.BlockSpec((1, tok, width), lambda s, c: (s, 0, 0))
    return pl.pallas_call(
        out_kernel,
        grid_spec=pltpu.PrefetchScalarGridSpec(
            num_scalar_prefetch=1,
            grid=(seqs,),
            in_specs=[
                tile,
                slot(0),
                slot(0),
                slot(0),
                slot(1),
                pl.BlockSpec((H * HD, width), lambda s, c: (0, 0)),
            ],
            out_specs=[tile, tile],
        ),
        out_shape=[
            jax.ShapeDtypeStruct((seqs, tok, width), F32),
            jax.ShapeDtypeStruct((seqs, tok, width), BF),
        ],
        compiler_params=params(48, ("arbitrary",)),
        cost_estimate=cost(8),
        name="out_proj",
    )(c, x, mixed, r1, r2, r2, w)


def rms_back(v, dyg):
    r = lax.rsqrt(jnp.mean(v * v, axis=-1, keepdims=True) + EPSILON)
    return r * dyg - v * (r * r * r * jnp.mean(dyg * v, axis=-1, keepdims=True))


def out_back_kernel(c_ref, part_a, part_b, resid, dy, w, dresid, dattn, dmixed):
    c = c_ref[0]
    dn = part_a[0].astype(F32) + part_b[0].astype(F32)
    total = dy[0].astype(F32) + rms_back(resid[0], dn)
    dresid[0] = total
    low = total.astype(BF)
    dattn[0] = low
    for d in range(CTX):
        rows = pl.ds(pl.multiple_of((d ^ c) * (QH * HD), QH * HD), QH * HD)
        dmixed[d, 0] = dot_nt(low, w[rows, :]).astype(BF)


def out_back_call(c, part_a, part_b, resid, dy, w):
    seqs, tok, width = dy.shape
    inner_w = QH * HD
    tile = pl.BlockSpec((1, tok, width), lambda s, c: (s, 0, 0))
    return pl.pallas_call(
        out_back_kernel,
        grid_spec=pltpu.PrefetchScalarGridSpec(
            num_scalar_prefetch=1,
            grid=(seqs,),
            in_specs=[
                tile,
                tile,
                tile,
                tile,
                pl.BlockSpec((H * HD, width), lambda s, c: (0, 0)),
            ],
            out_specs=[
                tile,
                tile,
                pl.BlockSpec((CTX, 1, tok, inner_w), lambda s, c: (0, s, 0, 0)),
            ],
        ),
        out_shape=[
            jax.ShapeDtypeStruct((seqs, tok, width), F32),
            jax.ShapeDtypeStruct((seqs, tok, width), BF),
            jax.ShapeDtypeStruct((CTX, seqs, tok, inner_w), BF),
        ],
        compiler_params=params(56, ("arbitrary",)),
        cost_estimate=cost(9.5),
        name="out_back",
    )(c, part_a, part_b, resid, dy, w)


def mlp_kernel(n2, dy, wg, wu, wd, hidden, grads):
    n, g_out = n2[...], dy[...]
    gate = dot_nn(n, wg[...])
    up = dot_nn(n, wu[...])
    dh = dot_nn(g_out, wd[...])
    sig = 1.0 / (1.0 + jnp.exp(-gate))
    act = gate * sig
    hidden[...] = (act * up).astype(BF)
    cols = wg.shape[1]
    grads[0] = (dh * up * (sig + act * (1.0 - sig))).astype(BF)
    grads[1] = (dh * act).astype(BF)


def mlp_call(n2, dy, w):
    rows, width = n2.shape
    ff = w.shape[1] // 3
    tile = BLK
    steps = ff // tile
    full = pl.BlockSpec((rows, width), lambda j: (0, 0))
    return pl.pallas_call(
        mlp_kernel,
        grid=(steps,),
        in_specs=[
            full,
            full,
            pl.BlockSpec((width, tile), lambda j: (0, j)),
            pl.BlockSpec((width, tile), lambda j: (0, j + steps)),
            pl.BlockSpec((width, tile), lambda j: (0, j + 2 * steps)),
        ],
        out_specs=[
            pl.BlockSpec((rows, tile), lambda j: (0, j)),
            pl.BlockSpec((2, rows, tile), lambda j: (0, 0, j)),
        ],
        out_shape=[
            jax.ShapeDtypeStruct((rows, ff), BF),
            jax.ShapeDtypeStruct((2, rows, ff), BF),
        ],
        compiler_params=params(40, ("arbitrary",)),
        cost_estimate=cost(4.5),
        name="mlp",
    )(n2, dy, w, w, w)


def sum_nt_kernel(slots, *refs):
    count = len(slots)
    out = refs[-1]
    acc = None
    for n in range(count):
        left = refs[n]
        part = dot_nt(left[0] if len(left.shape) == 3 else left[...], refs[count + n][...])
        acc = part if acc is None else acc + part
    out[...] = acc.astype(out.dtype)


def sum_nt_call(terms, tile):
    rows, k = terms[0][0].shape[-2:]
    n = terms[0][2].shape[0]
    lefts, rights = [], []
    for array, slot, weight, window in terms:
        if slot is None:
            lefts.append(pl.BlockSpec((rows, k), lambda j: (0, 0)))
        else:
            lefts.append(pl.BlockSpec((1, rows, k), functools.partial(lambda slot, j: (slot, 0, 0), slot)))
        rights.append(pl.BlockSpec((tile, k), functools.partial(lambda window, j: (j, window), window)))
    count = len(terms)
    return pl.pallas_call(
        functools.partial(sum_nt_kernel, tuple(t[1] for t in terms)),
        grid=(n // tile,),
        in_specs=lefts + rights,
        out_specs=pl.BlockSpec((rows, tile), lambda j: (0, j)),
        out_shape=jax.ShapeDtypeStruct((rows, n), BF),
        compiler_params=params(40, ("arbitrary",)),
        cost_estimate=cost(4.4),
        name="sum_nt",
    )(*[t[0] for t in terms], *[t[2] for t in terms])


def put_sides(f_ref, acc, mine, theirs):
    acc = acc.astype(BF)
    count, rows, _ = mine.shape
    for side in range(2):

        @pl.when(f_ref[0] % 2 == side)
        def _():
            for z in range(count):
                at = 2 * z * rows
                mine[z] = acc[at + side * rows : at + (side + 1) * rows]
                theirs[z] = acc[at + (1 - side) * rows : at + (2 - side) * rows]


def mlp_gram_kernel(count, *refs):
    dys, n2s = refs[:count], refs[count : 2 * count]
    hid, gu = refs[2 * count : 3 * count], refs[3 * count : 4 * count]
    out = refs[-1]

    @pl.when(pl.program_id(0) == 0)
    def _():
        acc = dot_tn(dys[0][...], hid[0][...])
        for n in range(1, count):
            acc = acc + dot_tn(dys[n][...], hid[n][...])
        out[...] = acc.astype(out.dtype)

    @pl.when(pl.program_id(0) != 0)
    def _():
        acc = dot_tn(n2s[0][...], gu[0][0])
        for n in range(1, count):
            acc = acc + dot_tn(n2s[n][...], gu[n][0])
        out[...] = acc.astype(out.dtype)


def mlp_gram_call(dys, n2s, hid, gu, tile_m):
    rows, m = dys[0].shape
    k = hid[0].shape[1]
    count = len(dys)
    return pl.pallas_call(
        functools.partial(mlp_gram_kernel, count),
        grid=(3, m // tile_m),
        in_specs=[pl.BlockSpec((rows, tile_m), lambda j, i: (0, jnp.where(j == 0, i, m // tile_m - 1)))] * count
        + [pl.BlockSpec((rows, tile_m), lambda j, i: (0, jnp.where(j == 0, 0, i)))] * count
        + [pl.BlockSpec((rows, k), lambda j, i: (0, 0))] * count
        + [pl.BlockSpec((1, rows, k), lambda j, i: (jnp.maximum(j - 1, 0), 0, 0))] * count,
        out_specs=pl.BlockSpec((tile_m, k), lambda j, i: (i, j)),
        out_shape=jax.ShapeDtypeStruct((m, 3 * k), BF),
        compiler_params=params(56, ("arbitrary", "arbitrary")),
        cost_estimate=cost(18),
        name="mlp_gram",
    )(*dys, *n2s, *hid, *gu)


def gram_kernel(f_ref, left, right, mine, theirs):
    put_sides(f_ref, dot_tn(left[...], right[...]), mine, theirs)


def gram_call(f, left, right):
    rows, m = left.shape
    n = right.shape[1]
    one = pl.BlockSpec((2, m // 8, n), lambda i, f: (i, 0, 0))
    return pl.pallas_call(
        gram_kernel,
        grid_spec=pltpu.PrefetchScalarGridSpec(
            num_scalar_prefetch=1,
            grid=(2,),
            in_specs=[
                pl.BlockSpec((rows, m // 2), lambda i, f: (0, i)),
                pl.BlockSpec((rows, n), lambda i, f: (0, 0)),
            ],
            out_specs=[one, one],
        ),
        out_shape=[jax.ShapeDtypeStruct((4, m // 8, n), BF)] * 2,
        compiler_params=params(40, ("arbitrary",)),
        cost_estimate=cost(6),
        name="gram",
    )(f, left, right)


def out_gram_kernel(c_ref, f_ref, m0, m1, m2, m3, dattn, out):
    side = f_ref[0] % 2
    rows = out.shape[3]
    for d, ref in enumerate((m0, m1, m2, m3)):

        @pl.when(pl.program_id(0) == d)
        def _():
            tok = ref.shape[1] * ref.shape[2]
            acc = dot_tn(ref[0].reshape(tok, ref.shape[3]), dattn[...]).astype(BF)

            @pl.when(side == 0)
            def _():
                out[0, 0, 0] = acc[:rows]
                out[0, 1, 0] = acc[rows:]

            @pl.when(side != 0)
            def _():
                out[0, 0, 0] = acc[rows:]
                out[0, 1, 0] = acc[:rows]


def out_gram_call(c, f, mixed, r1, r2, dattn):
    seqs, tok, inner_w = mixed.shape[1:]
    rows, width = dattn.shape
    quarter = width // CTX

    def slot(n):
        return pl.BlockSpec((1, seqs, tok, inner_w), lambda d, e, c, f: (n, 0, 0, 0))

    return pl.pallas_call(
        out_gram_kernel,
        grid_spec=pltpu.PrefetchScalarGridSpec(
            num_scalar_prefetch=2,
            grid=(CTX, CTX),
            in_specs=[
                slot(0),
                slot(0),
                slot(0),
                slot(1),
                pl.BlockSpec((rows, quarter), lambda d, e, c, f: (0, e ^ c[0])),
            ],
            out_specs=pl.BlockSpec(
                (1, 2, 1, inner_w // 2, quarter), lambda d, e, c, f: (e, 0, d ^ c[0], 0, 0)
            ),
        ),
        out_shape=jax.ShapeDtypeStruct((CTX, 2, 4, inner_w // 2, quarter), BF),
        compiler_params=params(40, ("arbitrary", "arbitrary")),
        cost_estimate=cost(9),
        name="out_gram",
    )(c, f, mixed, r1, r2, r2, dattn)


def unpack_kernel(c_ref, s0, s1, s2, s3, perm, wq, wk, wv, gain, gq, gk, gv, gg, gm, go):
    c = c_ref[0]
    qw, kw = QH * HD, KH * HD
    n = perm.shape[0]
    g = gain[...]
    for b in range(CTX):
        for d, ref in enumerate((s0, s1, s2, s3)):

            @pl.when((b ^ c) == d)
            def _():
                flat = dot_nt(ref[:, :n], perm[...])
                gq[:, b * qw : (b + 1) * qw] = flat[:, :qw]
                gk[:, b * kw : (b + 1) * kw] = flat[:, qw : qw + kw]
                gv[:, b * kw : (b + 1) * kw] = flat[:, qw + kw :]
                go[:, b * qw : (b + 1) * qw] = ref[:, n : n + qw].astype(F32)

    total = jnp.zeros_like(g)
    for grad, w in ((gq, wq), (gk, wk), (gv, wv)):
        total = total + jnp.sum(grad[...] * w[...].astype(F32), axis=-1, keepdims=True)
        grad[...] = grad[...] * g
    gg[...] = total
    gm[...] = (
        s0[:, n + qw :].astype(F32)
        + s1[:, n + qw :].astype(F32)
        + s2[:, n + qw :].astype(F32)
        + s3[:, n + qw :].astype(F32)
    )[:, 0:1]


def unpack_call(c, parts, perm, wq, wk, wv, gain):
    rows = parts[0].shape[0]
    vm = pl.BlockSpec(memory_space=pltpu.VMEM)
    return pl.pallas_call(
        unpack_kernel,
        in_specs=[pl.BlockSpec(memory_space=pltpu.SMEM)] + [vm] * 9,
        out_specs=[vm] * 6,
        out_shape=[
            jax.ShapeDtypeStruct((rows, H * HD), F32),
            jax.ShapeDtypeStruct((rows, KVH * HD), F32),
            jax.ShapeDtypeStruct((rows, KVH * HD), F32),
            jax.ShapeDtypeStruct((rows, 1), F32),
            jax.ShapeDtypeStruct((rows, 1), F32),
            jax.ShapeDtypeStruct((rows, CTX * QH * HD), F32),
        ],
        compiler_params=pltpu.CompilerParams(vmem_limit_bytes=40 << 20),
        cost_estimate=cost(5),
        name="unpack",
    )(c, *parts, perm, wq, wk, wv, gain)


def qkv_back_kernel(c_ref, g, w, out):
    out[0, 0] = dot_nt(g[...], w[...]).astype(BF)


def qkv_back_call(c, grads, w, seqs, base):
    width = w.shape[0]
    return pl.pallas_call(
        qkv_back_kernel,
        grid_spec=pltpu.PrefetchScalarGridSpec(
            num_scalar_prefetch=1,
            grid=(2, seqs),
            in_specs=[
                pl.BlockSpec((BLK, 768), lambda d, s, c: (s * CTX + ((d + base) ^ c[0]), 0)),
                pl.BlockSpec((width, 768), lambda d, s, c: (0, 0)),
            ],
            out_specs=pl.BlockSpec((1, 1, BLK, width), lambda d, s, c: (d, s, 0, 0)),
        ),
        out_shape=jax.ShapeDtypeStruct((2, seqs, BLK, width), BF),
        compiler_params=params(40, ("arbitrary", "arbitrary")),
        cost_estimate=cost(3.3),
        name="qkv_back",
    )(c, grads, w)


def final_kernel(part_a, part_b, x, dresid, out):
    dn = part_a[0].astype(F32) + part_b[0].astype(F32)
    out[0] = dresid[0] + rms_back(x[0].astype(F32), dn)


def final_call(part_a, part_b, x, dresid):
    seqs, tok, width = x.shape
    tile = pl.BlockSpec((1, tok, width), lambda s: (s, 0, 0))
    return pl.pallas_call(
        final_kernel,
        grid=(seqs,),
        in_specs=[tile] * 4,
        out_specs=tile,
        out_shape=jax.ShapeDtypeStruct((seqs, tok, width), F32),
        compiler_params=params(40, ("arbitrary",)),
        cost_estimate=cost(4),
        name="final",
    )(part_a, part_b, x, dresid)


CORE = [(i, i ^ 1) for i in range(CTX)]
ROW = [(i, i ^ 2) for i in range(CTX)]


def swap_core(x):
    return lax.ppermute(x, "context", CORE)


def swap_row(x):
    return lax.ppermute(x, "context", ROW)


def gather_blocks(x):
    far = swap_row(x)
    near = swap_core(x)
    return [x, near, far, swap_core(far)]


def after(x, *first):
    return lax.optimization_barrier((x,) + first)[0]


def swap_fsdp(x, bit):
    size = lax.axis_size("fsdp")
    return lax.ppermute(x, "fsdp", [(i, i ^ bit) for i in range(size)])


def gather_fsdp(x):
    near = swap_fsdp(x, 2)
    side = swap_fsdp(x, 1)
    far = swap_fsdp(jnp.stack([x, near]), 4)
    near_side = swap_fsdp(near, 1)
    far_side = swap_fsdp(far, 1)
    return jnp.stack([x, side, near, near_side, far[0], far_side[0], far[1], far_side[1]])


def z_groups():
    size = lax.axis_size("fsdp")
    return [list(range(0, size, 2)), list(range(1, size, 2))]


def reduce_x(mine, theirs, *first):
    total = add_low(after(mine, *first), swap_fsdp(theirs, 1))
    return total.reshape(-1, total.shape[-1])


def reduce_z(x):
    return lax.psum_scatter(x, "fsdp", scatter_dimension=0, tiled=True, axis_index_groups=z_groups())


def add_low(a, b):
    return (a.astype(F32) + b.astype(F32)).astype(BF)


def on_device(
    tokens,
    segments,
    w_query,
    w_key,
    w_value,
    w_out,
    w_gate,
    w_up,
    w_down,
    gain_attn,
    gain_mlp,
    cotangent,
):
    seqs, tok, width = tokens.shape
    rows = seqs * tok
    length = tok * CTX
    qkv_w = (QH + 2 * KH) * HD
    ctx = lax.axis_index("context")
    core = ctx % 2
    c = ctx.astype(jnp.int32).reshape(1)

    last = []

    def step(call, x, *ready):
        x = after(x, *last, *ready)
        out = call(x)
        last[:] = [out[0] if isinstance(out, (tuple, list)) else out]
        return out

    segs = gather_blocks(segments)
    xs = gather_blocks(after(tokens, segs[2]))
    dys = gather_blocks(after(cotangent, xs[2]))

    perm = pack_matrix()
    fsdp = lax.axis_index("fsdp").astype(jnp.int32).reshape(1)
    col_a, col_m = gain_attn.astype(F32)[:, None], gain_mlp.astype(F32)[:, None]
    shard = jnp.concatenate(
        [
            lax.dynamic_slice_in_dim(w_query, ctx * (QH * HD), QH * HD, 1),
            lax.dynamic_slice_in_dim(w_key, ctx * (KH * HD), KH * HD, 1),
            lax.dynamic_slice_in_dim(w_value, ctx * (KH * HD), KH * HD, 1),
        ],
        axis=1,
    )
    shard = jnp.dot(shard, perm, preferred_element_type=F32)
    shard = (shard * col_a).astype(BF)
    quarter = width // CTX
    w_qkv = lax.all_gather(shard, "fsdp", axis=0, tiled=True)
    out_part = gather_fsdp(lax.dynamic_slice_in_dim(w_out, ctx * quarter, quarter, 1))
    out_parts = gather_blocks(out_part)
    down_t = jnp.transpose(w_down)
    ff = w_gate.shape[1] // 2
    w_parts = []
    for n in range(2):
        cols = slice(n * ff, (n + 1) * ff)
        part = jnp.concatenate(
            [
                (w_gate[:, cols].astype(F32) * col_m).astype(BF),
                (w_up[:, cols].astype(F32) * col_m).astype(BF),
                down_t[:, cols],
            ],
            axis=1,
        )
        part = after(part, *(segs[2:3] if n else [shard]))
        w_parts.append(lax.all_gather(part, "fsdp", axis=0, tiled=True))
    w_one, w_two = w_parts

    seg_blocks = jnp.stack(segs)
    whole_seg = jnp.concatenate(
        [lax.dynamic_index_in_dim(seg_blocks, b ^ ctx, 0, keepdims=False) for b in range(CTX)], axis=1
    )
    index = jnp.arange(length, dtype=jnp.int32)
    starts = jnp.concatenate(
        [jnp.ones((seqs, 1), dtype=bool), whole_seg[:, 1:] != whole_seg[:, :-1]], axis=1
    )
    first = lax.cummax(jnp.where(starts, index[None, :], 0), axis=1)
    positions = (index[None, :] - first).astype(F32).reshape(seqs * length, 1)
    freq = np.zeros((LANES,), np.float32)
    base = (THETA ** -(np.arange(HALF, dtype=np.float64) * 2.0 / HD)).astype(np.float32)
    for g in range(KH):
        freq[g * HALF : (g + 1) * HALF] = base
    angles = positions * jnp.asarray(freq)[None, :]
    cos, sin = jnp.cos(angles), jnp.sin(angles)
    low_block = (first[:, ::BLK] // BLK).reshape(seqs * CTX).astype(jnp.int32)
    first_rows = first.reshape(seqs, CTX, 1, BLK)

    normed, q, k, v = step(lambda t: qkv_call(c, xs, t, cos, sin), w_qkv, first_rows)
    mixed, lse = step(
        lambda t: attend_call(c, low_block, t, k, v, first_rows, seqs, length), q, dys[2]
    )
    r1 = swap_core(jnp.stack([mixed[1], mixed[3]]))
    r2 = swap_row(jnp.stack([mixed[2], r1[1]]))
    w_out_full = step(lambda t: assemble_call(c, fsdp, out_parts[:3] + [t]), out_parts[3])
    resid, normed_two = step(lambda t: out_call(c, tokens, mixed, r1, t, w_out_full), r2)

    n2s = [n.reshape(rows, width) for n in gather_blocks(normed_two)]
    dys = [d.reshape(rows, width) for d in dys]
    first_pairs = [step(lambda t: mlp_call(t, dys[d], w_one), n2s[d]) for d in range(CTX)]
    def gram(pairs, *ready):
        hid, gu = [p[0] for p in pairs], [p[1] for p in pairs]
        return step(lambda t: mlp_gram_call(dys, [t] + n2s[1:], hid, gu, 768), n2s[0], *ready)

    share_one = gram(first_pairs)
    s_one = lax.psum_scatter(share_one, "fsdp", scatter_dimension=0, tiled=True)
    second_pairs = [None] * CTX

    def back_rows(d, *ready):
        def call(t):
            terms = [(first_pairs[d][1], slot, w_one, slot) for slot in range(2)]
            return sum_nt_call(terms + [(t, slot, w_two, slot) for slot in range(2)], 512)

        return step(call, second_pairs[d][1], *ready)

    def down_rows(d, *ready):
        call = lambda t: sum_nt_call([(first_pairs[d][0], None, w_one, 2), (t, None, w_two, 2)], 512)
        return step(call, second_pairs[d][0], *ready)

    def back_pair(near, far, *ready):
        for d in (far, near):
            second_pairs[d] = step(lambda t: mlp_call(t, dys[d], w_two), n2s[d])
        low = back_rows(far)
        return back_rows(near, *ready), swap_core(low)

    dn2 = add_low(*back_pair(2, 3))
    dn_b = swap_row(dn2)
    last.append(dn2)
    dn_a = add_low(*back_pair(0, 1))
    share_two = gram(second_pairs)
    s_two = lax.psum_scatter(share_two, "fsdp", scatter_dimension=0, tiled=True)
    dresid, dattn, dmixed = step(
        lambda t: out_back_call(
            c, dn_a.reshape(tokens.shape), t.reshape(tokens.shape), resid, cotangent, w_out_full
        ),
        dn_b,
    )

    b1 = swap_core(jnp.stack([dmixed[1], dmixed[3]]))
    b2_send = jnp.stack([dmixed[2], b1[1]])
    b2 = swap_row(b2_send)
    g_out = step(lambda t: out_gram_call(c, fsdp, mixed, r1, r2, t), dattn.reshape(rows, width))
    got = swap_core(jnp.stack([g_out[1], g_out[3]]))
    g_send = add_low(g_out[2], got[1])
    low3, low2 = down_rows(3), down_rows(2)
    dqkv = step(
        lambda t: attend_back_call(
            c, low_block, q, k, v, mixed, dmixed, b1[0], t, lse, first_rows, cos, sin, seqs, length
        ),
        b2,
        g_send,
    )
    got_row = swap_row(after(g_send, b2))

    g_out = add_low(add_low(g_out[0], got[0]), after(got_row, dqkv))
    x_out = reduce_x(g_out[0], g_out[1])
    qkv_mine, qkv_theirs = step(lambda t: gram_call(fsdp, normed, t), dqkv, g_out)
    far = step(lambda t: qkv_back_call(c, t, w_qkv, seqs, 2), dqkv, x_out)
    dx2 = add_low(far[0], swap_core(far[1]))
    dx_b = swap_row(dx2)
    near = step(lambda t: qkv_back_call(c, t, w_qkv, seqs, 0), dqkv)
    dx_a = add_low(near[0], swap_core(near[1]))
    down2 = add_low(low2, swap_core(low3))
    down_b = swap_row(after(down2, got_row))
    low1, low0 = down_rows(1, down_b), down_rows(0, dx_b)
    down_a = add_low(low0, swap_core(low1))
    x_all = jnp.concatenate([reduce_x(qkv_mine, qkv_theirs, near, dx2), x_out], axis=1)
    s_attn = reduce_z(x_all)
    grad_tokens = step(lambda t: final_call(dx_a, t, tokens, dresid), dx_b, x_all)
    s_down, s_gate, s_up = [
        jnp.concatenate([s[:, n * ff : (n + 1) * ff] for s in (s_one, s_two)], axis=1).astype(F32)
        for n in range(3)
    ]
    part_m = jnp.sum(s_gate * w_gate.astype(F32) + s_up * w_up.astype(F32), axis=1, keepdims=True)
    part_m = jnp.broadcast_to(part_m, (part_m.shape[0], LANES)).astype(BF)
    sums = gather_blocks(jnp.concatenate([s_attn, part_m], axis=1))
    output = (
        resid + down_a.astype(F32).reshape(resid.shape) + down_b.astype(F32).reshape(resid.shape)
    ).astype(BF)
    g_query, g_key, g_value, g_gain_a, g_gain_m, g_w_out = step(
        lambda t: unpack_call(c, sums[:3] + [t], perm, w_query, w_key, w_value, col_a), sums[3]
    )
    return (
        output,
        grad_tokens,
        g_query,
        g_key,
        g_value,
        g_w_out,
        s_gate * col_m,
        s_up * col_m,
        jnp.transpose(s_down),
        g_gain_a[:, 0],
        g_gain_m[:, 0],
    )


def solution(mesh):
    split_heads = mesh.shape["context"] == CTX
    return jax.shard_map(
        on_device if split_heads else on_device_general,
        mesh=mesh,
        in_specs=(
            P("fsdp", "context", None),
            P("fsdp", "context"),
            P("fsdp", None),
            P("fsdp", None),
            P("fsdp", None),
            P("fsdp", None),
            P("fsdp", "context"),
            P("fsdp", "context"),
            P("context", "fsdp"),
            P("fsdp"),
            P("fsdp"),
            P("fsdp", "context", None),
        ),
        out_specs=(
            P("fsdp", "context", None),
            P("fsdp", "context", None),
            P("fsdp", None),
            P("fsdp", None),
            P("fsdp", None),
            P("fsdp", None),
            P("fsdp", "context"),
            P("fsdp", "context"),
            P("context", "fsdp"),
            P("fsdp"),
            P("fsdp"),
        ),
        check_vma=False,
    )
```

```python
import functools
import math

import jax
import jax.numpy as jnp
import numpy as np
from jax import lax
from jax.experimental import pallas as pl
from jax.experimental.pallas import tpu as pltpu
from jax.sharding import PartitionSpec as P

H = 16
KVH = 8
HD = 96


EPSILON = 1e-05
THETA = 100000.0


def rms_scale(values, gain):
    return values * lax.rsqrt(jnp.mean(values * values, axis=-1, keepdims=True) + EPSILON) * gain


def rotate(values, cosines, sines):
    half_width = values.shape[-1] // 2
    leading = values[..., :half_width]
    trailing = values[..., half_width:]
    return jnp.concatenate(
        [leading * cosines - trailing * sines, trailing * cosines + leading * sines], axis=-1
    )


def gated(gate_act, up_act):
    return jax.nn.silu(gate_act) * up_act


def inner(left, right):
    return jnp.einsum("ti,tj->ij", left, right, preferred_element_type=jnp.float32)


def outer_back(grad_rows, weight):
    return jnp.einsum("ti,ji->tj", grad_rows, weight, preferred_element_type=jnp.float32)


def reduce_grads(parts):
    shares = (
        lax.psum_scatter(
            parts[0].astype(jnp.bfloat16), "fsdp", scatter_dimension=0, tiled=True
        ).astype(jnp.float32),
        lax.psum_scatter(
            parts[1].astype(jnp.bfloat16), "fsdp", scatter_dimension=0, tiled=True
        ).astype(jnp.float32),
        lax.psum_scatter(
            parts[2].astype(jnp.bfloat16), "fsdp", scatter_dimension=0, tiled=True
        ).astype(jnp.float32),
        lax.psum_scatter(
            parts[3].astype(jnp.bfloat16), "fsdp", scatter_dimension=0, tiled=True
        ).astype(jnp.float32),
        lax.psum_scatter(
            parts[4].astype(jnp.bfloat16), "fsdp", scatter_dimension=0, tiled=True
        ).astype(jnp.float32),
        lax.psum_scatter(
            parts[5].astype(jnp.bfloat16), "fsdp", scatter_dimension=0, tiled=True
        ).astype(jnp.float32),
    )
    result = (
        lax.psum(shares[0].astype(jnp.bfloat16), "context").astype(jnp.float32),
        lax.psum(shares[1].astype(jnp.bfloat16), "context").astype(jnp.float32),
        lax.psum(shares[2].astype(jnp.bfloat16), "context").astype(jnp.float32),
        lax.psum(shares[3].astype(jnp.bfloat16), "context").astype(jnp.float32),
        lax.psum(shares[4].astype(jnp.bfloat16), "context").astype(jnp.float32),
        lax.psum(shares[5].astype(jnp.bfloat16), "context").astype(jnp.float32),
    )
    return result


def gather_attention(shard_query, shard_key, shard_value, shard_out, shard_gain_a, shard_gain_m):
    return (
        lax.all_gather(shard_query, "fsdp", axis=0, tiled=True),
        lax.all_gather(shard_key, "fsdp", axis=0, tiled=True),
        lax.all_gather(shard_value, "fsdp", axis=0, tiled=True),
        lax.all_gather(shard_out, "fsdp", axis=0, tiled=True),
        lax.all_gather(shard_gain_a, "fsdp", axis=0, tiled=True),
        lax.all_gather(shard_gain_m, "fsdp", axis=0, tiled=True),
    )


def gather_mlp(shard_gate, shard_up, shard_down):
    return (
        lax.all_gather(shard_gate, "fsdp", axis=0, tiled=True),
        lax.all_gather(shard_up, "fsdp", axis=0, tiled=True),
        lax.all_gather(shard_down, "fsdp", axis=1, tiled=True),
    )


def on_device_general(
    tokens,
    segments,
    w_query,
    w_key,
    w_value,
    w_out,
    w_gate,
    w_up,
    w_down,
    gain_attn,
    gain_mlp,
    cotangent,
):
    seq_count, tok_local, model_width = tokens.shape
    row_count = seq_count * tok_local
    groups = H // KVH
    kv_width = KVH * HD
    logit_scale = 1.0 / math.sqrt(HD)
    whole_seg = lax.all_gather(segments, "context", axis=1, tiled=True)
    length = whole_seg.shape[1]
    all_rows = seq_count * length
    offset = lax.axis_index("context") * tok_local
    key_index = jnp.arange(length, dtype=jnp.int32)
    query_index = offset + jnp.arange(tok_local, dtype=jnp.int32)
    starts = jnp.concatenate(
        [jnp.ones((seq_count, 1), dtype=bool), whole_seg[:, 1:] != whole_seg[:, :-1]], axis=1
    )
    first_index = lax.cummax(jnp.where(starts, key_index[None, :], 0), axis=1)
    positions = lax.dynamic_slice_in_dim(key_index[None, :] - first_index, offset, tok_local, 1)
    frequency = jnp.power(THETA, -(jnp.arange(HD // 2, dtype=jnp.float32) * 2.0 / HD))
    angles = positions.astype(jnp.float32)[:, :, None] * frequency[None, None, :]
    cosines = jnp.cos(angles).reshape(row_count, 1, HD // 2)
    sines = jnp.sin(angles).reshape(row_count, 1, HD // 2)
    x_flat = tokens.reshape(row_count, model_width).astype(jnp.float32)

    def masked_scores(query_sequence, k_seq, q_seg, k_seg):
        unscaled_scores = (
            jnp.einsum(
                "wxif,axf->xiwa",
                query_sequence,
                k_seq.reshape(length, KVH, HD),
                preferred_element_type=jnp.float32,
            )
            * logit_scale
        )
        allowed = (q_seg[:, None] == k_seg[None, :]) & (key_index[None, :] <= query_index[:, None])
        return jnp.where(allowed[None, None], unscaled_scores, -1e30)

    def attend(items):
        query_sequence, k_seq, v_seq, q_seg, k_seg = items
        scores = masked_scores(query_sequence, k_seq, q_seg, k_seg)
        top_score = jnp.max(scores, axis=-1, keepdims=True)
        weights = jnp.exp(scores - top_score)
        total = jnp.sum(weights, axis=-1, keepdims=True)
        attention_probabilities = (weights / total).astype(jnp.bfloat16)
        mixed_seq = jnp.einsum(
            "uvqe,eua->quva",
            attention_probabilities,
            v_seq.reshape(length, KVH, HD),
            preferred_element_type=jnp.float32,
        ).astype(jnp.bfloat16)
        return (mixed_seq, top_score + jnp.log(total))

    def forward(attn_weights, mlp_weights):
        full_query, full_key, full_value, full_out, full_gain_a, full_gain_m = attn_weights
        normed = rms_scale(x_flat, full_gain_a.astype(jnp.float32)).astype(jnp.bfloat16)
        queries = jnp.dot(normed, full_query, preferred_element_type=jnp.float32).reshape(
            row_count, H, HD
        )
        key_rows = jnp.dot(normed, full_key, preferred_element_type=jnp.float32).reshape(
            row_count, KVH, HD
        )
        value_matrix_rows = jnp.dot(normed, full_value, preferred_element_type=jnp.float32).astype(
            jnp.bfloat16
        )
        qrot = (
            rotate(queries, cosines, sines)
            .astype(jnp.bfloat16)
            .reshape(seq_count, tok_local, KVH, groups, HD)
        )
        rotary_keys = (
            rotate(key_rows, cosines, sines)
            .astype(jnp.bfloat16)
            .reshape(seq_count, tok_local, kv_width)
        )
        all_keys, all_values = (
            lax.all_gather(rotary_keys, "context", axis=1, tiled=True),
            lax.all_gather(
                value_matrix_rows.reshape(seq_count, tok_local, kv_width),
                "context",
                axis=1,
                tiled=True,
            ),
        )
        mixed, log_totals = lax.map(attend, (qrot, all_keys, all_values, segments, whole_seg))
        mixed_flat = mixed.reshape(row_count, H * HD)
        resid = x_flat + jnp.dot(mixed_flat, full_out, preferred_element_type=jnp.float32)
        full_gate, full_up, full_down = mlp_weights
        normed_two = rms_scale(resid, full_gain_m.astype(jnp.float32)).astype(jnp.bfloat16)
        all_normed_two = lax.all_gather(
            normed_two.reshape(seq_count, tok_local, model_width), "context", axis=1, tiled=True
        ).reshape(all_rows, model_width)
        gate_act = jnp.dot(all_normed_two, full_gate, preferred_element_type=jnp.float32)
        up_act = jnp.dot(all_normed_two, full_up, preferred_element_type=jnp.float32)
        hidden = gated(gate_act, up_act).astype(jnp.bfloat16)
        partial_down = jnp.dot(hidden, full_down, preferred_element_type=jnp.float32)
        down_sum = (
            lax.psum_scatter(
                partial_down.reshape(seq_count, length, model_width).astype(jnp.bfloat16),
                "context",
                scatter_dimension=1,
                tiled=True,
            )
            .astype(jnp.float32)
            .reshape(row_count, model_width)
        )
        final = resid + down_sum
        return (
            final,
            normed,
            qrot,
            all_keys,
            all_values,
            mixed,
            log_totals,
            resid,
            all_normed_two,
            gate_act,
            up_act,
            hidden,
        )

    attn_weights = gather_attention(w_query, w_key, w_value, w_out, gain_attn, gain_mlp)
    mlp_weights = gather_mlp(w_gate, w_up, w_down)
    state = forward(attn_weights, mlp_weights)
    output = state[0].astype(jnp.bfloat16).reshape(seq_count, tok_local, model_width)
    (
        final,
        normed,
        qrot,
        all_keys,
        all_values,
        mixed,
        log_totals,
        resid,
        all_normed_two,
        gate_act,
        up_act,
        hidden,
    ) = state
    full_query, full_key, full_value, full_out, full_gain_a, full_gain_m = attn_weights
    full_gate, full_up, full_down = mlp_weights
    grad_out = cotangent.reshape(row_count, model_width)
    all_grad_out = lax.all_gather(cotangent, "context", axis=1, tiled=True).reshape(
        all_rows, model_width
    )
    grad_down_t = inner(all_grad_out, hidden)
    grad_hidden = outer_back(all_grad_out, full_down)
    gate_pull = jax.vjp(gated, gate_act, up_act)[1]
    grad_gate_f, grad_up_f = gate_pull(grad_hidden)
    grad_gate_act = grad_gate_f.astype(jnp.bfloat16)
    grad_up_act = grad_up_f.astype(jnp.bfloat16)
    grad_gate = inner(all_normed_two, grad_gate_act)
    grad_up = inner(all_normed_two, grad_up_act)
    part_normed_two = outer_back(grad_gate_act, full_gate) + outer_back(grad_up_act, full_up)
    grad_normed_two = lax.psum_scatter(
        part_normed_two.reshape(seq_count, length, model_width),
        "context",
        scatter_dimension=1,
        tiled=True,
    ).reshape(row_count, model_width)
    norm_pull = jax.vjp(rms_scale, resid, full_gain_m.astype(jnp.float32))[1]
    back_resid, grad_gain_m = norm_pull(grad_normed_two)
    mlp_shares = (
        lax.psum_scatter(
            grad_gate.astype(jnp.bfloat16), "fsdp", scatter_dimension=0, tiled=True
        ).astype(jnp.float32),
        lax.psum_scatter(
            grad_up.astype(jnp.bfloat16), "fsdp", scatter_dimension=0, tiled=True
        ).astype(jnp.float32),
        lax.psum_scatter(
            grad_down_t.astype(jnp.bfloat16), "fsdp", scatter_dimension=0, tiled=True
        ).astype(jnp.float32),
    )
    grad_resid = grad_out.astype(jnp.float32) + back_resid
    grad_attn = grad_resid.astype(jnp.bfloat16)
    mixed_flat = mixed.reshape(row_count, H * HD)
    grad_out_w = inner(mixed_flat, grad_attn)
    grad_mixed = (
        outer_back(grad_attn, full_out)
        .astype(jnp.bfloat16)
        .reshape(seq_count, tok_local, KVH, groups, HD)
    )

    def attend_back(items):
        query_sequence, k_seq, v_seq, q_seg, k_seg, log_total, grad_seq = items
        scores = masked_scores(query_sequence, k_seq, q_seg, k_seg)
        attention_probabilities = jnp.exp(scores - log_total)
        grad_probs = jnp.einsum(
            "wxif,axf->xiwa",
            grad_seq,
            v_seq.reshape(length, KVH, HD),
            preferred_element_type=jnp.float32,
        )
        weighted = jnp.sum(attention_probabilities * grad_probs, axis=-1, keepdims=True)
        score_gradient = (attention_probabilities * (grad_probs - weighted)).astype(jnp.bfloat16)
        grad_q = (
            jnp.einsum(
                "uvqe,eua->quva",
                score_gradient,
                k_seq.reshape(length, KVH, HD),
                preferred_element_type=jnp.float32,
            )
            * logit_scale
        )
        grad_k = (
            jnp.einsum(
                "jnbp,bjny->pjy", score_gradient, query_sequence, preferred_element_type=jnp.float32
            )
            * logit_scale
        )
        grad_v = jnp.einsum(
            "jnbp,bjny->pjy",
            attention_probabilities.astype(jnp.bfloat16),
            grad_seq,
            preferred_element_type=jnp.float32,
        )
        return (grad_q, grad_k.reshape(length, kv_width), grad_v.reshape(length, kv_width))

    grad_qrot, part_keys, part_values = lax.map(
        attend_back, (qrot, all_keys, all_values, segments, whole_seg, log_totals, grad_mixed)
    )
    grad_krot, grad_vals = (
        lax.psum_scatter(
            part_keys.astype(jnp.bfloat16), "context", scatter_dimension=1, tiled=True
        ).astype(jnp.float32),
        lax.psum_scatter(
            part_values.astype(jnp.bfloat16), "context", scatter_dimension=1, tiled=True
        ).astype(jnp.float32),
    )
    grad_queries = (
        rotate(grad_qrot.reshape(row_count, H, HD), cosines, -sines)
        .astype(jnp.bfloat16)
        .reshape(row_count, H * HD)
    )
    grad_keys = (
        rotate(grad_krot.reshape(row_count, KVH, HD), cosines, -sines)
        .astype(jnp.bfloat16)
        .reshape(row_count, kv_width)
    )
    grad_values = grad_vals.reshape(row_count, kv_width).astype(jnp.bfloat16)
    grad_query_w = inner(normed, grad_queries)
    grad_key_w = inner(normed, grad_keys)
    grad_value_w = inner(normed, grad_values)
    grad_normed = (
        outer_back(grad_queries, full_query)
        + outer_back(grad_keys, full_key)
        + outer_back(grad_values, full_value)
    )
    first_pull = jax.vjp(rms_scale, x_flat, full_gain_a.astype(jnp.float32))[1]
    back_input, grad_gain_a = first_pull(grad_normed)
    attn_grads = reduce_grads(
        (grad_query_w, grad_key_w, grad_value_w, grad_out_w, grad_gain_a, grad_gain_m)
    )
    grad_input = (grad_resid + back_input).reshape(seq_count, tok_local, model_width)
    return (
        output,
        grad_input,
        attn_grads[0],
        attn_grads[1],
        attn_grads[2],
        attn_grads[3],
        mlp_shares[0],
        mlp_shares[1],
        jnp.transpose(mlp_shares[2]),
        attn_grads[4],
        attn_grads[5],
    )


BF = jnp.bfloat16
F32 = jnp.float32
LANES = 128
HALF = HD // 2
NEG = -1e30
SCALE = 1.0 / math.sqrt(HD)
SCALE_LOG2 = SCALE * math.log2(math.e)
CTX = 4
QH = H // CTX
KH = KVH // CTX
BLK = 256
SHARE = 0.25
NT = (((1,), (1,)), ((), ()))
TN = (((0,), (0,)), ((), ()))


def dot_nt(a, b):
    return lax.dot_general(a, b, NT, preferred_element_type=F32)


def dot_tn(a, b):
    return lax.dot_general(a, b, TN, preferred_element_type=F32)


def dot_nn(a, b):
    return jnp.dot(a, b, preferred_element_type=F32)


def lane_iota(rows, width):
    return lax.broadcasted_iota(jnp.int32, (rows, width), 1)


def params(mb, sem):
    return pltpu.CompilerParams(vmem_limit_bytes=mb << 20, dimension_semantics=sem)


def cost(micros):
    return pl.CostEstimate(flops=int(micros * SHARE * 1.15e9), bytes_accessed=0, transcendentals=0)


def packed_columns():
    src = []
    for group in range(6):
        if group < 4:
            member, half = group // 2, group % 2
            for g in range(KH):
                head = 2 * g + member
                src += [head * HD + half * HALF + t for t in range(HALF)]
        else:
            half = group - 4
            for g in range(KH):
                src += [QH * HD + g * HD + half * HALF + t for t in range(HALF)]
        src += [(QH + KH) * HD + group * 32 + t for t in range(32)]
    return np.array(src, np.int32)


def pack_matrix():
    n = (QH + 2 * KH) * HD
    src = jnp.asarray(packed_columns())
    return (lax.broadcasted_iota(jnp.int32, (n, n), 0) == src[None, :]).astype(BF)


def rms_rows(x):
    return x * lax.rsqrt(jnp.mean(x * x, axis=-1, keepdims=True) + EPSILON)


def qkv_kernel(c_ref, x0, x1, x2, x3, w, cos, sin, normed, q, k, v, xs):
    for d, ref in enumerate((x0, x1, x2, x3)):

        @pl.when(pl.program_id(0) == d)
        def _():
            xs[...] = ref[0]

    n = rms_rows(xs[...].astype(F32)).astype(BF)
    normed[...] = n
    t = dot_nn(n, w[...])
    y = [t[:, LANES * p : LANES * (p + 1)] for p in range(6)]
    c, s = cos[...], sin[...]
    rot = []
    for p in range(0, 6, 2):
        rot += [y[p] * c - y[p + 1] * s, y[p + 1] * c + y[p] * s]
    for p in range(4):
        q[:, LANES * p : LANES * (p + 1)] = rot[p].astype(BF)
    for p in range(2):
        k[:, LANES * p : LANES * (p + 1)] = rot[4 + p].astype(BF)
    quarter = lane_iota(y[0].shape[0], LANES) // 32

    def place(parts):
        out = jnp.ones_like(y[0])
        for dst, p in parts:
            piece = y[p] if dst == 3 else pltpu.roll(y[p], 32 * (dst + 1), 1)
            out = jnp.where(quarter == dst, piece, out)
        return out.astype(BF)

    v[:, 0:128] = place(((0, 0), (1, 1), (2, 2), (3, 0)))
    v[:, 128:256] = place(((0, 1), (1, 2)))
    v[:, 256:384] = place(((2, 3), (3, 4)))
    v[:, 384:512] = place(((0, 5), (1, 3), (2, 4), (3, 5)))


def qkv_call(c, xs, w, cos, sin):
    seqs, tok, width = xs[0].shape
    total = seqs * CTX * tok
    cols = 768

    def own(d):
        return pl.BlockSpec(
            (1, tok, width),
            lambda i, s, c: (jnp.where(i == d, s, jnp.where(i < d, 0, seqs - 1)), 0, 0),
        )

    def rows(n):
        return pl.BlockSpec((tok, n), lambda i, s, c: (s * CTX + (i ^ c[0]), 0))

    return pl.pallas_call(
        qkv_kernel,
        grid_spec=pltpu.PrefetchScalarGridSpec(
            num_scalar_prefetch=1,
            grid=(CTX, seqs),
            in_specs=[
                own(0),
                own(1),
                own(2),
                own(3),
                pl.BlockSpec((width, cols), lambda i, s, c: (0, 0)),
                rows(LANES),
                rows(LANES),
            ],
            out_specs=[rows(width), rows(512), rows(256), rows(512)],
            scratch_shapes=[pltpu.VMEM((tok, width), BF)],
        ),
        out_shape=[
            jax.ShapeDtypeStruct((total, width), BF),
            jax.ShapeDtypeStruct((total, 512), BF),
            jax.ShapeDtypeStruct((total, 256), BF),
            jax.ShapeDtypeStruct((total, 512), BF),
        ],
        compiler_params=params(40, ("arbitrary", "arbitrary")),
        cost_estimate=cost(13),
        name="qkv",
    )(c, *xs, w, cos, sin)


def head_masks(rows):
    lane = lane_iota(rows, 256)
    inner_lane = lane % LANES
    by_kv = [inner_lane < HALF, (inner_lane >= HALF) & (inner_lane < HD)]
    in_mixed = [
        lane < HD,
        (lane >= HD) & (lane < 2 * HD),
        (lane >= 64) & (lane < 64 + HD),
        lane >= 64 + HD,
    ]
    return lane, by_kv, in_mixed


def attend_kernel(js_ref, c_ref, q, k, v, start, mixed, lse, vt_s, m_s, o_s):
    s_id, i = pl.program_id(0), pl.program_id(1)
    blocks = k.shape[0] // BLK
    lane, by_kv, in_mixed = head_masks(BLK)
    sub = lax.broadcasted_iota(jnp.int32, (256, BLK), 0)
    take_a = (sub < HD) | ((sub >= 192) & (sub < 224))
    take_b = ((sub >= 64) & (sub < 64 + HD)) | (sub < 32)
    zero = jnp.zeros((BLK, 256), BF)

    @pl.when(i == 0)
    def _():
        for b in range(blocks):
            vt_s[b] = jnp.transpose(v[b * BLK : (b + 1) * BLK, :])

    m_s[...] = jnp.full_like(m_s, -jnp.inf)
    o_s[...] = jnp.zeros_like(o_s)
    col = i * BLK + lax.broadcasted_iota(jnp.int32, (BLK, BLK), 1)
    first = start[0, 0]
    low = js_ref[s_id * CTX + i]

    def step(t, _):
        j = i - t
        kb = k[pl.ds(pl.multiple_of(j * BLK, BLK), BLK), :]
        row = j * BLK + lax.broadcasted_iota(jnp.int32, (BLK, BLK), 0)
        bias = jnp.where((row >= first) & (row <= col), 0.0, NEG)
        for win, take in enumerate((take_a, take_b)):
            vt = vt_s[j, 256 * win : 256 * (win + 1), :]
            outs, alphas = [], []
            for m in range(2):
                h = 2 * win + m
                qh = jnp.where(by_kv[win], q[:, 256 * m : 256 * (m + 1)], zero)
                sc = dot_nt(kb, qh) * SCALE_LOG2 + bias
                m_old = m_s[h : h + 1, :]
                m_new = jnp.maximum(m_old, jnp.max(sc, axis=0, keepdims=True))
                p = jnp.exp2(sc - m_new)
                alphas.append(jnp.exp2(m_old - m_new))
                m_s[h : h + 1, :] = m_new
                outs.append(dot_nn(vt, p.astype(BF)))
            o_s[win] = o_s[win] * jnp.where(take, alphas[0], alphas[1]) + jnp.where(take, outs[0], outs[1])
        return 0

    lax.fori_loop(0, i - low + 1, step, 0)
    sums = [o_s[0, 192:193, :], o_s[0, 224:225, :], o_s[1, 0:1, :], o_s[1, 32:33, :]]
    inv = [1.0 / x for x in sums]
    a = jnp.transpose(o_s[0] * jnp.where(take_a, inv[0], inv[1]))
    b = jnp.transpose(o_s[1] * jnp.where(take_b, inv[2], inv[3]))
    mixed[0, 0, :, 0:128] = a[:, 0:128].astype(BF)
    mixed[0, 0, :, 128:256] = jnp.where(lane[:, :LANES] < 64, a[:, 128:256], b[:, 0:128]).astype(BF)
    mixed[0, 0, :, 256:384] = b[:, 128:256].astype(BF)
    lse[0, 0] = jnp.zeros_like(lse[0, 0])
    for h in range(QH):
        lse[0, 0, h : h + 1, :] = m_s[h : h + 1, :] + jnp.log2(sums[h])


def attend_call(c, js, q, k, v, start, seqs, length):
    blocks = length // BLK
    return pl.pallas_call(
        attend_kernel,
        grid_spec=pltpu.PrefetchScalarGridSpec(
            num_scalar_prefetch=2,
            grid=(seqs, blocks),
            in_specs=[
                pl.BlockSpec((BLK, 512), lambda s, i, js, c: (s * CTX + i, 0)),
                pl.BlockSpec((length, 256), lambda s, i, js, c: (s, 0)),
                pl.BlockSpec((length, 512), lambda s, i, js, c: (s, 0)),
                pl.BlockSpec((1, 1, 1, BLK), lambda s, i, js, c: (s, i, 0, 0)),
            ],
            out_specs=[
                pl.BlockSpec((1, 1, BLK, QH * HD), lambda s, i, js, c: (i ^ c[0], s, 0, 0)),
                pl.BlockSpec((1, 1, 8, BLK), lambda s, i, js, c: (s, i, 0, 0)),
            ],
            scratch_shapes=[
                pltpu.VMEM((blocks, 512, BLK), BF),
                pltpu.VMEM((8, BLK), F32),
                pltpu.VMEM((2, 256, BLK), F32),
            ],
        ),
        out_shape=[
            jax.ShapeDtypeStruct((CTX, seqs, BLK, QH * HD), BF),
            jax.ShapeDtypeStruct((seqs, blocks, 8, BLK), F32),
        ],
        compiler_params=params(40, ("arbitrary", "arbitrary")),
        cost_estimate=cost(18),
        name="attend",
    )(js, c, q, k, v, start)


def attend_back_kernel(
    js_ref, c_ref, q, k, v, o, d0, d1, d23, lse, start, cos, sin, out, do_s, dl_s, kt_s, dq_s, dk_s, dv_s
):
    s_id = pl.program_id(0)
    c = c_ref[0]
    blocks = q.shape[0] // BLK
    lane, by_kv, in_mixed = head_masks(BLK)
    zero = jnp.zeros((BLK, 256), BF)
    mixed_lane = lane_iota(8, QH * HD)
    mixed_row = lax.broadcasted_iota(jnp.int32, (8, QH * HD), 0)
    picks = (mixed_lane // HD == mixed_row).astype(F32)
    for d in range(CTX):
        b = d ^ c
        rows = pl.ds(pl.multiple_of(b * BLK, BLK), BLK)
        g = d0[0, 0] if d == 0 else d1[0] if d == 1 else d23[d - 2, 0]
        do_s[rows, :] = g
        prod = g.astype(F32) * o[d, 0].astype(F32)
        dl_s[b] = lax.dot_general(
            picks, prod, NT, preferred_element_type=F32, precision=lax.Precision.HIGHEST
        )
    for b in range(blocks):
        kt_s[b] = jnp.transpose(k[b * BLK : (b + 1) * BLK, :])
    sub_in = lax.broadcasted_iota(jnp.int32, (256, BLK), 0) % LANES
    sub_kv = [sub_in < HALF, (sub_in >= HALF) & (sub_in < HD)]
    dq_s[...] = jnp.zeros_like(dq_s)
    dk_s[...] = jnp.zeros_like(dk_s)
    dv_s[...] = jnp.zeros_like(dv_s)

    def outer(i, _):
        qs = pl.ds(pl.multiple_of(i * BLK, BLK), BLK)
        col = i * BLK + lax.broadcasted_iota(jnp.int32, (BLK, BLK), 1)
        first = start[0, i]
        delta = dl_s[i]
        logs = lse[0, i]

        def step(t, _):
            j = i - t
            ks = pl.ds(pl.multiple_of(j * BLK, BLK), BLK)
            kb = k[ks, :]
            kt = kt_s[j]
            row = j * BLK + lax.broadcasted_iota(jnp.int32, (BLK, BLK), 0)
            bias = jnp.where((row >= first) & (row <= col), 0.0, NEG)
            dk = jnp.zeros((BLK, 256), F32)
            dq = [jnp.zeros((256, BLK), F32) for _ in range(2)]
            for win in range(KH):
                vb = v[ks, 256 * win : 256 * (win + 1)]
                kg = jnp.where(sub_kv[win], kt, zero)
                dv = jnp.zeros((BLK, 256), F32)
                for m in range(2):
                    h = 2 * win + m
                    qh = jnp.where(by_kv[win], q[qs, 256 * m : 256 * (m + 1)], zero)
                    do = jnp.where(in_mixed[h], do_s[qs, LANES * win : LANES * win + 256], zero)
                    sc = dot_nt(kb, qh) * SCALE_LOG2 + bias
                    p = jnp.exp2(sc - logs[h : h + 1, :])
                    dp = dot_nt(vb, do)
                    ds = (p * (dp - delta[h : h + 1, :])).astype(BF)
                    dv = dv + dot_nn(p.astype(BF), do)
                    dk = dk + dot_nn(ds, qh)
                    dq[m] = dq[m] + dot_nn(kg, ds)
                dv_s[ks, 256 * win : 256 * (win + 1)] += dv
            dk_s[ks, :] += dk
            for m in range(2):
                dq_s[i, m] += dq[m]
            return 0

        lax.fori_loop(0, i - js_ref[s_id * CTX + i] + 1, step, 0)
        return 0

    lax.fori_loop(0, blocks, outer, 0)
    head_lane = lane[:, :LANES] < HD

    def finish(i, _):
        rows = pl.ds(pl.multiple_of(i * BLK, BLK), BLK)
        cs, sn = cos[rows, :] * SCALE, sin[rows, :] * SCALE
        a0, a1 = dv_s[rows, 0:128], dv_s[rows, 128:256]
        b0, b1 = dv_s[rows, 256:384], dv_s[rows, 384:512]

        def r(x, n):
            return pltpu.roll(x, n, 1)

        pieces = [
            r(a0, 96) + a0,
            r(a0, 64) + r(a1, 96),
            r(a0, 32) + r(a1, 64),
            r(b0, 32) + r(b1, 64),
            b0 + r(b1, 32),
            r(b1, 96) + b1,
        ]
        grads = []
        for m in range(2):
            dq = jnp.transpose(dq_s[i, m])
            grads += [dq[:, 0:128], dq[:, 128:256]]
        grads += [dk_s[rows, 0:128], dk_s[rows, 128:256]]
        for p in range(0, 6, 2):
            first_half = grads[p] * cs + grads[p + 1] * sn
            second_half = grads[p + 1] * cs - grads[p] * sn
            out[rows, LANES * p : LANES * (p + 1)] = jnp.where(head_lane, first_half, pieces[p]).astype(BF)
            out[rows, LANES * (p + 1) : LANES * (p + 2)] = jnp.where(
                head_lane, second_half, pieces[p + 1]
            ).astype(BF)
        return 0

    lax.fori_loop(0, blocks, finish, 0)


def attend_back_call(c, js, q, k, v, o, d0, d1, d23, lse, start, cos, sin, seqs, length):
    blocks = length // BLK
    width = QH * HD
    return pl.pallas_call(
        attend_back_kernel,
        grid_spec=pltpu.PrefetchScalarGridSpec(
            num_scalar_prefetch=2,
            grid=(seqs,),
            in_specs=[
                pl.BlockSpec((length, 512), lambda s, js, c: (s, 0)),
                pl.BlockSpec((length, 256), lambda s, js, c: (s, 0)),
                pl.BlockSpec((length, 512), lambda s, js, c: (s, 0)),
                pl.BlockSpec((CTX, 1, BLK, width), lambda s, js, c: (0, s, 0, 0)),
                pl.BlockSpec((1, 1, BLK, width), lambda s, js, c: (0, s, 0, 0)),
                pl.BlockSpec((1, BLK, width), lambda s, js, c: (s, 0, 0)),
                pl.BlockSpec((2, 1, BLK, width), lambda s, js, c: (0, s, 0, 0)),
                pl.BlockSpec((1, blocks, 8, BLK), lambda s, js, c: (s, 0, 0, 0)),
                pl.BlockSpec((1, blocks, 1, BLK), lambda s, js, c: (s, 0, 0, 0)),
                pl.BlockSpec((length, LANES), lambda s, js, c: (s, 0)),
                pl.BlockSpec((length, LANES), lambda s, js, c: (s, 0)),
            ],
            out_specs=pl.BlockSpec((length, 768), lambda s, js, c: (s, 0)),
            scratch_shapes=[
                pltpu.VMEM((length, width), BF),
                pltpu.VMEM((blocks, 8, BLK), F32),
                pltpu.VMEM((blocks, 256, BLK), BF),
                pltpu.VMEM((blocks, 2, 256, BLK), F32),
                pltpu.VMEM((length, 256), F32),
                pltpu.VMEM((length, 512), F32),
            ],
        ),
        out_shape=jax.ShapeDtypeStruct((seqs * length, 768), BF),
        compiler_params=params(48, ("arbitrary",)),
        cost_estimate=cost(31),
        name="attend_back",
    )(js, c, q, k, v, o, d0, d1, d23, lse, start, cos, sin)


def assemble_kernel(c_ref, f_ref, p0, p1, p2, p3, out):
    quarter = p0.shape[-1]
    for b in range(CTX):
        for d, ref in enumerate((p0, p1, p2, p3)):

            @pl.when((b ^ c_ref[0]) == d)
            def _():
                out[:, b * quarter : (b + 1) * quarter] = ref[0]


def assemble_call(c, f, parts):
    count, rows, quarter = parts[0].shape
    part = pl.BlockSpec((1, rows, quarter), lambda b, c, f: (b ^ f[0], 0, 0))
    return pl.pallas_call(
        assemble_kernel,
        grid_spec=pltpu.PrefetchScalarGridSpec(
            num_scalar_prefetch=2,
            grid=(count,),
            in_specs=[part] * CTX,
            out_specs=pl.BlockSpec((rows, CTX * quarter), lambda b, c, f: (b, 0)),
        ),
        out_shape=jax.ShapeDtypeStruct((count * rows, CTX * quarter), BF),
        compiler_params=params(20, ("arbitrary",)),
        cost_estimate=cost(5),
        name="assemble",
    )(c, f, *parts)


def out_kernel(c_ref, x, m0, m1, m2, m3, w, resid, normed):
    c = c_ref[0]
    acc = x[0].astype(F32)
    for d, ref in enumerate((m0, m1, m2, m3)):
        rows = pl.ds(pl.multiple_of((d ^ c) * (QH * HD), QH * HD), QH * HD)
        acc = acc + dot_nn(ref[0, 0], w[rows, :])
    resid[0] = acc
    normed[0] = rms_rows(acc).astype(BF)


def out_call(c, x, mixed, r1, r2, w):
    seqs, tok, width = x.shape
    inner_w = QH * HD

    def slot(n):
        return pl.BlockSpec((1, 1, tok, inner_w), lambda s, c: (n, s, 0, 0))

    tile = pl.BlockSpec((1, tok, width), lambda s, c: (s, 0, 0))
    return pl.pallas_call(
        out_kernel,
        grid_spec=pltpu.PrefetchScalarGridSpec(
            num_scalar_prefetch=1,
            grid=(seqs,),
            in_specs=[
                tile,
                slot(0),
                slot(0),
                slot(0),
                slot(1),
                pl.BlockSpec((H * HD, width), lambda s, c: (0, 0)),
            ],
            out_specs=[tile, tile],
        ),
        out_shape=[
            jax.ShapeDtypeStruct((seqs, tok, width), F32),
            jax.ShapeDtypeStruct((seqs, tok, width), BF),
        ],
        compiler_params=params(48, ("arbitrary",)),
        cost_estimate=cost(8),
        name="out_proj",
    )(c, x, mixed, r1, r2, r2, w)


def rms_back(v, dyg):
    r = lax.rsqrt(jnp.mean(v * v, axis=-1, keepdims=True) + EPSILON)
    return r * dyg - v * (r * r * r * jnp.mean(dyg * v, axis=-1, keepdims=True))


def out_back_kernel(c_ref, part_a, part_b, resid, dy, w, dresid, dattn, dmixed):
    c = c_ref[0]
    dn = part_a[0].astype(F32) + part_b[0].astype(F32)
    total = dy[0].astype(F32) + rms_back(resid[0], dn)
    dresid[0] = total
    low = total.astype(BF)
    dattn[0] = low
    for d in range(CTX):
        rows = pl.ds(pl.multiple_of((d ^ c) * (QH * HD), QH * HD), QH * HD)
        dmixed[d, 0] = dot_nt(low, w[rows, :]).astype(BF)


def out_back_call(c, part_a, part_b, resid, dy, w):
    seqs, tok, width = dy.shape
    inner_w = QH * HD
    tile = pl.BlockSpec((1, tok, width), lambda s, c: (s, 0, 0))
    return pl.pallas_call(
        out_back_kernel,
        grid_spec=pltpu.PrefetchScalarGridSpec(
            num_scalar_prefetch=1,
            grid=(seqs,),
            in_specs=[
                tile,
                tile,
                tile,
                tile,
                pl.BlockSpec((H * HD, width), lambda s, c: (0, 0)),
            ],
            out_specs=[
                tile,
                tile,
                pl.BlockSpec((CTX, 1, tok, inner_w), lambda s, c: (0, s, 0, 0)),
            ],
        ),
        out_shape=[
            jax.ShapeDtypeStruct((seqs, tok, width), F32),
            jax.ShapeDtypeStruct((seqs, tok, width), BF),
            jax.ShapeDtypeStruct((CTX, seqs, tok, inner_w), BF),
        ],
        compiler_params=params(56, ("arbitrary",)),
        cost_estimate=cost(9.5),
        name="out_back",
    )(c, part_a, part_b, resid, dy, w)


def mlp_kernel(n2, dy, wg, wu, wd, hidden, grads):
    n, g_out = n2[...], dy[...]
    gate = dot_nn(n, wg[...])
    up = dot_nn(n, wu[...])
    dh = dot_nn(g_out, wd[...])
    sig = 1.0 / (1.0 + jnp.exp(-gate))
    act = gate * sig
    hidden[...] = (act * up).astype(BF)
    cols = wg.shape[1]
    grads[0] = (dh * up * (sig + act * (1.0 - sig))).astype(BF)
    grads[1] = (dh * act).astype(BF)


def mlp_call(n2, dy, w):
    rows, width = n2.shape
    ff = w.shape[1] // 3
    tile = BLK
    steps = ff // tile
    full = pl.BlockSpec((rows, width), lambda j: (0, 0))
    return pl.pallas_call(
        mlp_kernel,
        grid=(steps,),
        in_specs=[
            full,
            full,
            pl.BlockSpec((width, tile), lambda j: (0, j)),
            pl.BlockSpec((width, tile), lambda j: (0, j + steps)),
            pl.BlockSpec((width, tile), lambda j: (0, j + 2 * steps)),
        ],
        out_specs=[
            pl.BlockSpec((rows, tile), lambda j: (0, j)),
            pl.BlockSpec((2, rows, tile), lambda j: (0, 0, j)),
        ],
        out_shape=[
            jax.ShapeDtypeStruct((rows, ff), BF),
            jax.ShapeDtypeStruct((2, rows, ff), BF),
        ],
        compiler_params=params(40, ("arbitrary",)),
        cost_estimate=cost(4.5),
        name="mlp",
    )(n2, dy, w, w, w)


def sum_nt_kernel(slots, *refs):
    count = len(slots)
    out = refs[-1]
    acc = None
    for n in range(count):
        left = refs[n]
        part = dot_nt(left[0] if len(left.shape) == 3 else left[...], refs[count + n][...])
        acc = part if acc is None else acc + part
    out[...] = acc.astype(out.dtype)


def sum_nt_call(terms, tile):
    rows, k = terms[0][0].shape[-2:]
    n = terms[0][2].shape[0]
    lefts, rights = [], []
    for array, slot, weight, window in terms:
        if slot is None:
            lefts.append(pl.BlockSpec((rows, k), lambda j: (0, 0)))
        else:
            lefts.append(pl.BlockSpec((1, rows, k), functools.partial(lambda slot, j: (slot, 0, 0), slot)))
        rights.append(pl.BlockSpec((tile, k), functools.partial(lambda window, j: (j, window), window)))
    count = len(terms)
    return pl.pallas_call(
        functools.partial(sum_nt_kernel, tuple(t[1] for t in terms)),
        grid=(n // tile,),
        in_specs=lefts + rights,
        out_specs=pl.BlockSpec((rows, tile), lambda j: (0, j)),
        out_shape=jax.ShapeDtypeStruct((rows, n), BF),
        compiler_params=params(40, ("arbitrary",)),
        cost_estimate=cost(4.4),
        name="sum_nt",
    )(*[t[0] for t in terms], *[t[2] for t in terms])


def put_sides(f_ref, acc, mine, theirs):
    acc = acc.astype(BF)
    count, rows, _ = mine.shape
    for side in range(2):

        @pl.when(f_ref[0] % 2 == side)
        def _():
            for z in range(count):
                at = 2 * z * rows
                mine[z] = acc[at + side * rows : at + (side + 1) * rows]
                theirs[z] = acc[at + (1 - side) * rows : at + (2 - side) * rows]


def mlp_gram_kernel(count, *refs):
    dys, n2s = refs[:count], refs[count : 2 * count]
    hid, gu = refs[2 * count : 3 * count], refs[3 * count : 4 * count]
    out = refs[-1]

    @pl.when(pl.program_id(0) == 0)
    def _():
        acc = dot_tn(dys[0][...], hid[0][...])
        for n in range(1, count):
            acc = acc + dot_tn(dys[n][...], hid[n][...])
        out[...] = acc.astype(out.dtype)

    @pl.when(pl.program_id(0) != 0)
    def _():
        acc = dot_tn(n2s[0][...], gu[0][0])
        for n in range(1, count):
            acc = acc + dot_tn(n2s[n][...], gu[n][0])
        out[...] = acc.astype(out.dtype)


def mlp_gram_call(dys, n2s, hid, gu, tile_m):
    rows, m = dys[0].shape
    k = hid[0].shape[1]
    count = len(dys)
    return pl.pallas_call(
        functools.partial(mlp_gram_kernel, count),
        grid=(3, m // tile_m),
        in_specs=[pl.BlockSpec((rows, tile_m), lambda j, i: (0, jnp.where(j == 0, i, m // tile_m - 1)))] * count
        + [pl.BlockSpec((rows, tile_m), lambda j, i: (0, jnp.where(j == 0, 0, i)))] * count
        + [pl.BlockSpec((rows, k), lambda j, i: (0, 0))] * count
        + [pl.BlockSpec((1, rows, k), lambda j, i: (jnp.maximum(j - 1, 0), 0, 0))] * count,
        out_specs=pl.BlockSpec((tile_m, k), lambda j, i: (i, j)),
        out_shape=jax.ShapeDtypeStruct((m, 3 * k), BF),
        compiler_params=params(56, ("arbitrary", "arbitrary")),
        cost_estimate=cost(18),
        name="mlp_gram",
    )(*dys, *n2s, *hid, *gu)


def gram_kernel(f_ref, left, right, mine, theirs):
    put_sides(f_ref, dot_tn(left[...], right[...]), mine, theirs)


def gram_call(f, left, right):
    rows, m = left.shape
    n = right.shape[1]
    one = pl.BlockSpec((2, m // 8, n), lambda i, f: (i, 0, 0))
    return pl.pallas_call(
        gram_kernel,
        grid_spec=pltpu.PrefetchScalarGridSpec(
            num_scalar_prefetch=1,
            grid=(2,),
            in_specs=[
                pl.BlockSpec((rows, m // 2), lambda i, f: (0, i)),
                pl.BlockSpec((rows, n), lambda i, f: (0, 0)),
            ],
            out_specs=[one, one],
        ),
        out_shape=[jax.ShapeDtypeStruct((4, m // 8, n), BF)] * 2,
        compiler_params=params(40, ("arbitrary",)),
        cost_estimate=cost(6),
        name="gram",
    )(f, left, right)


def out_gram_kernel(c_ref, f_ref, m0, m1, m2, m3, dattn, out):
    side = f_ref[0] % 2
    rows = out.shape[3]
    for d, ref in enumerate((m0, m1, m2, m3)):

        @pl.when(pl.program_id(0) == d)
        def _():
            tok = ref.shape[1] * ref.shape[2]
            acc = dot_tn(ref[0].reshape(tok, ref.shape[3]), dattn[...]).astype(BF)

            @pl.when(side == 0)
            def _():
                out[0, 0, 0] = acc[:rows]
                out[0, 1, 0] = acc[rows:]

            @pl.when(side != 0)
            def _():
                out[0, 0, 0] = acc[rows:]
                out[0, 1, 0] = acc[:rows]


def out_gram_call(c, f, mixed, r1, r2, dattn):
    seqs, tok, inner_w = mixed.shape[1:]
    rows, width = dattn.shape
    quarter = width // CTX

    def slot(n):
        return pl.BlockSpec((1, seqs, tok, inner_w), lambda d, e, c, f: (n, 0, 0, 0))

    return pl.pallas_call(
        out_gram_kernel,
        grid_spec=pltpu.PrefetchScalarGridSpec(
            num_scalar_prefetch=2,
            grid=(CTX, CTX),
            in_specs=[
                slot(0),
                slot(0),
                slot(0),
                slot(1),
                pl.BlockSpec((rows, quarter), lambda d, e, c, f: (0, e ^ c[0])),
            ],
            out_specs=pl.BlockSpec(
                (1, 2, 1, inner_w // 2, quarter), lambda d, e, c, f: (e, 0, d ^ c[0], 0, 0)
            ),
        ),
        out_shape=jax.ShapeDtypeStruct((CTX, 2, 4, inner_w // 2, quarter), BF),
        compiler_params=params(40, ("arbitrary", "arbitrary")),
        cost_estimate=cost(9),
        name="out_gram",
    )(c, f, mixed, r1, r2, r2, dattn)


def unpack_kernel(c_ref, s0, s1, s2, s3, perm, wq, wk, wv, gain, gq, gk, gv, gg, gm, go):
    c = c_ref[0]
    qw, kw = QH * HD, KH * HD
    n = perm.shape[0]
    g = gain[...]
    for b in range(CTX):
        for d, ref in enumerate((s0, s1, s2, s3)):

            @pl.when((b ^ c) == d)
            def _():
                flat = dot_nt(ref[:, :n], perm[...])
                gq[:, b * qw : (b + 1) * qw] = flat[:, :qw]
                gk[:, b * kw : (b + 1) * kw] = flat[:, qw : qw + kw]
                gv[:, b * kw : (b + 1) * kw] = flat[:, qw + kw :]
                go[:, b * qw : (b + 1) * qw] = ref[:, n : n + qw].astype(F32)

    total = jnp.zeros_like(g)
    for grad, w in ((gq, wq), (gk, wk), (gv, wv)):
        total = total + jnp.sum(grad[...] * w[...].astype(F32), axis=-1, keepdims=True)
        grad[...] = grad[...] * g
    gg[...] = total
    gm[...] = (
        s0[:, n + qw :].astype(F32)
        + s1[:, n + qw :].astype(F32)
        + s2[:, n + qw :].astype(F32)
        + s3[:, n + qw :].astype(F32)
    )[:, 0:1]


def unpack_call(c, parts, perm, wq, wk, wv, gain):
    rows = parts[0].shape[0]
    vm = pl.BlockSpec(memory_space=pltpu.VMEM)
    return pl.pallas_call(
        unpack_kernel,
        in_specs=[pl.BlockSpec(memory_space=pltpu.SMEM)] + [vm] * 9,
        out_specs=[vm] * 6,
        out_shape=[
            jax.ShapeDtypeStruct((rows, H * HD), F32),
            jax.ShapeDtypeStruct((rows, KVH * HD), F32),
            jax.ShapeDtypeStruct((rows, KVH * HD), F32),
            jax.ShapeDtypeStruct((rows, 1), F32),
            jax.ShapeDtypeStruct((rows, 1), F32),
            jax.ShapeDtypeStruct((rows, CTX * QH * HD), F32),
        ],
        compiler_params=pltpu.CompilerParams(vmem_limit_bytes=40 << 20),
        cost_estimate=cost(5),
        name="unpack",
    )(c, *parts, perm, wq, wk, wv, gain)


def qkv_back_kernel(c_ref, g, w, out):
    out[0, 0] = dot_nt(g[...], w[...]).astype(BF)


def qkv_back_call(c, grads, w, seqs, base):
    width = w.shape[0]
    return pl.pallas_call(
        qkv_back_kernel,
        grid_spec=pltpu.PrefetchScalarGridSpec(
            num_scalar_prefetch=1,
            grid=(2, seqs),
            in_specs=[
                pl.BlockSpec((BLK, 768), lambda d, s, c: (s * CTX + ((d + base) ^ c[0]), 0)),
                pl.BlockSpec((width, 768), lambda d, s, c: (0, 0)),
            ],
            out_specs=pl.BlockSpec((1, 1, BLK, width), lambda d, s, c: (d, s, 0, 0)),
        ),
        out_shape=jax.ShapeDtypeStruct((2, seqs, BLK, width), BF),
        compiler_params=params(40, ("arbitrary", "arbitrary")),
        cost_estimate=cost(3.3),
        name="qkv_back",
    )(c, grads, w)


def final_kernel(part_a, part_b, x, dresid, out):
    dn = part_a[0].astype(F32) + part_b[0].astype(F32)
    out[0] = dresid[0] + rms_back(x[0].astype(F32), dn)


def final_call(part_a, part_b, x, dresid):
    seqs, tok, width = x.shape
    tile = pl.BlockSpec((1, tok, width), lambda s: (s, 0, 0))
    return pl.pallas_call(
        final_kernel,
        grid=(seqs,),
        in_specs=[tile] * 4,
        out_specs=tile,
        out_shape=jax.ShapeDtypeStruct((seqs, tok, width), F32),
        compiler_params=params(40, ("arbitrary",)),
        cost_estimate=cost(4),
        name="final",
    )(part_a, part_b, x, dresid)


CORE = [(i, i ^ 1) for i in range(CTX)]
ROW = [(i, i ^ 2) for i in range(CTX)]


def swap_core(x):
    return lax.ppermute(x, "context", CORE)


def swap_row(x):
    return lax.ppermute(x, "context", ROW)


def gather_blocks(x):
    far = swap_row(x)
    near = swap_core(x)
    return [x, near, far, swap_core(far)]


def after(x, *first):
    return lax.optimization_barrier((x,) + first)[0]


def swap_fsdp(x, bit):
    size = lax.axis_size("fsdp")
    return lax.ppermute(x, "fsdp", [(i, i ^ bit) for i in range(size)])


def gather_fsdp(x):
    near = swap_fsdp(x, 2)
    side = swap_fsdp(x, 1)
    far = swap_fsdp(jnp.stack([x, near]), 4)
    near_side = swap_fsdp(near, 1)
    far_side = swap_fsdp(far, 1)
    return jnp.stack([x, side, near, near_side, far[0], far_side[0], far[1], far_side[1]])


def z_groups():
    size = lax.axis_size("fsdp")
    return [list(range(0, size, 2)), list(range(1, size, 2))]


def reduce_x(mine, theirs, *first):
    total = add_low(after(mine, *first), swap_fsdp(theirs, 1))
    return total.reshape(-1, total.shape[-1])


def reduce_z(x):
    return lax.psum_scatter(x, "fsdp", scatter_dimension=0, tiled=True, axis_index_groups=z_groups())


def add_low(a, b):
    return (a.astype(F32) + b.astype(F32)).astype(BF)


def on_device(
    tokens,
    segments,
    w_query,
    w_key,
    w_value,
    w_out,
    w_gate,
    w_up,
    w_down,
    gain_attn,
    gain_mlp,
    cotangent,
):
    seqs, tok, width = tokens.shape
    rows = seqs * tok
    length = tok * CTX
    qkv_w = (QH + 2 * KH) * HD
    ctx = lax.axis_index("context")
    core = ctx % 2
    c = ctx.astype(jnp.int32).reshape(1)

    last = []

    def step(call, x, *ready):
        x = after(x, *last, *ready)
        out = call(x)
        last[:] = [out[0] if isinstance(out, (tuple, list)) else out]
        return out

    segs = gather_blocks(segments)
    xs = gather_blocks(after(tokens, segs[2]))
    dys = gather_blocks(after(cotangent, xs[2]))

    perm = pack_matrix()
    fsdp = lax.axis_index("fsdp").astype(jnp.int32).reshape(1)
    col_a, col_m = gain_attn.astype(F32)[:, None], gain_mlp.astype(F32)[:, None]
    shard = jnp.concatenate(
        [
            lax.dynamic_slice_in_dim(w_query, ctx * (QH * HD), QH * HD, 1),
            lax.dynamic_slice_in_dim(w_key, ctx * (KH * HD), KH * HD, 1),
            lax.dynamic_slice_in_dim(w_value, ctx * (KH * HD), KH * HD, 1),
        ],
        axis=1,
    )
    shard = jnp.dot(shard, perm, preferred_element_type=F32)
    shard = (shard * col_a).astype(BF)
    quarter = width // CTX
    w_qkv = lax.all_gather(shard, "fsdp", axis=0, tiled=True)
    out_part = gather_fsdp(lax.dynamic_slice_in_dim(w_out, ctx * quarter, quarter, 1))
    out_parts = gather_blocks(out_part)
    down_t = jnp.transpose(w_down)
    ff = w_gate.shape[1] // 2
    w_parts = []
    for n in range(2):
        cols = slice(n * ff, (n + 1) * ff)
        part = jnp.concatenate(
            [
                (w_gate[:, cols].astype(F32) * col_m).astype(BF),
                (w_up[:, cols].astype(F32) * col_m).astype(BF),
                down_t[:, cols],
            ],
            axis=1,
        )
        part = after(part, *(segs[2:3] if n else [shard]))
        w_parts.append(lax.all_gather(part, "fsdp", axis=0, tiled=True))
    w_one, w_two = w_parts

    seg_blocks = jnp.stack(segs)
    whole_seg = jnp.concatenate(
        [lax.dynamic_index_in_dim(seg_blocks, b ^ ctx, 0, keepdims=False) for b in range(CTX)], axis=1
    )
    index = jnp.arange(length, dtype=jnp.int32)
    starts = jnp.concatenate(
        [jnp.ones((seqs, 1), dtype=bool), whole_seg[:, 1:] != whole_seg[:, :-1]], axis=1
    )
    first = lax.cummax(jnp.where(starts, index[None, :], 0), axis=1)
    positions = (index[None, :] - first).astype(F32).reshape(seqs * length, 1)
    freq = np.zeros((LANES,), np.float32)
    base = (THETA ** -(np.arange(HALF, dtype=np.float64) * 2.0 / HD)).astype(np.float32)
    for g in range(KH):
        freq[g * HALF : (g + 1) * HALF] = base
    angles = positions * jnp.asarray(freq)[None, :]
    cos, sin = jnp.cos(angles), jnp.sin(angles)
    low_block = (first[:, ::BLK] // BLK).reshape(seqs * CTX).astype(jnp.int32)
    first_rows = first.reshape(seqs, CTX, 1, BLK)

    normed, q, k, v = step(lambda t: qkv_call(c, xs, t, cos, sin), w_qkv, first_rows)
    mixed, lse = step(
        lambda t: attend_call(c, low_block, t, k, v, first_rows, seqs, length), q, dys[2]
    )
    r1 = swap_core(jnp.stack([mixed[1], mixed[3]]))
    r2 = swap_row(jnp.stack([mixed[2], r1[1]]))
    w_out_full = step(lambda t: assemble_call(c, fsdp, out_parts[:3] + [t]), out_parts[3])
    resid, normed_two = step(lambda t: out_call(c, tokens, mixed, r1, t, w_out_full), r2)

    n2s = [n.reshape(rows, width) for n in gather_blocks(normed_two)]
    dys = [d.reshape(rows, width) for d in dys]
    first_pairs = [step(lambda t: mlp_call(t, dys[d], w_one), n2s[d]) for d in range(CTX)]
    def gram(pairs, *ready):
        hid, gu = [p[0] for p in pairs], [p[1] for p in pairs]
        return step(lambda t: mlp_gram_call(dys, [t] + n2s[1:], hid, gu, 768), n2s[0], *ready)

    share_one = gram(first_pairs)
    s_one = lax.psum_scatter(share_one, "fsdp", scatter_dimension=0, tiled=True)
    second_pairs = [None] * CTX

    def back_rows(d, *ready):
        def call(t):
            terms = [(first_pairs[d][1], slot, w_one, slot) for slot in range(2)]
            return sum_nt_call(terms + [(t, slot, w_two, slot) for slot in range(2)], 512)

        return step(call, second_pairs[d][1], *ready)

    def down_rows(d, *ready):
        call = lambda t: sum_nt_call([(first_pairs[d][0], None, w_one, 2), (t, None, w_two, 2)], 512)
        return step(call, second_pairs[d][0], *ready)

    def back_pair(near, far, *ready):
        for d in (far, near):
            second_pairs[d] = step(lambda t: mlp_call(t, dys[d], w_two), n2s[d])
        low = back_rows(far)
        return back_rows(near, *ready), swap_core(low)

    dn2 = add_low(*back_pair(2, 3))
    dn_b = swap_row(dn2)
    last.append(dn2)
    dn_a = add_low(*back_pair(0, 1))
    share_two = gram(second_pairs)
    s_two = lax.psum_scatter(share_two, "fsdp", scatter_dimension=0, tiled=True)
    dresid, dattn, dmixed = step(
        lambda t: out_back_call(
            c, dn_a.reshape(tokens.shape), t.reshape(tokens.shape), resid, cotangent, w_out_full
        ),
        dn_b,
    )

    b1 = swap_core(jnp.stack([dmixed[1], dmixed[3]]))
    b2_send = jnp.stack([dmixed[2], b1[1]])
    b2 = swap_row(b2_send)
    g_out = step(lambda t: out_gram_call(c, fsdp, mixed, r1, r2, t), dattn.reshape(rows, width))
    got = swap_core(jnp.stack([g_out[1], g_out[3]]))
    g_send = add_low(g_out[2], got[1])
    low3, low2 = down_rows(3), down_rows(2)
    dqkv = step(
        lambda t: attend_back_call(
            c, low_block, q, k, v, mixed, dmixed, b1[0], t, lse, first_rows, cos, sin, seqs, length
        ),
        b2,
        g_send,
    )
    got_row = swap_row(after(g_send, b2))

    g_out = add_low(add_low(g_out[0], got[0]), after(got_row, dqkv))
    x_out = reduce_x(g_out[0], g_out[1])
    far = step(lambda t: qkv_back_call(c, t, w_qkv, seqs, 2), dqkv, g_out)
    dx2 = add_low(far[0], swap_core(far[1]))
    dx_b = swap_row(dx2)
    near = step(lambda t: qkv_back_call(c, t, w_qkv, seqs, 0), dqkv)
    dx_a = add_low(near[0], swap_core(near[1]))
    qkv_mine, qkv_theirs = step(lambda t: gram_call(fsdp, normed, t), dqkv, x_out)
    down2 = add_low(low2, swap_core(low3))
    down_b = swap_row(after(down2, got_row))
    low1, low0 = down_rows(1, down_b), down_rows(0)
    down_a = add_low(low0, swap_core(low1))
    x_all = jnp.concatenate([reduce_x(qkv_mine, qkv_theirs, dx2), x_out], axis=1)
    s_attn = reduce_z(x_all)
    grad_tokens = step(lambda t: final_call(dx_a, t, tokens, dresid), dx_b, x_all)
    s_down, s_gate, s_up = [
        jnp.concatenate([s[:, n * ff : (n + 1) * ff] for s in (s_one, s_two)], axis=1).astype(F32)
        for n in range(3)
    ]
    part_m = jnp.sum(s_gate * w_gate.astype(F32) + s_up * w_up.astype(F32), axis=1, keepdims=True)
    part_m = jnp.broadcast_to(part_m, (part_m.shape[0], LANES)).astype(BF)
    sums = gather_blocks(after(jnp.concatenate([s_attn, part_m], axis=1), grad_tokens))
    output = (
        resid + down_a.astype(F32).reshape(resid.shape) + down_b.astype(F32).reshape(resid.shape)
    ).astype(BF)
    g_query, g_key, g_value, g_gain_a, g_gain_m, g_w_out = step(
        lambda t: unpack_call(c, sums[:3] + [t], perm, w_query, w_key, w_value, col_a), sums[3]
    )
    return (
        output,
        grad_tokens,
        g_query,
        g_key,
        g_value,
        g_w_out,
        s_gate * col_m,
        s_up * col_m,
        jnp.transpose(s_down),
        g_gain_a[:, 0],
        g_gain_m[:, 0],
    )


def solution(mesh):
    split_heads = mesh.shape["context"] == CTX
    return jax.shard_map(
        on_device if split_heads else on_device_general,
        mesh=mesh,
        in_specs=(
            P("fsdp", "context", None),
            P("fsdp", "context"),
            P("fsdp", None),
            P("fsdp", None),
            P("fsdp", None),
            P("fsdp", None),
            P("fsdp", "context"),
            P("fsdp", "context"),
            P("context", "fsdp"),
            P("fsdp"),
            P("fsdp"),
            P("fsdp", "context", None),
        ),
        out_specs=(
            P("fsdp", "context", None),
            P("fsdp", "context", None),
            P("fsdp", None),
            P("fsdp", None),
            P("fsdp", None),
            P("fsdp", None),
            P("fsdp", "context"),
            P("fsdp", "context"),
            P("context", "fsdp"),
            P("fsdp"),
            P("fsdp"),
        ),
        check_vma=False,
    )
```

```python
import functools
import math

import jax
import jax.numpy as jnp
import numpy as np
from jax import lax
from jax.experimental import pallas as pl
from jax.experimental.pallas import tpu as pltpu
from jax.sharding import PartitionSpec as P

H = 16
KVH = 8
HD = 96


EPSILON = 1e-05
THETA = 100000.0


def rms_scale(values, gain):
    return values * lax.rsqrt(jnp.mean(values * values, axis=-1, keepdims=True) + EPSILON) * gain


def rotate(values, cosines, sines):
    half_width = values.shape[-1] // 2
    leading = values[..., :half_width]
    trailing = values[..., half_width:]
    return jnp.concatenate(
        [leading * cosines - trailing * sines, trailing * cosines + leading * sines], axis=-1
    )


def gated(gate_act, up_act):
    return jax.nn.silu(gate_act) * up_act


def inner(left, right):
    return jnp.einsum("ti,tj->ij", left, right, preferred_element_type=jnp.float32)


def outer_back(grad_rows, weight):
    return jnp.einsum("ti,ji->tj", grad_rows, weight, preferred_element_type=jnp.float32)


def reduce_grads(parts):
    shares = (
        lax.psum_scatter(
            parts[0].astype(jnp.bfloat16), "fsdp", scatter_dimension=0, tiled=True
        ).astype(jnp.float32),
        lax.psum_scatter(
            parts[1].astype(jnp.bfloat16), "fsdp", scatter_dimension=0, tiled=True
        ).astype(jnp.float32),
        lax.psum_scatter(
            parts[2].astype(jnp.bfloat16), "fsdp", scatter_dimension=0, tiled=True
        ).astype(jnp.float32),
        lax.psum_scatter(
            parts[3].astype(jnp.bfloat16), "fsdp", scatter_dimension=0, tiled=True
        ).astype(jnp.float32),
        lax.psum_scatter(
            parts[4].astype(jnp.bfloat16), "fsdp", scatter_dimension=0, tiled=True
        ).astype(jnp.float32),
        lax.psum_scatter(
            parts[5].astype(jnp.bfloat16), "fsdp", scatter_dimension=0, tiled=True
        ).astype(jnp.float32),
    )
    result = (
        lax.psum(shares[0].astype(jnp.bfloat16), "context").astype(jnp.float32),
        lax.psum(shares[1].astype(jnp.bfloat16), "context").astype(jnp.float32),
        lax.psum(shares[2].astype(jnp.bfloat16), "context").astype(jnp.float32),
        lax.psum(shares[3].astype(jnp.bfloat16), "context").astype(jnp.float32),
        lax.psum(shares[4].astype(jnp.bfloat16), "context").astype(jnp.float32),
        lax.psum(shares[5].astype(jnp.bfloat16), "context").astype(jnp.float32),
    )
    return result


def gather_attention(shard_query, shard_key, shard_value, shard_out, shard_gain_a, shard_gain_m):
    return (
        lax.all_gather(shard_query, "fsdp", axis=0, tiled=True),
        lax.all_gather(shard_key, "fsdp", axis=0, tiled=True),
        lax.all_gather(shard_value, "fsdp", axis=0, tiled=True),
        lax.all_gather(shard_out, "fsdp", axis=0, tiled=True),
        lax.all_gather(shard_gain_a, "fsdp", axis=0, tiled=True),
        lax.all_gather(shard_gain_m, "fsdp", axis=0, tiled=True),
    )


def gather_mlp(shard_gate, shard_up, shard_down):
    return (
        lax.all_gather(shard_gate, "fsdp", axis=0, tiled=True),
        lax.all_gather(shard_up, "fsdp", axis=0, tiled=True),
        lax.all_gather(shard_down, "fsdp", axis=1, tiled=True),
    )


def on_device_general(
    tokens,
    segments,
    w_query,
    w_key,
    w_value,
    w_out,
    w_gate,
    w_up,
    w_down,
    gain_attn,
    gain_mlp,
    cotangent,
):
    seq_count, tok_local, model_width = tokens.shape
    row_count = seq_count * tok_local
    groups = H // KVH
    kv_width = KVH * HD
    logit_scale = 1.0 / math.sqrt(HD)
    whole_seg = lax.all_gather(segments, "context", axis=1, tiled=True)
    length = whole_seg.shape[1]
    all_rows = seq_count * length
    offset = lax.axis_index("context") * tok_local
    key_index = jnp.arange(length, dtype=jnp.int32)
    query_index = offset + jnp.arange(tok_local, dtype=jnp.int32)
    starts = jnp.concatenate(
        [jnp.ones((seq_count, 1), dtype=bool), whole_seg[:, 1:] != whole_seg[:, :-1]], axis=1
    )
    first_index = lax.cummax(jnp.where(starts, key_index[None, :], 0), axis=1)
    positions = lax.dynamic_slice_in_dim(key_index[None, :] - first_index, offset, tok_local, 1)
    frequency = jnp.power(THETA, -(jnp.arange(HD // 2, dtype=jnp.float32) * 2.0 / HD))
    angles = positions.astype(jnp.float32)[:, :, None] * frequency[None, None, :]
    cosines = jnp.cos(angles).reshape(row_count, 1, HD // 2)
    sines = jnp.sin(angles).reshape(row_count, 1, HD // 2)
    x_flat = tokens.reshape(row_count, model_width).astype(jnp.float32)

    def masked_scores(query_sequence, k_seq, q_seg, k_seg):
        unscaled_scores = (
            jnp.einsum(
                "wxif,axf->xiwa",
                query_sequence,
                k_seq.reshape(length, KVH, HD),
                preferred_element_type=jnp.float32,
            )
            * logit_scale
        )
        allowed = (q_seg[:, None] == k_seg[None, :]) & (key_index[None, :] <= query_index[:, None])
        return jnp.where(allowed[None, None], unscaled_scores, -1e30)

    def attend(items):
        query_sequence, k_seq, v_seq, q_seg, k_seg = items
        scores = masked_scores(query_sequence, k_seq, q_seg, k_seg)
        top_score = jnp.max(scores, axis=-1, keepdims=True)
        weights = jnp.exp(scores - top_score)
        total = jnp.sum(weights, axis=-1, keepdims=True)
        attention_probabilities = (weights / total).astype(jnp.bfloat16)
        mixed_seq = jnp.einsum(
            "uvqe,eua->quva",
            attention_probabilities,
            v_seq.reshape(length, KVH, HD),
            preferred_element_type=jnp.float32,
        ).astype(jnp.bfloat16)
        return (mixed_seq, top_score + jnp.log(total))

    def forward(attn_weights, mlp_weights):
        full_query, full_key, full_value, full_out, full_gain_a, full_gain_m = attn_weights
        normed = rms_scale(x_flat, full_gain_a.astype(jnp.float32)).astype(jnp.bfloat16)
        queries = jnp.dot(normed, full_query, preferred_element_type=jnp.float32).reshape(
            row_count, H, HD
        )
        key_rows = jnp.dot(normed, full_key, preferred_element_type=jnp.float32).reshape(
            row_count, KVH, HD
        )
        value_matrix_rows = jnp.dot(normed, full_value, preferred_element_type=jnp.float32).astype(
            jnp.bfloat16
        )
        qrot = (
            rotate(queries, cosines, sines)
            .astype(jnp.bfloat16)
            .reshape(seq_count, tok_local, KVH, groups, HD)
        )
        rotary_keys = (
            rotate(key_rows, cosines, sines)
            .astype(jnp.bfloat16)
            .reshape(seq_count, tok_local, kv_width)
        )
        all_keys, all_values = (
            lax.all_gather(rotary_keys, "context", axis=1, tiled=True),
            lax.all_gather(
                value_matrix_rows.reshape(seq_count, tok_local, kv_width),
                "context",
                axis=1,
                tiled=True,
            ),
        )
        mixed, log_totals = lax.map(attend, (qrot, all_keys, all_values, segments, whole_seg))
        mixed_flat = mixed.reshape(row_count, H * HD)
        resid = x_flat + jnp.dot(mixed_flat, full_out, preferred_element_type=jnp.float32)
        full_gate, full_up, full_down = mlp_weights
        normed_two = rms_scale(resid, full_gain_m.astype(jnp.float32)).astype(jnp.bfloat16)
        all_normed_two = lax.all_gather(
            normed_two.reshape(seq_count, tok_local, model_width), "context", axis=1, tiled=True
        ).reshape(all_rows, model_width)
        gate_act = jnp.dot(all_normed_two, full_gate, preferred_element_type=jnp.float32)
        up_act = jnp.dot(all_normed_two, full_up, preferred_element_type=jnp.float32)
        hidden = gated(gate_act, up_act).astype(jnp.bfloat16)
        partial_down = jnp.dot(hidden, full_down, preferred_element_type=jnp.float32)
        down_sum = (
            lax.psum_scatter(
                partial_down.reshape(seq_count, length, model_width).astype(jnp.bfloat16),
                "context",
                scatter_dimension=1,
                tiled=True,
            )
            .astype(jnp.float32)
            .reshape(row_count, model_width)
        )
        final = resid + down_sum
        return (
            final,
            normed,
            qrot,
            all_keys,
            all_values,
            mixed,
            log_totals,
            resid,
            all_normed_two,
            gate_act,
            up_act,
            hidden,
        )

    attn_weights = gather_attention(w_query, w_key, w_value, w_out, gain_attn, gain_mlp)
    mlp_weights = gather_mlp(w_gate, w_up, w_down)
    state = forward(attn_weights, mlp_weights)
    output = state[0].astype(jnp.bfloat16).reshape(seq_count, tok_local, model_width)
    (
        final,
        normed,
        qrot,
        all_keys,
        all_values,
        mixed,
        log_totals,
        resid,
        all_normed_two,
        gate_act,
        up_act,
        hidden,
    ) = state
    full_query, full_key, full_value, full_out, full_gain_a, full_gain_m = attn_weights
    full_gate, full_up, full_down = mlp_weights
    grad_out = cotangent.reshape(row_count, model_width)
    all_grad_out = lax.all_gather(cotangent, "context", axis=1, tiled=True).reshape(
        all_rows, model_width
    )
    grad_down_t = inner(all_grad_out, hidden)
    grad_hidden = outer_back(all_grad_out, full_down)
    gate_pull = jax.vjp(gated, gate_act, up_act)[1]
    grad_gate_f, grad_up_f = gate_pull(grad_hidden)
    grad_gate_act = grad_gate_f.astype(jnp.bfloat16)
    grad_up_act = grad_up_f.astype(jnp.bfloat16)
    grad_gate = inner(all_normed_two, grad_gate_act)
    grad_up = inner(all_normed_two, grad_up_act)
    part_normed_two = outer_back(grad_gate_act, full_gate) + outer_back(grad_up_act, full_up)
    grad_normed_two = lax.psum_scatter(
        part_normed_two.reshape(seq_count, length, model_width),
        "context",
        scatter_dimension=1,
        tiled=True,
    ).reshape(row_count, model_width)
    norm_pull = jax.vjp(rms_scale, resid, full_gain_m.astype(jnp.float32))[1]
    back_resid, grad_gain_m = norm_pull(grad_normed_two)
    mlp_shares = (
        lax.psum_scatter(
            grad_gate.astype(jnp.bfloat16), "fsdp", scatter_dimension=0, tiled=True
        ).astype(jnp.float32),
        lax.psum_scatter(
            grad_up.astype(jnp.bfloat16), "fsdp", scatter_dimension=0, tiled=True
        ).astype(jnp.float32),
        lax.psum_scatter(
            grad_down_t.astype(jnp.bfloat16), "fsdp", scatter_dimension=0, tiled=True
        ).astype(jnp.float32),
    )
    grad_resid = grad_out.astype(jnp.float32) + back_resid
    grad_attn = grad_resid.astype(jnp.bfloat16)
    mixed_flat = mixed.reshape(row_count, H * HD)
    grad_out_w = inner(mixed_flat, grad_attn)
    grad_mixed = (
        outer_back(grad_attn, full_out)
        .astype(jnp.bfloat16)
        .reshape(seq_count, tok_local, KVH, groups, HD)
    )

    def attend_back(items):
        query_sequence, k_seq, v_seq, q_seg, k_seg, log_total, grad_seq = items
        scores = masked_scores(query_sequence, k_seq, q_seg, k_seg)
        attention_probabilities = jnp.exp(scores - log_total)
        grad_probs = jnp.einsum(
            "wxif,axf->xiwa",
            grad_seq,
            v_seq.reshape(length, KVH, HD),
            preferred_element_type=jnp.float32,
        )
        weighted = jnp.sum(attention_probabilities * grad_probs, axis=-1, keepdims=True)
        score_gradient = (attention_probabilities * (grad_probs - weighted)).astype(jnp.bfloat16)
        grad_q = (
            jnp.einsum(
                "uvqe,eua->quva",
                score_gradient,
                k_seq.reshape(length, KVH, HD),
                preferred_element_type=jnp.float32,
            )
            * logit_scale
        )
        grad_k = (
            jnp.einsum(
                "jnbp,bjny->pjy", score_gradient, query_sequence, preferred_element_type=jnp.float32
            )
            * logit_scale
        )
        grad_v = jnp.einsum(
            "jnbp,bjny->pjy",
            attention_probabilities.astype(jnp.bfloat16),
            grad_seq,
            preferred_element_type=jnp.float32,
        )
        return (grad_q, grad_k.reshape(length, kv_width), grad_v.reshape(length, kv_width))

    grad_qrot, part_keys, part_values = lax.map(
        attend_back, (qrot, all_keys, all_values, segments, whole_seg, log_totals, grad_mixed)
    )
    grad_krot, grad_vals = (
        lax.psum_scatter(
            part_keys.astype(jnp.bfloat16), "context", scatter_dimension=1, tiled=True
        ).astype(jnp.float32),
        lax.psum_scatter(
            part_values.astype(jnp.bfloat16), "context", scatter_dimension=1, tiled=True
        ).astype(jnp.float32),
    )
    grad_queries = (
        rotate(grad_qrot.reshape(row_count, H, HD), cosines, -sines)
        .astype(jnp.bfloat16)
        .reshape(row_count, H * HD)
    )
    grad_keys = (
        rotate(grad_krot.reshape(row_count, KVH, HD), cosines, -sines)
        .astype(jnp.bfloat16)
        .reshape(row_count, kv_width)
    )
    grad_values = grad_vals.reshape(row_count, kv_width).astype(jnp.bfloat16)
    grad_query_w = inner(normed, grad_queries)
    grad_key_w = inner(normed, grad_keys)
    grad_value_w = inner(normed, grad_values)
    grad_normed = (
        outer_back(grad_queries, full_query)
        + outer_back(grad_keys, full_key)
        + outer_back(grad_values, full_value)
    )
    first_pull = jax.vjp(rms_scale, x_flat, full_gain_a.astype(jnp.float32))[1]
    back_input, grad_gain_a = first_pull(grad_normed)
    attn_grads = reduce_grads(
        (grad_query_w, grad_key_w, grad_value_w, grad_out_w, grad_gain_a, grad_gain_m)
    )
    grad_input = (grad_resid + back_input).reshape(seq_count, tok_local, model_width)
    return (
        output,
        grad_input,
        attn_grads[0],
        attn_grads[1],
        attn_grads[2],
        attn_grads[3],
        mlp_shares[0],
        mlp_shares[1],
        jnp.transpose(mlp_shares[2]),
        attn_grads[4],
        attn_grads[5],
    )


BF = jnp.bfloat16
F32 = jnp.float32
LANES = 128
HALF = HD // 2
NEG = -1e30
SCALE = 1.0 / math.sqrt(HD)
SCALE_LOG2 = SCALE * math.log2(math.e)
CTX = 4
QH = H // CTX
KH = KVH // CTX
BLK = 256
SHARE = 0.25
NT = (((1,), (1,)), ((), ()))
TN = (((0,), (0,)), ((), ()))


def dot_nt(a, b):
    return lax.dot_general(a, b, NT, preferred_element_type=F32)


def dot_tn(a, b):
    return lax.dot_general(a, b, TN, preferred_element_type=F32)


def dot_nn(a, b):
    return jnp.dot(a, b, preferred_element_type=F32)


def lane_iota(rows, width):
    return lax.broadcasted_iota(jnp.int32, (rows, width), 1)


def params(mb, sem):
    return pltpu.CompilerParams(vmem_limit_bytes=mb << 20, dimension_semantics=sem)


def cost(micros):
    return pl.CostEstimate(flops=int(micros * SHARE * 1.15e9), bytes_accessed=0, transcendentals=0)


def packed_columns():
    src = []
    for group in range(6):
        if group < 4:
            member, half = group // 2, group % 2
            for g in range(KH):
                head = 2 * g + member
                src += [head * HD + half * HALF + t for t in range(HALF)]
        else:
            half = group - 4
            for g in range(KH):
                src += [QH * HD + g * HD + half * HALF + t for t in range(HALF)]
        src += [(QH + KH) * HD + group * 32 + t for t in range(32)]
    return np.array(src, np.int32)


def pack_matrix():
    n = (QH + 2 * KH) * HD
    src = jnp.asarray(packed_columns())
    return (lax.broadcasted_iota(jnp.int32, (n, n), 0) == src[None, :]).astype(BF)


def rms_rows(x):
    return x * lax.rsqrt(jnp.mean(x * x, axis=-1, keepdims=True) + EPSILON)


def qkv_kernel(c_ref, x0, x1, x2, x3, w, cos, sin, normed, q, k, v, xs):
    for d, ref in enumerate((x0, x1, x2, x3)):

        @pl.when(pl.program_id(0) == d)
        def _():
            xs[...] = ref[0]

    n = rms_rows(xs[...].astype(F32)).astype(BF)
    normed[...] = n
    t = dot_nn(n, w[...])
    y = [t[:, LANES * p : LANES * (p + 1)] for p in range(6)]
    c, s = cos[...], sin[...]
    rot = []
    for p in range(0, 6, 2):
        rot += [y[p] * c - y[p + 1] * s, y[p + 1] * c + y[p] * s]
    for p in range(4):
        q[:, LANES * p : LANES * (p + 1)] = rot[p].astype(BF)
    for p in range(2):
        k[:, LANES * p : LANES * (p + 1)] = rot[4 + p].astype(BF)
    quarter = lane_iota(y[0].shape[0], LANES) // 32

    def place(parts):
        out = jnp.ones_like(y[0])
        for dst, p in parts:
            piece = y[p] if dst == 3 else pltpu.roll(y[p], 32 * (dst + 1), 1)
            out = jnp.where(quarter == dst, piece, out)
        return out.astype(BF)

    v[:, 0:128] = place(((0, 0), (1, 1), (2, 2), (3, 0)))
    v[:, 128:256] = place(((0, 1), (1, 2)))
    v[:, 256:384] = place(((2, 3), (3, 4)))
    v[:, 384:512] = place(((0, 5), (1, 3), (2, 4), (3, 5)))


def qkv_call(c, xs, w, cos, sin):
    seqs, tok, width = xs[0].shape
    total = seqs * CTX * tok
    cols = 768

    def own(d):
        return pl.BlockSpec(
            (1, tok, width),
            lambda i, s, c: (jnp.where(i == d, s, jnp.where(i < d, 0, seqs - 1)), 0, 0),
        )

    def rows(n):
        return pl.BlockSpec((tok, n), lambda i, s, c: (s * CTX + (i ^ c[0]), 0))

    return pl.pallas_call(
        qkv_kernel,
        grid_spec=pltpu.PrefetchScalarGridSpec(
            num_scalar_prefetch=1,
            grid=(CTX, seqs),
            in_specs=[
                own(0),
                own(1),
                own(2),
                own(3),
                pl.BlockSpec((width, cols), lambda i, s, c: (0, 0)),
                rows(LANES),
                rows(LANES),
            ],
            out_specs=[rows(width), rows(512), rows(256), rows(512)],
            scratch_shapes=[pltpu.VMEM((tok, width), BF)],
        ),
        out_shape=[
            jax.ShapeDtypeStruct((total, width), BF),
            jax.ShapeDtypeStruct((total, 512), BF),
            jax.ShapeDtypeStruct((total, 256), BF),
            jax.ShapeDtypeStruct((total, 512), BF),
        ],
        compiler_params=params(40, ("arbitrary", "arbitrary")),
        cost_estimate=cost(13),
        name="qkv",
    )(c, *xs, w, cos, sin)


def head_masks(rows):
    lane = lane_iota(rows, 256)
    inner_lane = lane % LANES
    by_kv = [inner_lane < HALF, (inner_lane >= HALF) & (inner_lane < HD)]
    in_mixed = [
        lane < HD,
        (lane >= HD) & (lane < 2 * HD),
        (lane >= 64) & (lane < 64 + HD),
        lane >= 64 + HD,
    ]
    return lane, by_kv, in_mixed


def attend_kernel(js_ref, c_ref, q, k, v, start, mixed, lse, vt_s, m_s, o_s):
    s_id, i = pl.program_id(0), pl.program_id(1)
    blocks = k.shape[0] // BLK
    lane, by_kv, in_mixed = head_masks(BLK)
    sub = lax.broadcasted_iota(jnp.int32, (256, BLK), 0)
    take_a = (sub < HD) | ((sub >= 192) & (sub < 224))
    take_b = ((sub >= 64) & (sub < 64 + HD)) | (sub < 32)
    zero = jnp.zeros((BLK, 256), BF)

    @pl.when(i == 0)
    def _():
        for b in range(blocks):
            vt_s[b] = jnp.transpose(v[b * BLK : (b + 1) * BLK, :])

    m_s[...] = jnp.full_like(m_s, -jnp.inf)
    o_s[...] = jnp.zeros_like(o_s)
    col = i * BLK + lax.broadcasted_iota(jnp.int32, (BLK, BLK), 1)
    first = start[0, 0]
    low = js_ref[s_id * CTX + i]

    def step(t, _):
        j = i - t
        kb = k[pl.ds(pl.multiple_of(j * BLK, BLK), BLK), :]
        row = j * BLK + lax.broadcasted_iota(jnp.int32, (BLK, BLK), 0)
        bias = jnp.where((row >= first) & (row <= col), 0.0, NEG)
        for win, take in enumerate((take_a, take_b)):
            vt = vt_s[j, 256 * win : 256 * (win + 1), :]
            outs, alphas = [], []
            for m in range(2):
                h = 2 * win + m
                qh = jnp.where(by_kv[win], q[:, 256 * m : 256 * (m + 1)], zero)
                sc = dot_nt(kb, qh) * SCALE_LOG2 + bias
                m_old = m_s[h : h + 1, :]
                m_new = jnp.maximum(m_old, jnp.max(sc, axis=0, keepdims=True))
                p = jnp.exp2(sc - m_new)
                alphas.append(jnp.exp2(m_old - m_new))
                m_s[h : h + 1, :] = m_new
                outs.append(dot_nn(vt, p.astype(BF)))
            o_s[win] = o_s[win] * jnp.where(take, alphas[0], alphas[1]) + jnp.where(take, outs[0], outs[1])
        return 0

    lax.fori_loop(0, i - low + 1, step, 0)
    sums = [o_s[0, 192:193, :], o_s[0, 224:225, :], o_s[1, 0:1, :], o_s[1, 32:33, :]]
    inv = [1.0 / x for x in sums]
    a = jnp.transpose(o_s[0] * jnp.where(take_a, inv[0], inv[1]))
    b = jnp.transpose(o_s[1] * jnp.where(take_b, inv[2], inv[3]))
    mixed[0, 0, :, 0:128] = a[:, 0:128].astype(BF)
    mixed[0, 0, :, 128:256] = jnp.where(lane[:, :LANES] < 64, a[:, 128:256], b[:, 0:128]).astype(BF)
    mixed[0, 0, :, 256:384] = b[:, 128:256].astype(BF)
    lse[0, 0] = jnp.zeros_like(lse[0, 0])
    for h in range(QH):
        lse[0, 0, h : h + 1, :] = m_s[h : h + 1, :] + jnp.log2(sums[h])


def attend_call(c, js, q, k, v, start, seqs, length):
    blocks = length // BLK
    return pl.pallas_call(
        attend_kernel,
        grid_spec=pltpu.PrefetchScalarGridSpec(
            num_scalar_prefetch=2,
            grid=(seqs, blocks),
            in_specs=[
                pl.BlockSpec((BLK, 512), lambda s, i, js, c: (s * CTX + i, 0)),
                pl.BlockSpec((length, 256), lambda s, i, js, c: (s, 0)),
                pl.BlockSpec((length, 512), lambda s, i, js, c: (s, 0)),
                pl.BlockSpec((1, 1, 1, BLK), lambda s, i, js, c: (s, i, 0, 0)),
            ],
            out_specs=[
                pl.BlockSpec((1, 1, BLK, QH * HD), lambda s, i, js, c: (i ^ c[0], s, 0, 0)),
                pl.BlockSpec((1, 1, 8, BLK), lambda s, i, js, c: (s, i, 0, 0)),
            ],
            scratch_shapes=[
                pltpu.VMEM((blocks, 512, BLK), BF),
                pltpu.VMEM((8, BLK), F32),
                pltpu.VMEM((2, 256, BLK), F32),
            ],
        ),
        out_shape=[
            jax.ShapeDtypeStruct((CTX, seqs, BLK, QH * HD), BF),
            jax.ShapeDtypeStruct((seqs, blocks, 8, BLK), F32),
        ],
        compiler_params=params(40, ("arbitrary", "arbitrary")),
        cost_estimate=cost(18),
        name="attend",
    )(js, c, q, k, v, start)


def attend_back_kernel(
    js_ref, c_ref, q, k, v, o, d0, d1, d23, lse, start, cos, sin, out, do_s, dl_s, kt_s, dq_s, dk_s, dv_s
):
    s_id = pl.program_id(0)
    c = c_ref[0]
    blocks = q.shape[0] // BLK
    lane, by_kv, in_mixed = head_masks(BLK)
    zero = jnp.zeros((BLK, 256), BF)
    mixed_lane = lane_iota(8, QH * HD)
    mixed_row = lax.broadcasted_iota(jnp.int32, (8, QH * HD), 0)
    picks = (mixed_lane // HD == mixed_row).astype(F32)
    for d in range(CTX):
        b = d ^ c
        rows = pl.ds(pl.multiple_of(b * BLK, BLK), BLK)
        g = d0[0, 0] if d == 0 else d1[0] if d == 1 else d23[d - 2, 0]
        do_s[rows, :] = g
        prod = g.astype(F32) * o[d, 0].astype(F32)
        dl_s[b] = lax.dot_general(
            picks, prod, NT, preferred_element_type=F32, precision=lax.Precision.HIGHEST
        )
    for b in range(blocks):
        kt_s[b] = jnp.transpose(k[b * BLK : (b + 1) * BLK, :])
    sub_in = lax.broadcasted_iota(jnp.int32, (256, BLK), 0) % LANES
    sub_kv = [sub_in < HALF, (sub_in >= HALF) & (sub_in < HD)]
    dq_s[...] = jnp.zeros_like(dq_s)
    dk_s[...] = jnp.zeros_like(dk_s)
    dv_s[...] = jnp.zeros_like(dv_s)

    def outer(i, _):
        qs = pl.ds(pl.multiple_of(i * BLK, BLK), BLK)
        col = i * BLK + lax.broadcasted_iota(jnp.int32, (BLK, BLK), 1)
        first = start[0, i]
        delta = dl_s[i]
        logs = lse[0, i]

        def step(t, _):
            j = i - t
            ks = pl.ds(pl.multiple_of(j * BLK, BLK), BLK)
            kb = k[ks, :]
            kt = kt_s[j]
            row = j * BLK + lax.broadcasted_iota(jnp.int32, (BLK, BLK), 0)
            bias = jnp.where((row >= first) & (row <= col), 0.0, NEG)
            dk = jnp.zeros((BLK, 256), F32)
            dq = [jnp.zeros((256, BLK), F32) for _ in range(2)]
            for win in range(KH):
                vb = v[ks, 256 * win : 256 * (win + 1)]
                kg = jnp.where(sub_kv[win], kt, zero)
                dv = jnp.zeros((BLK, 256), F32)
                for m in range(2):
                    h = 2 * win + m
                    qh = jnp.where(by_kv[win], q[qs, 256 * m : 256 * (m + 1)], zero)
                    do = jnp.where(in_mixed[h], do_s[qs, LANES * win : LANES * win + 256], zero)
                    sc = dot_nt(kb, qh) * SCALE_LOG2 + bias
                    p = jnp.exp2(sc - logs[h : h + 1, :])
                    dp = dot_nt(vb, do)
                    ds = (p * (dp - delta[h : h + 1, :])).astype(BF)
                    dv = dv + dot_nn(p.astype(BF), do)
                    dk = dk + dot_nn(ds, qh)
                    dq[m] = dq[m] + dot_nn(kg, ds)
                dv_s[ks, 256 * win : 256 * (win + 1)] += dv
            dk_s[ks, :] += dk
            for m in range(2):
                dq_s[i, m] += dq[m]
            return 0

        lax.fori_loop(0, i - js_ref[s_id * CTX + i] + 1, step, 0)
        return 0

    lax.fori_loop(0, blocks, outer, 0)
    head_lane = lane[:, :LANES] < HD

    def finish(i, _):
        rows = pl.ds(pl.multiple_of(i * BLK, BLK), BLK)
        cs, sn = cos[rows, :] * SCALE, sin[rows, :] * SCALE
        a0, a1 = dv_s[rows, 0:128], dv_s[rows, 128:256]
        b0, b1 = dv_s[rows, 256:384], dv_s[rows, 384:512]

        def r(x, n):
            return pltpu.roll(x, n, 1)

        pieces = [
            r(a0, 96) + a0,
            r(a0, 64) + r(a1, 96),
            r(a0, 32) + r(a1, 64),
            r(b0, 32) + r(b1, 64),
            b0 + r(b1, 32),
            r(b1, 96) + b1,
        ]
        grads = []
        for m in range(2):
            dq = jnp.transpose(dq_s[i, m])
            grads += [dq[:, 0:128], dq[:, 128:256]]
        grads += [dk_s[rows, 0:128], dk_s[rows, 128:256]]
        for p in range(0, 6, 2):
            first_half = grads[p] * cs + grads[p + 1] * sn
            second_half = grads[p + 1] * cs - grads[p] * sn
            out[rows, LANES * p : LANES * (p + 1)] = jnp.where(head_lane, first_half, pieces[p]).astype(BF)
            out[rows, LANES * (p + 1) : LANES * (p + 2)] = jnp.where(
                head_lane, second_half, pieces[p + 1]
            ).astype(BF)
        return 0

    lax.fori_loop(0, blocks, finish, 0)


def attend_back_call(c, js, q, k, v, o, d0, d1, d23, lse, start, cos, sin, seqs, length):
    blocks = length // BLK
    width = QH * HD
    return pl.pallas_call(
        attend_back_kernel,
        grid_spec=pltpu.PrefetchScalarGridSpec(
            num_scalar_prefetch=2,
            grid=(seqs,),
            in_specs=[
                pl.BlockSpec((length, 512), lambda s, js, c: (s, 0)),
                pl.BlockSpec((length, 256), lambda s, js, c: (s, 0)),
                pl.BlockSpec((length, 512), lambda s, js, c: (s, 0)),
                pl.BlockSpec((CTX, 1, BLK, width), lambda s, js, c: (0, s, 0, 0)),
                pl.BlockSpec((1, 1, BLK, width), lambda s, js, c: (0, s, 0, 0)),
                pl.BlockSpec((1, BLK, width), lambda s, js, c: (s, 0, 0)),
                pl.BlockSpec((2, 1, BLK, width), lambda s, js, c: (0, s, 0, 0)),
                pl.BlockSpec((1, blocks, 8, BLK), lambda s, js, c: (s, 0, 0, 0)),
                pl.BlockSpec((1, blocks, 1, BLK), lambda s, js, c: (s, 0, 0, 0)),
                pl.BlockSpec((length, LANES), lambda s, js, c: (s, 0)),
                pl.BlockSpec((length, LANES), lambda s, js, c: (s, 0)),
            ],
            out_specs=pl.BlockSpec((length, 768), lambda s, js, c: (s, 0)),
            scratch_shapes=[
                pltpu.VMEM((length, width), BF),
                pltpu.VMEM((blocks, 8, BLK), F32),
                pltpu.VMEM((blocks, 256, BLK), BF),
                pltpu.VMEM((blocks, 2, 256, BLK), F32),
                pltpu.VMEM((length, 256), F32),
                pltpu.VMEM((length, 512), F32),
            ],
        ),
        out_shape=jax.ShapeDtypeStruct((seqs * length, 768), BF),
        compiler_params=params(48, ("arbitrary",)),
        cost_estimate=cost(31),
        name="attend_back",
    )(js, c, q, k, v, o, d0, d1, d23, lse, start, cos, sin)


def assemble_kernel(c_ref, f_ref, p0, p1, p2, p3, out):
    quarter = p0.shape[-1]
    for b in range(CTX):
        for d, ref in enumerate((p0, p1, p2, p3)):

            @pl.when((b ^ c_ref[0]) == d)
            def _():
                out[:, b * quarter : (b + 1) * quarter] = ref[0]


def assemble_call(c, f, parts):
    count, rows, quarter = parts[0].shape
    part = pl.BlockSpec((1, rows, quarter), lambda b, c, f: (b ^ f[0], 0, 0))
    return pl.pallas_call(
        assemble_kernel,
        grid_spec=pltpu.PrefetchScalarGridSpec(
            num_scalar_prefetch=2,
            grid=(count,),
            in_specs=[part] * CTX,
            out_specs=pl.BlockSpec((rows, CTX * quarter), lambda b, c, f: (b, 0)),
        ),
        out_shape=jax.ShapeDtypeStruct((count * rows, CTX * quarter), BF),
        compiler_params=params(20, ("arbitrary",)),
        cost_estimate=cost(5),
        name="assemble",
    )(c, f, *parts)


def out_kernel(c_ref, x, m0, m1, m2, m3, w, resid, normed):
    c = c_ref[0]
    acc = x[0].astype(F32)
    for d, ref in enumerate((m0, m1, m2, m3)):
        rows = pl.ds(pl.multiple_of((d ^ c) * (QH * HD), QH * HD), QH * HD)
        acc = acc + dot_nn(ref[0, 0], w[rows, :])
    resid[0] = acc
    normed[0] = rms_rows(acc).astype(BF)


def out_call(c, x, mixed, r1, r2, w):
    seqs, tok, width = x.shape
    inner_w = QH * HD

    def slot(n):
        return pl.BlockSpec((1, 1, tok, inner_w), lambda s, c: (n, s, 0, 0))

    tile = pl.BlockSpec((1, tok, width), lambda s, c: (s, 0, 0))
    return pl.pallas_call(
        out_kernel,
        grid_spec=pltpu.PrefetchScalarGridSpec(
            num_scalar_prefetch=1,
            grid=(seqs,),
            in_specs=[
                tile,
                slot(0),
                slot(0),
                slot(0),
                slot(1),
                pl.BlockSpec((H * HD, width), lambda s, c: (0, 0)),
            ],
            out_specs=[tile, tile],
        ),
        out_shape=[
            jax.ShapeDtypeStruct((seqs, tok, width), F32),
            jax.ShapeDtypeStruct((seqs, tok, width), BF),
        ],
        compiler_params=params(48, ("arbitrary",)),
        cost_estimate=cost(8),
        name="out_proj",
    )(c, x, mixed, r1, r2, r2, w)


def rms_back(v, dyg):
    r = lax.rsqrt(jnp.mean(v * v, axis=-1, keepdims=True) + EPSILON)
    return r * dyg - v * (r * r * r * jnp.mean(dyg * v, axis=-1, keepdims=True))


def out_back_kernel(c_ref, part_a, part_b, resid, dy, w, dresid, dattn, dmixed):
    c = c_ref[0]
    dn = part_a[0].astype(F32) + part_b[0].astype(F32)
    total = dy[0].astype(F32) + rms_back(resid[0], dn)
    dresid[0] = total
    low = total.astype(BF)
    dattn[0] = low
    for d in range(CTX):
        rows = pl.ds(pl.multiple_of((d ^ c) * (QH * HD), QH * HD), QH * HD)
        dmixed[d, 0] = dot_nt(low, w[rows, :]).astype(BF)


def out_back_call(c, part_a, part_b, resid, dy, w):
    seqs, tok, width = dy.shape
    inner_w = QH * HD
    tile = pl.BlockSpec((1, tok, width), lambda s, c: (s, 0, 0))
    return pl.pallas_call(
        out_back_kernel,
        grid_spec=pltpu.PrefetchScalarGridSpec(
            num_scalar_prefetch=1,
            grid=(seqs,),
            in_specs=[
                tile,
                tile,
                tile,
                tile,
                pl.BlockSpec((H * HD, width), lambda s, c: (0, 0)),
            ],
            out_specs=[
                tile,
                tile,
                pl.BlockSpec((CTX, 1, tok, inner_w), lambda s, c: (0, s, 0, 0)),
            ],
        ),
        out_shape=[
            jax.ShapeDtypeStruct((seqs, tok, width), F32),
            jax.ShapeDtypeStruct((seqs, tok, width), BF),
            jax.ShapeDtypeStruct((CTX, seqs, tok, inner_w), BF),
        ],
        compiler_params=params(56, ("arbitrary",)),
        cost_estimate=cost(9.5),
        name="out_back",
    )(c, part_a, part_b, resid, dy, w)


def mlp_kernel(n2, dy, wg, wu, wd, hidden, grads):
    n, g_out = n2[...], dy[...]
    gate = dot_nn(n, wg[...])
    up = dot_nn(n, wu[...])
    dh = dot_nn(g_out, wd[...])
    sig = 1.0 / (1.0 + jnp.exp(-gate))
    act = gate * sig
    hidden[...] = (act * up).astype(BF)
    cols = wg.shape[1]
    grads[0] = (dh * up * (sig + act * (1.0 - sig))).astype(BF)
    grads[1] = (dh * act).astype(BF)


def mlp_call(n2, dy, w):
    rows, width = n2.shape
    ff = w.shape[1] // 3
    tile = BLK
    steps = ff // tile
    full = pl.BlockSpec((rows, width), lambda j: (0, 0))
    return pl.pallas_call(
        mlp_kernel,
        grid=(steps,),
        in_specs=[
            full,
            full,
            pl.BlockSpec((width, tile), lambda j: (0, j)),
            pl.BlockSpec((width, tile), lambda j: (0, j + steps)),
            pl.BlockSpec((width, tile), lambda j: (0, j + 2 * steps)),
        ],
        out_specs=[
            pl.BlockSpec((rows, tile), lambda j: (0, j)),
            pl.BlockSpec((2, rows, tile), lambda j: (0, 0, j)),
        ],
        out_shape=[
            jax.ShapeDtypeStruct((rows, ff), BF),
            jax.ShapeDtypeStruct((2, rows, ff), BF),
        ],
        compiler_params=params(40, ("arbitrary",)),
        cost_estimate=cost(4.5),
        name="mlp",
    )(n2, dy, w, w, w)


def sum_nt_kernel(slots, *refs):
    count = len(slots)
    out = refs[-1]
    acc = None
    for n in range(count):
        left = refs[n]
        part = dot_nt(left[0] if len(left.shape) == 3 else left[...], refs[count + n][...])
        acc = part if acc is None else acc + part
    out[...] = acc.astype(out.dtype)


def sum_nt_call(terms, tile):
    rows, k = terms[0][0].shape[-2:]
    n = terms[0][2].shape[0]
    lefts, rights = [], []
    for array, slot, weight, window in terms:
        if slot is None:
            lefts.append(pl.BlockSpec((rows, k), lambda j: (0, 0)))
        else:
            lefts.append(pl.BlockSpec((1, rows, k), functools.partial(lambda slot, j: (slot, 0, 0), slot)))
        rights.append(pl.BlockSpec((tile, k), functools.partial(lambda window, j: (j, window), window)))
    count = len(terms)
    return pl.pallas_call(
        functools.partial(sum_nt_kernel, tuple(t[1] for t in terms)),
        grid=(n // tile,),
        in_specs=lefts + rights,
        out_specs=pl.BlockSpec((rows, tile), lambda j: (0, j)),
        out_shape=jax.ShapeDtypeStruct((rows, n), BF),
        compiler_params=params(40, ("arbitrary",)),
        cost_estimate=cost(4.4),
        name="sum_nt",
    )(*[t[0] for t in terms], *[t[2] for t in terms])


def put_sides(f_ref, acc, mine, theirs):
    acc = acc.astype(BF)
    count, rows, _ = mine.shape
    for side in range(2):

        @pl.when(f_ref[0] % 2 == side)
        def _():
            for z in range(count):
                at = 2 * z * rows
                mine[z] = acc[at + side * rows : at + (side + 1) * rows]
                theirs[z] = acc[at + (1 - side) * rows : at + (2 - side) * rows]


def mlp_gram_kernel(count, *refs):
    dys, n2s = refs[:count], refs[count : 2 * count]
    hid, gu = refs[2 * count : 3 * count], refs[3 * count : 4 * count]
    out = refs[-1]

    @pl.when(pl.program_id(0) == 0)
    def _():
        acc = dot_tn(dys[0][...], hid[0][...])
        for n in range(1, count):
            acc = acc + dot_tn(dys[n][...], hid[n][...])
        out[...] = acc.astype(out.dtype)

    @pl.when(pl.program_id(0) != 0)
    def _():
        acc = dot_tn(n2s[0][...], gu[0][0])
        for n in range(1, count):
            acc = acc + dot_tn(n2s[n][...], gu[n][0])
        out[...] = acc.astype(out.dtype)


def mlp_gram_call(dys, n2s, hid, gu, tile_m):
    rows, m = dys[0].shape
    k = hid[0].shape[1]
    count = len(dys)
    return pl.pallas_call(
        functools.partial(mlp_gram_kernel, count),
        grid=(3, m // tile_m),
        in_specs=[pl.BlockSpec((rows, tile_m), lambda j, i: (0, jnp.where(j == 0, i, m // tile_m - 1)))] * count
        + [pl.BlockSpec((rows, tile_m), lambda j, i: (0, jnp.where(j == 0, 0, i)))] * count
        + [pl.BlockSpec((rows, k), lambda j, i: (0, 0))] * count
        + [pl.BlockSpec((1, rows, k), lambda j, i: (jnp.maximum(j - 1, 0), 0, 0))] * count,
        out_specs=pl.BlockSpec((tile_m, k), lambda j, i: (i, j)),
        out_shape=jax.ShapeDtypeStruct((m, 3 * k), BF),
        compiler_params=params(56, ("arbitrary", "arbitrary")),
        cost_estimate=cost(18),
        name="mlp_gram",
    )(*dys, *n2s, *hid, *gu)


def gram_kernel(f_ref, left, right, mine, theirs):
    put_sides(f_ref, dot_tn(left[...], right[...]), mine, theirs)


def gram_call(f, left, right):
    rows, m = left.shape
    n = right.shape[1]
    one = pl.BlockSpec((2, m // 8, n), lambda i, f: (i, 0, 0))
    return pl.pallas_call(
        gram_kernel,
        grid_spec=pltpu.PrefetchScalarGridSpec(
            num_scalar_prefetch=1,
            grid=(2,),
            in_specs=[
                pl.BlockSpec((rows, m // 2), lambda i, f: (0, i)),
                pl.BlockSpec((rows, n), lambda i, f: (0, 0)),
            ],
            out_specs=[one, one],
        ),
        out_shape=[jax.ShapeDtypeStruct((4, m // 8, n), BF)] * 2,
        compiler_params=params(40, ("arbitrary",)),
        cost_estimate=cost(6),
        name="gram",
    )(f, left, right)


def out_gram_kernel(c_ref, f_ref, m0, m1, m2, m3, dattn, out):
    side = f_ref[0] % 2
    rows = out.shape[3]
    for d, ref in enumerate((m0, m1, m2, m3)):

        @pl.when(pl.program_id(0) == d)
        def _():
            tok = ref.shape[1] * ref.shape[2]
            acc = dot_tn(ref[0].reshape(tok, ref.shape[3]), dattn[...]).astype(BF)

            @pl.when(side == 0)
            def _():
                out[0, 0, 0] = acc[:rows]
                out[0, 1, 0] = acc[rows:]

            @pl.when(side != 0)
            def _():
                out[0, 0, 0] = acc[rows:]
                out[0, 1, 0] = acc[:rows]


def out_gram_call(c, f, mixed, r1, r2, dattn):
    seqs, tok, inner_w = mixed.shape[1:]
    rows, width = dattn.shape
    quarter = width // CTX

    def slot(n):
        return pl.BlockSpec((1, seqs, tok, inner_w), lambda d, e, c, f: (n, 0, 0, 0))

    return pl.pallas_call(
        out_gram_kernel,
        grid_spec=pltpu.PrefetchScalarGridSpec(
            num_scalar_prefetch=2,
            grid=(CTX, CTX),
            in_specs=[
                slot(0),
                slot(0),
                slot(0),
                slot(1),
                pl.BlockSpec((rows, quarter), lambda d, e, c, f: (0, e ^ c[0])),
            ],
            out_specs=pl.BlockSpec(
                (1, 2, 1, inner_w // 2, quarter), lambda d, e, c, f: (e, 0, d ^ c[0], 0, 0)
            ),
        ),
        out_shape=jax.ShapeDtypeStruct((CTX, 2, 4, inner_w // 2, quarter), BF),
        compiler_params=params(40, ("arbitrary", "arbitrary")),
        cost_estimate=cost(9),
        name="out_gram",
    )(c, f, mixed, r1, r2, r2, dattn)


def unpack_kernel(c_ref, s0, s1, s2, s3, perm, wq, wk, wv, gain, gq, gk, gv, gg, gm, go):
    c = c_ref[0]
    qw, kw = QH * HD, KH * HD
    n = perm.shape[0]
    g = gain[...]
    for b in range(CTX):
        for d, ref in enumerate((s0, s1, s2, s3)):

            @pl.when((b ^ c) == d)
            def _():
                flat = dot_nt(ref[:, :n], perm[...])
                gq[:, b * qw : (b + 1) * qw] = flat[:, :qw]
                gk[:, b * kw : (b + 1) * kw] = flat[:, qw : qw + kw]
                gv[:, b * kw : (b + 1) * kw] = flat[:, qw + kw :]
                go[:, b * qw : (b + 1) * qw] = ref[:, n : n + qw].astype(F32)

    total = jnp.zeros_like(g)
    for grad, w in ((gq, wq), (gk, wk), (gv, wv)):
        total = total + jnp.sum(grad[...] * w[...].astype(F32), axis=-1, keepdims=True)
        grad[...] = grad[...] * g
    gg[...] = total
    gm[...] = (
        s0[:, n + qw :].astype(F32)
        + s1[:, n + qw :].astype(F32)
        + s2[:, n + qw :].astype(F32)
        + s3[:, n + qw :].astype(F32)
    )[:, 0:1]


def unpack_call(c, parts, perm, wq, wk, wv, gain):
    rows = parts[0].shape[0]
    vm = pl.BlockSpec(memory_space=pltpu.VMEM)
    return pl.pallas_call(
        unpack_kernel,
        in_specs=[pl.BlockSpec(memory_space=pltpu.SMEM)] + [vm] * 9,
        out_specs=[vm] * 6,
        out_shape=[
            jax.ShapeDtypeStruct((rows, H * HD), F32),
            jax.ShapeDtypeStruct((rows, KVH * HD), F32),
            jax.ShapeDtypeStruct((rows, KVH * HD), F32),
            jax.ShapeDtypeStruct((rows, 1), F32),
            jax.ShapeDtypeStruct((rows, 1), F32),
            jax.ShapeDtypeStruct((rows, CTX * QH * HD), F32),
        ],
        compiler_params=pltpu.CompilerParams(vmem_limit_bytes=40 << 20),
        cost_estimate=cost(5),
        name="unpack",
    )(c, *parts, perm, wq, wk, wv, gain)


def qkv_back_kernel(c_ref, g, w, out):
    out[0, 0] = dot_nt(g[...], w[...]).astype(BF)


def qkv_back_call(c, grads, w, seqs, base):
    width = w.shape[0]
    return pl.pallas_call(
        qkv_back_kernel,
        grid_spec=pltpu.PrefetchScalarGridSpec(
            num_scalar_prefetch=1,
            grid=(2, seqs),
            in_specs=[
                pl.BlockSpec((BLK, 768), lambda d, s, c: (s * CTX + ((d + base) ^ c[0]), 0)),
                pl.BlockSpec((width, 768), lambda d, s, c: (0, 0)),
            ],
            out_specs=pl.BlockSpec((1, 1, BLK, width), lambda d, s, c: (d, s, 0, 0)),
        ),
        out_shape=jax.ShapeDtypeStruct((2, seqs, BLK, width), BF),
        compiler_params=params(40, ("arbitrary", "arbitrary")),
        cost_estimate=cost(3.3),
        name="qkv_back",
    )(c, grads, w)


def final_kernel(part_a, part_b, x, dresid, out):
    dn = part_a[0].astype(F32) + part_b[0].astype(F32)
    out[0] = dresid[0] + rms_back(x[0].astype(F32), dn)


def final_call(part_a, part_b, x, dresid):
    seqs, tok, width = x.shape
    tile = pl.BlockSpec((1, tok, width), lambda s: (s, 0, 0))
    return pl.pallas_call(
        final_kernel,
        grid=(seqs,),
        in_specs=[tile] * 4,
        out_specs=tile,
        out_shape=jax.ShapeDtypeStruct((seqs, tok, width), F32),
        compiler_params=params(40, ("arbitrary",)),
        cost_estimate=cost(4),
        name="final",
    )(part_a, part_b, x, dresid)


CORE = [(i, i ^ 1) for i in range(CTX)]
ROW = [(i, i ^ 2) for i in range(CTX)]


def swap_core(x):
    return lax.ppermute(x, "context", CORE)


def swap_row(x):
    return lax.ppermute(x, "context", ROW)


def gather_blocks(x):
    far = swap_row(x)
    near = swap_core(x)
    return [x, near, far, swap_core(far)]


def after(x, *first):
    return lax.optimization_barrier((x,) + first)[0]


def swap_fsdp(x, bit):
    size = lax.axis_size("fsdp")
    return lax.ppermute(x, "fsdp", [(i, i ^ bit) for i in range(size)])


def gather_fsdp(x):
    near = swap_fsdp(x, 2)
    side = swap_fsdp(x, 1)
    far = swap_fsdp(jnp.stack([x, near]), 4)
    near_side = swap_fsdp(near, 1)
    far_side = swap_fsdp(far, 1)
    return jnp.stack([x, side, near, near_side, far[0], far_side[0], far[1], far_side[1]])


def z_groups():
    size = lax.axis_size("fsdp")
    return [list(range(0, size, 2)), list(range(1, size, 2))]


def reduce_x(mine, theirs, *first):
    total = add_low(after(mine, *first), swap_fsdp(theirs, 1))
    return total.reshape(-1, total.shape[-1])


def reduce_z(x):
    return lax.psum_scatter(x, "fsdp", scatter_dimension=0, tiled=True, axis_index_groups=z_groups())


def add_low(a, b):
    return (a.astype(F32) + b.astype(F32)).astype(BF)


def on_device(
    tokens,
    segments,
    w_query,
    w_key,
    w_value,
    w_out,
    w_gate,
    w_up,
    w_down,
    gain_attn,
    gain_mlp,
    cotangent,
):
    seqs, tok, width = tokens.shape
    rows = seqs * tok
    length = tok * CTX
    qkv_w = (QH + 2 * KH) * HD
    ctx = lax.axis_index("context")
    core = ctx % 2
    c = ctx.astype(jnp.int32).reshape(1)

    last = []

    def step(call, x, *ready):
        x = after(x, *last, *ready)
        out = call(x)
        last[:] = [out[0] if isinstance(out, (tuple, list)) else out]
        return out

    segs = gather_blocks(segments)
    xs = gather_blocks(after(tokens, segs[2]))
    dys = gather_blocks(after(cotangent, xs[2]))

    perm = pack_matrix()
    fsdp = lax.axis_index("fsdp").astype(jnp.int32).reshape(1)
    col_a, col_m = gain_attn.astype(F32)[:, None], gain_mlp.astype(F32)[:, None]
    shard = jnp.concatenate(
        [
            lax.dynamic_slice_in_dim(w_query, ctx * (QH * HD), QH * HD, 1),
            lax.dynamic_slice_in_dim(w_key, ctx * (KH * HD), KH * HD, 1),
            lax.dynamic_slice_in_dim(w_value, ctx * (KH * HD), KH * HD, 1),
        ],
        axis=1,
    )
    shard = jnp.dot(shard, perm, preferred_element_type=F32)
    shard = (shard * col_a).astype(BF)
    quarter = width // CTX
    w_qkv = lax.all_gather(shard, "fsdp", axis=0, tiled=True)
    out_part = gather_fsdp(lax.dynamic_slice_in_dim(w_out, ctx * quarter, quarter, 1))
    out_parts = gather_blocks(out_part)
    down_t = jnp.transpose(w_down)
    ff = w_gate.shape[1] // 2
    w_parts = []
    for n in range(2):
        cols = slice(n * ff, (n + 1) * ff)
        part = jnp.concatenate(
            [
                (w_gate[:, cols].astype(F32) * col_m).astype(BF),
                (w_up[:, cols].astype(F32) * col_m).astype(BF),
                down_t[:, cols],
            ],
            axis=1,
        )
        part = after(part, *(segs[2:3] if n else [shard]))
        w_parts.append(lax.all_gather(part, "fsdp", axis=0, tiled=True))
    w_one, w_two = w_parts

    seg_blocks = jnp.stack(segs)
    whole_seg = jnp.concatenate(
        [lax.dynamic_index_in_dim(seg_blocks, b ^ ctx, 0, keepdims=False) for b in range(CTX)], axis=1
    )
    index = jnp.arange(length, dtype=jnp.int32)
    starts = jnp.concatenate(
        [jnp.ones((seqs, 1), dtype=bool), whole_seg[:, 1:] != whole_seg[:, :-1]], axis=1
    )
    first = lax.cummax(jnp.where(starts, index[None, :], 0), axis=1)
    positions = (index[None, :] - first).astype(F32).reshape(seqs * length, 1)
    freq = np.zeros((LANES,), np.float32)
    base = (THETA ** -(np.arange(HALF, dtype=np.float64) * 2.0 / HD)).astype(np.float32)
    for g in range(KH):
        freq[g * HALF : (g + 1) * HALF] = base
    angles = positions * jnp.asarray(freq)[None, :]
    cos, sin = jnp.cos(angles), jnp.sin(angles)
    low_block = (first[:, ::BLK] // BLK).reshape(seqs * CTX).astype(jnp.int32)
    first_rows = first.reshape(seqs, CTX, 1, BLK)

    normed, q, k, v = step(lambda t: qkv_call(c, xs, t, cos, sin), w_qkv, first_rows)
    mixed, lse = step(
        lambda t: attend_call(c, low_block, t, k, v, first_rows, seqs, length), q, dys[2]
    )
    r1 = swap_core(jnp.stack([mixed[1], mixed[3]]))
    r2 = swap_row(jnp.stack([mixed[2], r1[1]]))
    w_out_full = step(lambda t: assemble_call(c, fsdp, out_parts[:3] + [t]), out_parts[3])
    resid, normed_two = step(lambda t: out_call(c, tokens, mixed, r1, t, w_out_full), r2)

    n2s = [n.reshape(rows, width) for n in gather_blocks(normed_two)]
    dys = [d.reshape(rows, width) for d in dys]
    first_pairs = [step(lambda t: mlp_call(t, dys[d], w_one), n2s[d]) for d in range(CTX)]
    def gram(pairs, *ready):
        hid, gu = [p[0] for p in pairs], [p[1] for p in pairs]
        return step(lambda t: mlp_gram_call(dys, [t] + n2s[1:], hid, gu, 768), n2s[0], *ready)

    share_one = gram(first_pairs)
    s_one = lax.psum_scatter(share_one, "fsdp", scatter_dimension=0, tiled=True)
    second_pairs = [None] * CTX

    def back_rows(d, *ready):
        def call(t):
            terms = [(first_pairs[d][1], slot, w_one, slot) for slot in range(2)]
            return sum_nt_call(terms + [(t, slot, w_two, slot) for slot in range(2)], 512)

        return step(call, second_pairs[d][1], *ready)

    def down_rows(d, *ready):
        call = lambda t: sum_nt_call([(first_pairs[d][0], None, w_one, 2), (t, None, w_two, 2)], 512)
        return step(call, second_pairs[d][0], *ready)

    def back_pair(near, far, *ready):
        for d in (far, near):
            second_pairs[d] = step(lambda t: mlp_call(t, dys[d], w_two), n2s[d])
        low = back_rows(far)
        return back_rows(near, *ready), swap_core(low)

    dn2 = add_low(*back_pair(2, 3))
    dn_b = swap_row(dn2)
    last.append(dn2)
    dn_a = add_low(*back_pair(0, 1))
    share_two = gram(second_pairs)
    s_two = lax.psum_scatter(share_two, "fsdp", scatter_dimension=0, tiled=True)
    dresid, dattn, dmixed = step(
        lambda t: out_back_call(
            c, dn_a.reshape(tokens.shape), t.reshape(tokens.shape), resid, cotangent, w_out_full
        ),
        dn_b,
    )

    b1 = swap_core(jnp.stack([dmixed[1], dmixed[3]]))
    b2_send = jnp.stack([dmixed[2], b1[1]])
    b2 = swap_row(b2_send)
    g_out = step(lambda t: out_gram_call(c, fsdp, mixed, r1, r2, t), dattn.reshape(rows, width))
    got = swap_core(jnp.stack([g_out[1], g_out[3]]))
    g_send = add_low(g_out[2], got[1])
    low3, low2 = down_rows(3), down_rows(2)
    dqkv = step(
        lambda t: attend_back_call(
            c, low_block, q, k, v, mixed, dmixed, b1[0], t, lse, first_rows, cos, sin, seqs, length
        ),
        b2,
        g_send,
    )
    got_row = swap_row(after(g_send, b2))

    g_out = add_low(add_low(g_out[0], got[0]), after(got_row, dqkv))
    x_out = reduce_x(g_out[0], g_out[1])
    qkv_mine, qkv_theirs = step(lambda t: gram_call(fsdp, normed, t), dqkv, g_out)
    far = step(lambda t: qkv_back_call(c, t, w_qkv, seqs, 2), dqkv, x_out)
    dx2 = add_low(far[0], swap_core(far[1]))
    dx_b = swap_row(dx2)
    near = step(lambda t: qkv_back_call(c, t, w_qkv, seqs, 0), dqkv)
    dx_a = add_low(near[0], swap_core(near[1]))
    down2 = add_low(low2, swap_core(low3))
    down_b = swap_row(after(down2, got_row))
    low1, low0 = down_rows(1, down_b, dx2), down_rows(0)
    down_a = add_low(low0, swap_core(low1))
    x_all = jnp.concatenate([reduce_x(qkv_mine, qkv_theirs, near), x_out], axis=1)
    s_attn = reduce_z(x_all)
    grad_tokens = step(lambda t: final_call(dx_a, t, tokens, dresid), dx_b, x_all)
    s_down, s_gate, s_up = [
        jnp.concatenate([s[:, n * ff : (n + 1) * ff] for s in (s_one, s_two)], axis=1).astype(F32)
        for n in range(3)
    ]
    part_m = jnp.sum(s_gate * w_gate.astype(F32) + s_up * w_up.astype(F32), axis=1, keepdims=True)
    part_m = jnp.broadcast_to(part_m, (part_m.shape[0], LANES)).astype(BF)
    sums = gather_blocks(after(jnp.concatenate([s_attn, part_m], axis=1), grad_tokens))
    output = (
        resid + down_a.astype(F32).reshape(resid.shape) + down_b.astype(F32).reshape(resid.shape)
    ).astype(BF)
    g_query, g_key, g_value, g_gain_a, g_gain_m, g_w_out = step(
        lambda t: unpack_call(c, sums[:3] + [t], perm, w_query, w_key, w_value, col_a), sums[3]
    )
    return (
        output,
        grad_tokens,
        g_query,
        g_key,
        g_value,
        g_w_out,
        s_gate * col_m,
        s_up * col_m,
        jnp.transpose(s_down),
        g_gain_a[:, 0],
        g_gain_m[:, 0],
    )


def solution(mesh):
    split_heads = mesh.shape["context"] == CTX
    return jax.shard_map(
        on_device if split_heads else on_device_general,
        mesh=mesh,
        in_specs=(
            P("fsdp", "context", None),
            P("fsdp", "context"),
            P("fsdp", None),
            P("fsdp", None),
            P("fsdp", None),
            P("fsdp", None),
            P("fsdp", "context"),
            P("fsdp", "context"),
            P("context", "fsdp"),
            P("fsdp"),
            P("fsdp"),
            P("fsdp", "context", None),
        ),
        out_specs=(
            P("fsdp", "context", None),
            P("fsdp", "context", None),
            P("fsdp", None),
            P("fsdp", None),
            P("fsdp", None),
            P("fsdp", None),
            P("fsdp", "context"),
            P("fsdp", "context"),
            P("context", "fsdp"),
            P("fsdp"),
            P("fsdp"),
        ),
        check_vma=False,
    )
```

```python
import functools
import math

import jax
import jax.numpy as jnp
import numpy as np
from jax import lax
from jax.experimental import pallas as pl
from jax.experimental.pallas import tpu as pltpu
from jax.sharding import PartitionSpec as P

H = 16
KVH = 8
HD = 96


EPSILON = 1e-05
THETA = 100000.0


def rms_scale(values, gain):
    return values * lax.rsqrt(jnp.mean(values * values, axis=-1, keepdims=True) + EPSILON) * gain


def rotate(values, cosines, sines):
    half_width = values.shape[-1] // 2
    leading = values[..., :half_width]
    trailing = values[..., half_width:]
    return jnp.concatenate(
        [leading * cosines - trailing * sines, trailing * cosines + leading * sines], axis=-1
    )


def gated(gate_act, up_act):
    return jax.nn.silu(gate_act) * up_act


def inner(left, right):
    return jnp.einsum("ti,tj->ij", left, right, preferred_element_type=jnp.float32)


def outer_back(grad_rows, weight):
    return jnp.einsum("ti,ji->tj", grad_rows, weight, preferred_element_type=jnp.float32)


def reduce_grads(parts):
    shares = (
        lax.psum_scatter(
            parts[0].astype(jnp.bfloat16), "fsdp", scatter_dimension=0, tiled=True
        ).astype(jnp.float32),
        lax.psum_scatter(
            parts[1].astype(jnp.bfloat16), "fsdp", scatter_dimension=0, tiled=True
        ).astype(jnp.float32),
        lax.psum_scatter(
            parts[2].astype(jnp.bfloat16), "fsdp", scatter_dimension=0, tiled=True
        ).astype(jnp.float32),
        lax.psum_scatter(
            parts[3].astype(jnp.bfloat16), "fsdp", scatter_dimension=0, tiled=True
        ).astype(jnp.float32),
        lax.psum_scatter(
            parts[4].astype(jnp.bfloat16), "fsdp", scatter_dimension=0, tiled=True
        ).astype(jnp.float32),
        lax.psum_scatter(
            parts[5].astype(jnp.bfloat16), "fsdp", scatter_dimension=0, tiled=True
        ).astype(jnp.float32),
    )
    result = (
        lax.psum(shares[0].astype(jnp.bfloat16), "context").astype(jnp.float32),
        lax.psum(shares[1].astype(jnp.bfloat16), "context").astype(jnp.float32),
        lax.psum(shares[2].astype(jnp.bfloat16), "context").astype(jnp.float32),
        lax.psum(shares[3].astype(jnp.bfloat16), "context").astype(jnp.float32),
        lax.psum(shares[4].astype(jnp.bfloat16), "context").astype(jnp.float32),
        lax.psum(shares[5].astype(jnp.bfloat16), "context").astype(jnp.float32),
    )
    return result


def gather_attention(shard_query, shard_key, shard_value, shard_out, shard_gain_a, shard_gain_m):
    return (
        lax.all_gather(shard_query, "fsdp", axis=0, tiled=True),
        lax.all_gather(shard_key, "fsdp", axis=0, tiled=True),
        lax.all_gather(shard_value, "fsdp", axis=0, tiled=True),
        lax.all_gather(shard_out, "fsdp", axis=0, tiled=True),
        lax.all_gather(shard_gain_a, "fsdp", axis=0, tiled=True),
        lax.all_gather(shard_gain_m, "fsdp", axis=0, tiled=True),
    )


def gather_mlp(shard_gate, shard_up, shard_down):
    return (
        lax.all_gather(shard_gate, "fsdp", axis=0, tiled=True),
        lax.all_gather(shard_up, "fsdp", axis=0, tiled=True),
        lax.all_gather(shard_down, "fsdp", axis=1, tiled=True),
    )


def on_device_general(
    tokens,
    segments,
    w_query,
    w_key,
    w_value,
    w_out,
    w_gate,
    w_up,
    w_down,
    gain_attn,
    gain_mlp,
    cotangent,
):
    seq_count, tok_local, model_width = tokens.shape
    row_count = seq_count * tok_local
    groups = H // KVH
    kv_width = KVH * HD
    logit_scale = 1.0 / math.sqrt(HD)
    whole_seg = lax.all_gather(segments, "context", axis=1, tiled=True)
    length = whole_seg.shape[1]
    all_rows = seq_count * length
    offset = lax.axis_index("context") * tok_local
    key_index = jnp.arange(length, dtype=jnp.int32)
    query_index = offset + jnp.arange(tok_local, dtype=jnp.int32)
    starts = jnp.concatenate(
        [jnp.ones((seq_count, 1), dtype=bool), whole_seg[:, 1:] != whole_seg[:, :-1]], axis=1
    )
    first_index = lax.cummax(jnp.where(starts, key_index[None, :], 0), axis=1)
    positions = lax.dynamic_slice_in_dim(key_index[None, :] - first_index, offset, tok_local, 1)
    frequency = jnp.power(THETA, -(jnp.arange(HD // 2, dtype=jnp.float32) * 2.0 / HD))
    angles = positions.astype(jnp.float32)[:, :, None] * frequency[None, None, :]
    cosines = jnp.cos(angles).reshape(row_count, 1, HD // 2)
    sines = jnp.sin(angles).reshape(row_count, 1, HD // 2)
    x_flat = tokens.reshape(row_count, model_width).astype(jnp.float32)

    def masked_scores(query_sequence, k_seq, q_seg, k_seg):
        unscaled_scores = (
            jnp.einsum(
                "wxif,axf->xiwa",
                query_sequence,
                k_seq.reshape(length, KVH, HD),
                preferred_element_type=jnp.float32,
            )
            * logit_scale
        )
        allowed = (q_seg[:, None] == k_seg[None, :]) & (key_index[None, :] <= query_index[:, None])
        return jnp.where(allowed[None, None], unscaled_scores, -1e30)

    def attend(items):
        query_sequence, k_seq, v_seq, q_seg, k_seg = items
        scores = masked_scores(query_sequence, k_seq, q_seg, k_seg)
        top_score = jnp.max(scores, axis=-1, keepdims=True)
        weights = jnp.exp(scores - top_score)
        total = jnp.sum(weights, axis=-1, keepdims=True)
        attention_probabilities = (weights / total).astype(jnp.bfloat16)
        mixed_seq = jnp.einsum(
            "uvqe,eua->quva",
            attention_probabilities,
            v_seq.reshape(length, KVH, HD),
            preferred_element_type=jnp.float32,
        ).astype(jnp.bfloat16)
        return (mixed_seq, top_score + jnp.log(total))

    def forward(attn_weights, mlp_weights):
        full_query, full_key, full_value, full_out, full_gain_a, full_gain_m = attn_weights
        normed = rms_scale(x_flat, full_gain_a.astype(jnp.float32)).astype(jnp.bfloat16)
        queries = jnp.dot(normed, full_query, preferred_element_type=jnp.float32).reshape(
            row_count, H, HD
        )
        key_rows = jnp.dot(normed, full_key, preferred_element_type=jnp.float32).reshape(
            row_count, KVH, HD
        )
        value_matrix_rows = jnp.dot(normed, full_value, preferred_element_type=jnp.float32).astype(
            jnp.bfloat16
        )
        qrot = (
            rotate(queries, cosines, sines)
            .astype(jnp.bfloat16)
            .reshape(seq_count, tok_local, KVH, groups, HD)
        )
        rotary_keys = (
            rotate(key_rows, cosines, sines)
            .astype(jnp.bfloat16)
            .reshape(seq_count, tok_local, kv_width)
        )
        all_keys, all_values = (
            lax.all_gather(rotary_keys, "context", axis=1, tiled=True),
            lax.all_gather(
                value_matrix_rows.reshape(seq_count, tok_local, kv_width),
                "context",
                axis=1,
                tiled=True,
            ),
        )
        mixed, log_totals = lax.map(attend, (qrot, all_keys, all_values, segments, whole_seg))
        mixed_flat = mixed.reshape(row_count, H * HD)
        resid = x_flat + jnp.dot(mixed_flat, full_out, preferred_element_type=jnp.float32)
        full_gate, full_up, full_down = mlp_weights
        normed_two = rms_scale(resid, full_gain_m.astype(jnp.float32)).astype(jnp.bfloat16)
        all_normed_two = lax.all_gather(
            normed_two.reshape(seq_count, tok_local, model_width), "context", axis=1, tiled=True
        ).reshape(all_rows, model_width)
        gate_act = jnp.dot(all_normed_two, full_gate, preferred_element_type=jnp.float32)
        up_act = jnp.dot(all_normed_two, full_up, preferred_element_type=jnp.float32)
        hidden = gated(gate_act, up_act).astype(jnp.bfloat16)
        partial_down = jnp.dot(hidden, full_down, preferred_element_type=jnp.float32)
        down_sum = (
            lax.psum_scatter(
                partial_down.reshape(seq_count, length, model_width).astype(jnp.bfloat16),
                "context",
                scatter_dimension=1,
                tiled=True,
            )
            .astype(jnp.float32)
            .reshape(row_count, model_width)
        )
        final = resid + down_sum
        return (
            final,
            normed,
            qrot,
            all_keys,
            all_values,
            mixed,
            log_totals,
            resid,
            all_normed_two,
            gate_act,
            up_act,
            hidden,
        )

    attn_weights = gather_attention(w_query, w_key, w_value, w_out, gain_attn, gain_mlp)
    mlp_weights = gather_mlp(w_gate, w_up, w_down)
    state = forward(attn_weights, mlp_weights)
    output = state[0].astype(jnp.bfloat16).reshape(seq_count, tok_local, model_width)
    (
        final,
        normed,
        qrot,
        all_keys,
        all_values,
        mixed,
        log_totals,
        resid,
        all_normed_two,
        gate_act,
        up_act,
        hidden,
    ) = state
    full_query, full_key, full_value, full_out, full_gain_a, full_gain_m = attn_weights
    full_gate, full_up, full_down = mlp_weights
    grad_out = cotangent.reshape(row_count, model_width)
    all_grad_out = lax.all_gather(cotangent, "context", axis=1, tiled=True).reshape(
        all_rows, model_width
    )
    grad_down_t = inner(all_grad_out, hidden)
    grad_hidden = outer_back(all_grad_out, full_down)
    gate_pull = jax.vjp(gated, gate_act, up_act)[1]
    grad_gate_f, grad_up_f = gate_pull(grad_hidden)
    grad_gate_act = grad_gate_f.astype(jnp.bfloat16)
    grad_up_act = grad_up_f.astype(jnp.bfloat16)
    grad_gate = inner(all_normed_two, grad_gate_act)
    grad_up = inner(all_normed_two, grad_up_act)
    part_normed_two = outer_back(grad_gate_act, full_gate) + outer_back(grad_up_act, full_up)
    grad_normed_two = lax.psum_scatter(
        part_normed_two.reshape(seq_count, length, model_width),
        "context",
        scatter_dimension=1,
        tiled=True,
    ).reshape(row_count, model_width)
    norm_pull = jax.vjp(rms_scale, resid, full_gain_m.astype(jnp.float32))[1]
    back_resid, grad_gain_m = norm_pull(grad_normed_two)
    mlp_shares = (
        lax.psum_scatter(
            grad_gate.astype(jnp.bfloat16), "fsdp", scatter_dimension=0, tiled=True
        ).astype(jnp.float32),
        lax.psum_scatter(
            grad_up.astype(jnp.bfloat16), "fsdp", scatter_dimension=0, tiled=True
        ).astype(jnp.float32),
        lax.psum_scatter(
            grad_down_t.astype(jnp.bfloat16), "fsdp", scatter_dimension=0, tiled=True
        ).astype(jnp.float32),
    )
    grad_resid = grad_out.astype(jnp.float32) + back_resid
    grad_attn = grad_resid.astype(jnp.bfloat16)
    mixed_flat = mixed.reshape(row_count, H * HD)
    grad_out_w = inner(mixed_flat, grad_attn)
    grad_mixed = (
        outer_back(grad_attn, full_out)
        .astype(jnp.bfloat16)
        .reshape(seq_count, tok_local, KVH, groups, HD)
    )

    def attend_back(items):
        query_sequence, k_seq, v_seq, q_seg, k_seg, log_total, grad_seq = items
        scores = masked_scores(query_sequence, k_seq, q_seg, k_seg)
        attention_probabilities = jnp.exp(scores - log_total)
        grad_probs = jnp.einsum(
            "wxif,axf->xiwa",
            grad_seq,
            v_seq.reshape(length, KVH, HD),
            preferred_element_type=jnp.float32,
        )
        weighted = jnp.sum(attention_probabilities * grad_probs, axis=-1, keepdims=True)
        score_gradient = (attention_probabilities * (grad_probs - weighted)).astype(jnp.bfloat16)
        grad_q = (
            jnp.einsum(
                "uvqe,eua->quva",
                score_gradient,
                k_seq.reshape(length, KVH, HD),
                preferred_element_type=jnp.float32,
            )
            * logit_scale
        )
        grad_k = (
            jnp.einsum(
                "jnbp,bjny->pjy", score_gradient, query_sequence, preferred_element_type=jnp.float32
            )
            * logit_scale
        )
        grad_v = jnp.einsum(
            "jnbp,bjny->pjy",
            attention_probabilities.astype(jnp.bfloat16),
            grad_seq,
            preferred_element_type=jnp.float32,
        )
        return (grad_q, grad_k.reshape(length, kv_width), grad_v.reshape(length, kv_width))

    grad_qrot, part_keys, part_values = lax.map(
        attend_back, (qrot, all_keys, all_values, segments, whole_seg, log_totals, grad_mixed)
    )
    grad_krot, grad_vals = (
        lax.psum_scatter(
            part_keys.astype(jnp.bfloat16), "context", scatter_dimension=1, tiled=True
        ).astype(jnp.float32),
        lax.psum_scatter(
            part_values.astype(jnp.bfloat16), "context", scatter_dimension=1, tiled=True
        ).astype(jnp.float32),
    )
    grad_queries = (
        rotate(grad_qrot.reshape(row_count, H, HD), cosines, -sines)
        .astype(jnp.bfloat16)
        .reshape(row_count, H * HD)
    )
    grad_keys = (
        rotate(grad_krot.reshape(row_count, KVH, HD), cosines, -sines)
        .astype(jnp.bfloat16)
        .reshape(row_count, kv_width)
    )
    grad_values = grad_vals.reshape(row_count, kv_width).astype(jnp.bfloat16)
    grad_query_w = inner(normed, grad_queries)
    grad_key_w = inner(normed, grad_keys)
    grad_value_w = inner(normed, grad_values)
    grad_normed = (
        outer_back(grad_queries, full_query)
        + outer_back(grad_keys, full_key)
        + outer_back(grad_values, full_value)
    )
    first_pull = jax.vjp(rms_scale, x_flat, full_gain_a.astype(jnp.float32))[1]
    back_input, grad_gain_a = first_pull(grad_normed)
    attn_grads = reduce_grads(
        (grad_query_w, grad_key_w, grad_value_w, grad_out_w, grad_gain_a, grad_gain_m)
    )
    grad_input = (grad_resid + back_input).reshape(seq_count, tok_local, model_width)
    return (
        output,
        grad_input,
        attn_grads[0],
        attn_grads[1],
        attn_grads[2],
        attn_grads[3],
        mlp_shares[0],
        mlp_shares[1],
        jnp.transpose(mlp_shares[2]),
        attn_grads[4],
        attn_grads[5],
    )


BF = jnp.bfloat16
F32 = jnp.float32
LANES = 128
HALF = HD // 2
NEG = -1e30
SCALE = 1.0 / math.sqrt(HD)
SCALE_LOG2 = SCALE * math.log2(math.e)
CTX = 4
QH = H // CTX
KH = KVH // CTX
BLK = 256
SHARE = 0.25
NT = (((1,), (1,)), ((), ()))
TN = (((0,), (0,)), ((), ()))


def dot_nt(a, b):
    return lax.dot_general(a, b, NT, preferred_element_type=F32)


def dot_tn(a, b):
    return lax.dot_general(a, b, TN, preferred_element_type=F32)


def dot_nn(a, b):
    return jnp.dot(a, b, preferred_element_type=F32)


def lane_iota(rows, width):
    return lax.broadcasted_iota(jnp.int32, (rows, width), 1)


def params(mb, sem):
    return pltpu.CompilerParams(vmem_limit_bytes=mb << 20, dimension_semantics=sem)


def cost(micros):
    return pl.CostEstimate(flops=int(micros * SHARE * 1.15e9), bytes_accessed=0, transcendentals=0)


def packed_columns():
    src = []
    for group in range(6):
        if group < 4:
            member, half = group // 2, group % 2
            for g in range(KH):
                head = 2 * g + member
                src += [head * HD + half * HALF + t for t in range(HALF)]
        else:
            half = group - 4
            for g in range(KH):
                src += [QH * HD + g * HD + half * HALF + t for t in range(HALF)]
        src += [(QH + KH) * HD + group * 32 + t for t in range(32)]
    return np.array(src, np.int32)


def pack_matrix():
    n = (QH + 2 * KH) * HD
    src = jnp.asarray(packed_columns())
    return (lax.broadcasted_iota(jnp.int32, (n, n), 0) == src[None, :]).astype(BF)


def rms_rows(x):
    return x * lax.rsqrt(jnp.mean(x * x, axis=-1, keepdims=True) + EPSILON)


def qkv_kernel(c_ref, x0, x1, x2, x3, w, cos, sin, normed, q, k, v, xs):
    for d, ref in enumerate((x0, x1, x2, x3)):

        @pl.when(pl.program_id(0) == d)
        def _():
            xs[...] = ref[0]

    n = rms_rows(xs[...].astype(F32)).astype(BF)
    normed[...] = n
    t = dot_nn(n, w[...])
    y = [t[:, LANES * p : LANES * (p + 1)] for p in range(6)]
    c, s = cos[...], sin[...]
    rot = []
    for p in range(0, 6, 2):
        rot += [y[p] * c - y[p + 1] * s, y[p + 1] * c + y[p] * s]
    for p in range(4):
        q[:, LANES * p : LANES * (p + 1)] = rot[p].astype(BF)
    for p in range(2):
        k[:, LANES * p : LANES * (p + 1)] = rot[4 + p].astype(BF)
    quarter = lane_iota(y[0].shape[0], LANES) // 32

    def place(parts):
        out = jnp.ones_like(y[0])
        for dst, p in parts:
            piece = y[p] if dst == 3 else pltpu.roll(y[p], 32 * (dst + 1), 1)
            out = jnp.where(quarter == dst, piece, out)
        return out.astype(BF)

    v[:, 0:128] = place(((0, 0), (1, 1), (2, 2), (3, 0)))
    v[:, 128:256] = place(((0, 1), (1, 2)))
    v[:, 256:384] = place(((2, 3), (3, 4)))
    v[:, 384:512] = place(((0, 5), (1, 3), (2, 4), (3, 5)))


def qkv_call(c, xs, w, cos, sin):
    seqs, tok, width = xs[0].shape
    total = seqs * CTX * tok
    cols = 768

    def own(d):
        return pl.BlockSpec(
            (1, tok, width),
            lambda i, s, c: (jnp.where(i == d, s, jnp.where(i < d, 0, seqs - 1)), 0, 0),
        )

    def rows(n):
        return pl.BlockSpec((tok, n), lambda i, s, c: (s * CTX + (i ^ c[0]), 0))

    return pl.pallas_call(
        qkv_kernel,
        grid_spec=pltpu.PrefetchScalarGridSpec(
            num_scalar_prefetch=1,
            grid=(CTX, seqs),
            in_specs=[
                own(0),
                own(1),
                own(2),
                own(3),
                pl.BlockSpec((width, cols), lambda i, s, c: (0, 0)),
                rows(LANES),
                rows(LANES),
            ],
            out_specs=[rows(width), rows(512), rows(256), rows(512)],
            scratch_shapes=[pltpu.VMEM((tok, width), BF)],
        ),
        out_shape=[
            jax.ShapeDtypeStruct((total, width), BF),
            jax.ShapeDtypeStruct((total, 512), BF),
            jax.ShapeDtypeStruct((total, 256), BF),
            jax.ShapeDtypeStruct((total, 512), BF),
        ],
        compiler_params=params(40, ("arbitrary", "arbitrary")),
        cost_estimate=cost(13),
        name="qkv",
    )(c, *xs, w, cos, sin)


def head_masks(rows):
    lane = lane_iota(rows, 256)
    inner_lane = lane % LANES
    by_kv = [inner_lane < HALF, (inner_lane >= HALF) & (inner_lane < HD)]
    in_mixed = [
        lane < HD,
        (lane >= HD) & (lane < 2 * HD),
        (lane >= 64) & (lane < 64 + HD),
        lane >= 64 + HD,
    ]
    return lane, by_kv, in_mixed


def attend_kernel(js_ref, c_ref, q, k, v, start, mixed, lse, vt_s, m_s, o_s):
    s_id, i = pl.program_id(0), pl.program_id(1)
    blocks = k.shape[0] // BLK
    lane, by_kv, in_mixed = head_masks(BLK)
    sub = lax.broadcasted_iota(jnp.int32, (256, BLK), 0)
    take_a = (sub < HD) | ((sub >= 192) & (sub < 224))
    take_b = ((sub >= 64) & (sub < 64 + HD)) | (sub < 32)
    zero = jnp.zeros((BLK, 256), BF)

    @pl.when(i == 0)
    def _():
        for b in range(blocks):
            vt_s[b] = jnp.transpose(v[b * BLK : (b + 1) * BLK, :])

    m_s[...] = jnp.full_like(m_s, -jnp.inf)
    o_s[...] = jnp.zeros_like(o_s)
    col = i * BLK + lax.broadcasted_iota(jnp.int32, (BLK, BLK), 1)
    first = start[0, 0]
    low = js_ref[s_id * CTX + i]

    def step(t, _):
        j = i - t
        kb = k[pl.ds(pl.multiple_of(j * BLK, BLK), BLK), :]
        row = j * BLK + lax.broadcasted_iota(jnp.int32, (BLK, BLK), 0)
        bias = jnp.where((row >= first) & (row <= col), 0.0, NEG)
        for win, take in enumerate((take_a, take_b)):
            vt = vt_s[j, 256 * win : 256 * (win + 1), :]
            outs, alphas = [], []
            for m in range(2):
                h = 2 * win + m
                qh = jnp.where(by_kv[win], q[:, 256 * m : 256 * (m + 1)], zero)
                sc = dot_nt(kb, qh) * SCALE_LOG2 + bias
                m_old = m_s[h : h + 1, :]
                m_new = jnp.maximum(m_old, jnp.max(sc, axis=0, keepdims=True))
                p = jnp.exp2(sc - m_new)
                alphas.append(jnp.exp2(m_old - m_new))
                m_s[h : h + 1, :] = m_new
                outs.append(dot_nn(vt, p.astype(BF)))
            o_s[win] = o_s[win] * jnp.where(take, alphas[0], alphas[1]) + jnp.where(take, outs[0], outs[1])
        return 0

    lax.fori_loop(0, i - low + 1, step, 0)
    sums = [o_s[0, 192:193, :], o_s[0, 224:225, :], o_s[1, 0:1, :], o_s[1, 32:33, :]]
    inv = [1.0 / x for x in sums]
    a = jnp.transpose(o_s[0] * jnp.where(take_a, inv[0], inv[1]))
    b = jnp.transpose(o_s[1] * jnp.where(take_b, inv[2], inv[3]))
    mixed[0, 0, :, 0:128] = a[:, 0:128].astype(BF)
    mixed[0, 0, :, 128:256] = jnp.where(lane[:, :LANES] < 64, a[:, 128:256], b[:, 0:128]).astype(BF)
    mixed[0, 0, :, 256:384] = b[:, 128:256].astype(BF)
    lse[0, 0] = jnp.zeros_like(lse[0, 0])
    for h in range(QH):
        lse[0, 0, h : h + 1, :] = m_s[h : h + 1, :] + jnp.log2(sums[h])


def attend_call(c, js, q, k, v, start, seqs, length):
    blocks = length // BLK
    return pl.pallas_call(
        attend_kernel,
        grid_spec=pltpu.PrefetchScalarGridSpec(
            num_scalar_prefetch=2,
            grid=(seqs, blocks),
            in_specs=[
                pl.BlockSpec((BLK, 512), lambda s, i, js, c: (s * CTX + i, 0)),
                pl.BlockSpec((length, 256), lambda s, i, js, c: (s, 0)),
                pl.BlockSpec((length, 512), lambda s, i, js, c: (s, 0)),
                pl.BlockSpec((1, 1, 1, BLK), lambda s, i, js, c: (s, i, 0, 0)),
            ],
            out_specs=[
                pl.BlockSpec((1, 1, BLK, QH * HD), lambda s, i, js, c: (i ^ c[0], s, 0, 0)),
                pl.BlockSpec((1, 1, 8, BLK), lambda s, i, js, c: (s, i, 0, 0)),
            ],
            scratch_shapes=[
                pltpu.VMEM((blocks, 512, BLK), BF),
                pltpu.VMEM((8, BLK), F32),
                pltpu.VMEM((2, 256, BLK), F32),
            ],
        ),
        out_shape=[
            jax.ShapeDtypeStruct((CTX, seqs, BLK, QH * HD), BF),
            jax.ShapeDtypeStruct((seqs, blocks, 8, BLK), F32),
        ],
        compiler_params=params(40, ("arbitrary", "arbitrary")),
        cost_estimate=cost(18),
        name="attend",
    )(js, c, q, k, v, start)


def attend_back_kernel(
    js_ref, c_ref, q, k, v, o, d0, d1, d23, lse, start, cos, sin, out, do_s, dl_s, kt_s, dq_s, dk_s, dv_s
):
    s_id = pl.program_id(0)
    c = c_ref[0]
    blocks = q.shape[0] // BLK
    lane, by_kv, in_mixed = head_masks(BLK)
    zero = jnp.zeros((BLK, 256), BF)
    mixed_lane = lane_iota(8, QH * HD)
    mixed_row = lax.broadcasted_iota(jnp.int32, (8, QH * HD), 0)
    picks = (mixed_lane // HD == mixed_row).astype(F32)
    for d in range(CTX):
        b = d ^ c
        rows = pl.ds(pl.multiple_of(b * BLK, BLK), BLK)
        g = d0[0, 0] if d == 0 else d1[0] if d == 1 else d23[d - 2, 0]
        do_s[rows, :] = g
        prod = g.astype(F32) * o[d, 0].astype(F32)
        dl_s[b] = lax.dot_general(
            picks, prod, NT, preferred_element_type=F32, precision=lax.Precision.HIGHEST
        )
    for b in range(blocks):
        kt_s[b] = jnp.transpose(k[b * BLK : (b + 1) * BLK, :])
    sub_in = lax.broadcasted_iota(jnp.int32, (256, BLK), 0) % LANES
    sub_kv = [sub_in < HALF, (sub_in >= HALF) & (sub_in < HD)]
    dq_s[...] = jnp.zeros_like(dq_s)
    dk_s[...] = jnp.zeros_like(dk_s)
    dv_s[...] = jnp.zeros_like(dv_s)

    def outer(i, _):
        qs = pl.ds(pl.multiple_of(i * BLK, BLK), BLK)
        col = i * BLK + lax.broadcasted_iota(jnp.int32, (BLK, BLK), 1)
        first = start[0, i]
        delta = dl_s[i]
        logs = lse[0, i]

        def step(t, _):
            j = i - t
            ks = pl.ds(pl.multiple_of(j * BLK, BLK), BLK)
            kb = k[ks, :]
            kt = kt_s[j]
            row = j * BLK + lax.broadcasted_iota(jnp.int32, (BLK, BLK), 0)
            bias = jnp.where((row >= first) & (row <= col), 0.0, NEG)
            dk = jnp.zeros((BLK, 256), F32)
            dq = [jnp.zeros((256, BLK), F32) for _ in range(2)]
            for win in range(KH):
                vb = v[ks, 256 * win : 256 * (win + 1)]
                kg = jnp.where(sub_kv[win], kt, zero)
                dv = jnp.zeros((BLK, 256), F32)
                for m in range(2):
                    h = 2 * win + m
                    qh = jnp.where(by_kv[win], q[qs, 256 * m : 256 * (m + 1)], zero)
                    do = jnp.where(in_mixed[h], do_s[qs, LANES * win : LANES * win + 256], zero)
                    sc = dot_nt(kb, qh) * SCALE_LOG2 + bias
                    p = jnp.exp2(sc - logs[h : h + 1, :])
                    dp = dot_nt(vb, do)
                    ds = (p * (dp - delta[h : h + 1, :])).astype(BF)
                    dv = dv + dot_nn(p.astype(BF), do)
                    dk = dk + dot_nn(ds, qh)
                    dq[m] = dq[m] + dot_nn(kg, ds)
                dv_s[ks, 256 * win : 256 * (win + 1)] += dv
            dk_s[ks, :] += dk
            for m in range(2):
                dq_s[i, m] += dq[m]
            return 0

        lax.fori_loop(0, i - js_ref[s_id * CTX + i] + 1, step, 0)
        return 0

    lax.fori_loop(0, blocks, outer, 0)
    head_lane = lane[:, :LANES] < HD

    def finish(i, _):
        rows = pl.ds(pl.multiple_of(i * BLK, BLK), BLK)
        cs, sn = cos[rows, :] * SCALE, sin[rows, :] * SCALE
        a0, a1 = dv_s[rows, 0:128], dv_s[rows, 128:256]
        b0, b1 = dv_s[rows, 256:384], dv_s[rows, 384:512]

        def r(x, n):
            return pltpu.roll(x, n, 1)

        pieces = [
            r(a0, 96) + a0,
            r(a0, 64) + r(a1, 96),
            r(a0, 32) + r(a1, 64),
            r(b0, 32) + r(b1, 64),
            b0 + r(b1, 32),
            r(b1, 96) + b1,
        ]
        grads = []
        for m in range(2):
            dq = jnp.transpose(dq_s[i, m])
            grads += [dq[:, 0:128], dq[:, 128:256]]
        grads += [dk_s[rows, 0:128], dk_s[rows, 128:256]]
        for p in range(0, 6, 2):
            first_half = grads[p] * cs + grads[p + 1] * sn
            second_half = grads[p + 1] * cs - grads[p] * sn
            out[rows, LANES * p : LANES * (p + 1)] = jnp.where(head_lane, first_half, pieces[p]).astype(BF)
            out[rows, LANES * (p + 1) : LANES * (p + 2)] = jnp.where(
                head_lane, second_half, pieces[p + 1]
            ).astype(BF)
        return 0

    lax.fori_loop(0, blocks, finish, 0)


def attend_back_call(c, js, q, k, v, o, d0, d1, d23, lse, start, cos, sin, seqs, length):
    blocks = length // BLK
    width = QH * HD
    return pl.pallas_call(
        attend_back_kernel,
        grid_spec=pltpu.PrefetchScalarGridSpec(
            num_scalar_prefetch=2,
            grid=(seqs,),
            in_specs=[
                pl.BlockSpec((length, 512), lambda s, js, c: (s, 0)),
                pl.BlockSpec((length, 256), lambda s, js, c: (s, 0)),
                pl.BlockSpec((length, 512), lambda s, js, c: (s, 0)),
                pl.BlockSpec((CTX, 1, BLK, width), lambda s, js, c: (0, s, 0, 0)),
                pl.BlockSpec((1, 1, BLK, width), lambda s, js, c: (0, s, 0, 0)),
                pl.BlockSpec((1, BLK, width), lambda s, js, c: (s, 0, 0)),
                pl.BlockSpec((2, 1, BLK, width), lambda s, js, c: (0, s, 0, 0)),
                pl.BlockSpec((1, blocks, 8, BLK), lambda s, js, c: (s, 0, 0, 0)),
                pl.BlockSpec((1, blocks, 1, BLK), lambda s, js, c: (s, 0, 0, 0)),
                pl.BlockSpec((length, LANES), lambda s, js, c: (s, 0)),
                pl.BlockSpec((length, LANES), lambda s, js, c: (s, 0)),
            ],
            out_specs=pl.BlockSpec((length, 768), lambda s, js, c: (s, 0)),
            scratch_shapes=[
                pltpu.VMEM((length, width), BF),
                pltpu.VMEM((blocks, 8, BLK), F32),
                pltpu.VMEM((blocks, 256, BLK), BF),
                pltpu.VMEM((blocks, 2, 256, BLK), F32),
                pltpu.VMEM((length, 256), F32),
                pltpu.VMEM((length, 512), F32),
            ],
        ),
        out_shape=jax.ShapeDtypeStruct((seqs * length, 768), BF),
        compiler_params=params(48, ("arbitrary",)),
        cost_estimate=cost(31),
        name="attend_back",
    )(js, c, q, k, v, o, d0, d1, d23, lse, start, cos, sin)


def assemble_kernel(c_ref, f_ref, p0, p1, p2, p3, out):
    quarter = p0.shape[-1]
    for b in range(CTX):
        for d, ref in enumerate((p0, p1, p2, p3)):

            @pl.when((b ^ c_ref[0]) == d)
            def _():
                out[:, b * quarter : (b + 1) * quarter] = ref[0]


def assemble_call(c, f, parts):
    count, rows, quarter = parts[0].shape
    part = pl.BlockSpec((1, rows, quarter), lambda b, c, f: (b ^ f[0], 0, 0))
    return pl.pallas_call(
        assemble_kernel,
        grid_spec=pltpu.PrefetchScalarGridSpec(
            num_scalar_prefetch=2,
            grid=(count,),
            in_specs=[part] * CTX,
            out_specs=pl.BlockSpec((rows, CTX * quarter), lambda b, c, f: (b, 0)),
        ),
        out_shape=jax.ShapeDtypeStruct((count * rows, CTX * quarter), BF),
        compiler_params=params(20, ("arbitrary",)),
        cost_estimate=cost(5),
        name="assemble",
    )(c, f, *parts)


def out_kernel(c_ref, x, m0, m1, m2, m3, w, resid, normed):
    c = c_ref[0]
    acc = x[0].astype(F32)
    for d, ref in enumerate((m0, m1, m2, m3)):
        rows = pl.ds(pl.multiple_of((d ^ c) * (QH * HD), QH * HD), QH * HD)
        acc = acc + dot_nn(ref[0, 0], w[rows, :])
    resid[0] = acc
    normed[0] = rms_rows(acc).astype(BF)


def out_call(c, x, mixed, r1, r2, w):
    seqs, tok, width = x.shape
    inner_w = QH * HD

    def slot(n):
        return pl.BlockSpec((1, 1, tok, inner_w), lambda s, c: (n, s, 0, 0))

    tile = pl.BlockSpec((1, tok, width), lambda s, c: (s, 0, 0))
    return pl.pallas_call(
        out_kernel,
        grid_spec=pltpu.PrefetchScalarGridSpec(
            num_scalar_prefetch=1,
            grid=(seqs,),
            in_specs=[
                tile,
                slot(0),
                slot(0),
                slot(0),
                slot(1),
                pl.BlockSpec((H * HD, width), lambda s, c: (0, 0)),
            ],
            out_specs=[tile, tile],
        ),
        out_shape=[
            jax.ShapeDtypeStruct((seqs, tok, width), F32),
            jax.ShapeDtypeStruct((seqs, tok, width), BF),
        ],
        compiler_params=params(48, ("arbitrary",)),
        cost_estimate=cost(8),
        name="out_proj",
    )(c, x, mixed, r1, r2, r2, w)


def rms_back(v, dyg):
    r = lax.rsqrt(jnp.mean(v * v, axis=-1, keepdims=True) + EPSILON)
    return r * dyg - v * (r * r * r * jnp.mean(dyg * v, axis=-1, keepdims=True))


def out_back_kernel(c_ref, part_a, part_b, resid, dy, w, dresid, dattn, dmixed):
    c = c_ref[0]
    dn = part_a[0].astype(F32) + part_b[0].astype(F32)
    total = dy[0].astype(F32) + rms_back(resid[0], dn)
    dresid[0] = total
    low = total.astype(BF)
    dattn[0] = low
    for d in range(CTX):
        rows = pl.ds(pl.multiple_of((d ^ c) * (QH * HD), QH * HD), QH * HD)
        dmixed[d, 0] = dot_nt(low, w[rows, :]).astype(BF)


def out_back_call(c, part_a, part_b, resid, dy, w):
    seqs, tok, width = dy.shape
    inner_w = QH * HD
    tile = pl.BlockSpec((1, tok, width), lambda s, c: (s, 0, 0))
    return pl.pallas_call(
        out_back_kernel,
        grid_spec=pltpu.PrefetchScalarGridSpec(
            num_scalar_prefetch=1,
            grid=(seqs,),
            in_specs=[
                tile,
                tile,
                tile,
                tile,
                pl.BlockSpec((H * HD, width), lambda s, c: (0, 0)),
            ],
            out_specs=[
                tile,
                tile,
                pl.BlockSpec((CTX, 1, tok, inner_w), lambda s, c: (0, s, 0, 0)),
            ],
        ),
        out_shape=[
            jax.ShapeDtypeStruct((seqs, tok, width), F32),
            jax.ShapeDtypeStruct((seqs, tok, width), BF),
            jax.ShapeDtypeStruct((CTX, seqs, tok, inner_w), BF),
        ],
        compiler_params=params(56, ("arbitrary",)),
        cost_estimate=cost(9.5),
        name="out_back",
    )(c, part_a, part_b, resid, dy, w)


def mlp_kernel(n2, dy, wg, wu, wd, hidden, grads):
    n, g_out = n2[...], dy[...]
    gate = dot_nn(n, wg[...])
    up = dot_nn(n, wu[...])
    dh = dot_nn(g_out, wd[...])
    sig = 1.0 / (1.0 + jnp.exp(-gate))
    act = gate * sig
    hidden[...] = (act * up).astype(BF)
    cols = wg.shape[1]
    grads[0] = (dh * up * (sig + act * (1.0 - sig))).astype(BF)
    grads[1] = (dh * act).astype(BF)


def mlp_call(n2, dy, w):
    rows, width = n2.shape
    ff = w.shape[1] // 3
    tile = BLK
    steps = ff // tile
    full = pl.BlockSpec((rows, width), lambda j: (0, 0))
    return pl.pallas_call(
        mlp_kernel,
        grid=(steps,),
        in_specs=[
            full,
            full,
            pl.BlockSpec((width, tile), lambda j: (0, j)),
            pl.BlockSpec((width, tile), lambda j: (0, j + steps)),
            pl.BlockSpec((width, tile), lambda j: (0, j + 2 * steps)),
        ],
        out_specs=[
            pl.BlockSpec((rows, tile), lambda j: (0, j)),
            pl.BlockSpec((2, rows, tile), lambda j: (0, 0, j)),
        ],
        out_shape=[
            jax.ShapeDtypeStruct((rows, ff), BF),
            jax.ShapeDtypeStruct((2, rows, ff), BF),
        ],
        compiler_params=params(40, ("arbitrary",)),
        cost_estimate=cost(4.5),
        name="mlp",
    )(n2, dy, w, w, w)


def sum_nt_kernel(slots, *refs):
    count = len(slots)
    out = refs[-1]
    acc = None
    for n in range(count):
        left = refs[n]
        part = dot_nt(left[0] if len(left.shape) == 3 else left[...], refs[count + n][...])
        acc = part if acc is None else acc + part
    out[...] = acc.astype(out.dtype)


def sum_nt_call(terms, tile):
    rows, k = terms[0][0].shape[-2:]
    n = terms[0][2].shape[0]
    lefts, rights = [], []
    for array, slot, weight, window in terms:
        if slot is None:
            lefts.append(pl.BlockSpec((rows, k), lambda j: (0, 0)))
        else:
            lefts.append(pl.BlockSpec((1, rows, k), functools.partial(lambda slot, j: (slot, 0, 0), slot)))
        rights.append(pl.BlockSpec((tile, k), functools.partial(lambda window, j: (j, window), window)))
    count = len(terms)
    return pl.pallas_call(
        functools.partial(sum_nt_kernel, tuple(t[1] for t in terms)),
        grid=(n // tile,),
        in_specs=lefts + rights,
        out_specs=pl.BlockSpec((rows, tile), lambda j: (0, j)),
        out_shape=jax.ShapeDtypeStruct((rows, n), BF),
        compiler_params=params(40, ("arbitrary",)),
        cost_estimate=cost(4.4),
        name="sum_nt",
    )(*[t[0] for t in terms], *[t[2] for t in terms])


def put_sides(f_ref, acc, mine, theirs):
    acc = acc.astype(BF)
    count, rows, _ = mine.shape
    for side in range(2):

        @pl.when(f_ref[0] % 2 == side)
        def _():
            for z in range(count):
                at = 2 * z * rows
                mine[z] = acc[at + side * rows : at + (side + 1) * rows]
                theirs[z] = acc[at + (1 - side) * rows : at + (2 - side) * rows]


def mlp_gram_kernel(count, *refs):
    dys, n2s = refs[:count], refs[count : 2 * count]
    hid, gu = refs[2 * count : 3 * count], refs[3 * count : 4 * count]
    out = refs[-1]

    @pl.when(pl.program_id(0) == 0)
    def _():
        acc = dot_tn(dys[0][...], hid[0][...])
        for n in range(1, count):
            acc = acc + dot_tn(dys[n][...], hid[n][...])
        out[...] = acc.astype(out.dtype)

    @pl.when(pl.program_id(0) != 0)
    def _():
        acc = dot_tn(n2s[0][...], gu[0][0])
        for n in range(1, count):
            acc = acc + dot_tn(n2s[n][...], gu[n][0])
        out[...] = acc.astype(out.dtype)


def mlp_gram_call(dys, n2s, hid, gu, tile_m):
    rows, m = dys[0].shape
    k = hid[0].shape[1]
    count = len(dys)
    return pl.pallas_call(
        functools.partial(mlp_gram_kernel, count),
        grid=(3, m // tile_m),
        in_specs=[pl.BlockSpec((rows, tile_m), lambda j, i: (0, jnp.where(j == 0, i, m // tile_m - 1)))] * count
        + [pl.BlockSpec((rows, tile_m), lambda j, i: (0, jnp.where(j == 0, 0, i)))] * count
        + [pl.BlockSpec((rows, k), lambda j, i: (0, 0))] * count
        + [pl.BlockSpec((1, rows, k), lambda j, i: (jnp.maximum(j - 1, 0), 0, 0))] * count,
        out_specs=pl.BlockSpec((tile_m, k), lambda j, i: (i, j)),
        out_shape=jax.ShapeDtypeStruct((m, 3 * k), BF),
        compiler_params=params(56, ("arbitrary", "arbitrary")),
        cost_estimate=cost(18),
        name="mlp_gram",
    )(*dys, *n2s, *hid, *gu)


def gram_kernel(f_ref, left, right, mine, theirs):
    put_sides(f_ref, dot_tn(left[...], right[...]), mine, theirs)


def gram_call(f, left, right):
    rows, m = left.shape
    n = right.shape[1]
    one = pl.BlockSpec((2, m // 8, n), lambda i, f: (i, 0, 0))
    return pl.pallas_call(
        gram_kernel,
        grid_spec=pltpu.PrefetchScalarGridSpec(
            num_scalar_prefetch=1,
            grid=(2,),
            in_specs=[
                pl.BlockSpec((rows, m // 2), lambda i, f: (0, i)),
                pl.BlockSpec((rows, n), lambda i, f: (0, 0)),
            ],
            out_specs=[one, one],
        ),
        out_shape=[jax.ShapeDtypeStruct((4, m // 8, n), BF)] * 2,
        compiler_params=params(40, ("arbitrary",)),
        cost_estimate=cost(6),
        name="gram",
    )(f, left, right)


def out_gram_kernel(c_ref, f_ref, m0, m1, m2, m3, dattn, out):
    side = f_ref[0] % 2
    rows = out.shape[3]
    for d, ref in enumerate((m0, m1, m2, m3)):

        @pl.when(pl.program_id(0) == d)
        def _():
            tok = ref.shape[1] * ref.shape[2]
            acc = dot_tn(ref[0].reshape(tok, ref.shape[3]), dattn[...]).astype(BF)

            @pl.when(side == 0)
            def _():
                out[0, 0, 0] = acc[:rows]
                out[0, 1, 0] = acc[rows:]

            @pl.when(side != 0)
            def _():
                out[0, 0, 0] = acc[rows:]
                out[0, 1, 0] = acc[:rows]


def out_gram_call(c, f, mixed, r1, r2, dattn):
    seqs, tok, inner_w = mixed.shape[1:]
    rows, width = dattn.shape
    quarter = width // CTX

    def slot(n):
        return pl.BlockSpec((1, seqs, tok, inner_w), lambda d, e, c, f: (n, 0, 0, 0))

    return pl.pallas_call(
        out_gram_kernel,
        grid_spec=pltpu.PrefetchScalarGridSpec(
            num_scalar_prefetch=2,
            grid=(CTX, CTX),
            in_specs=[
                slot(0),
                slot(0),
                slot(0),
                slot(1),
                pl.BlockSpec((rows, quarter), lambda d, e, c, f: (0, e ^ c[0])),
            ],
            out_specs=pl.BlockSpec(
                (1, 2, 1, inner_w // 2, quarter), lambda d, e, c, f: (e, 0, d ^ c[0], 0, 0)
            ),
        ),
        out_shape=jax.ShapeDtypeStruct((CTX, 2, 4, inner_w // 2, quarter), BF),
        compiler_params=params(40, ("arbitrary", "arbitrary")),
        cost_estimate=cost(9),
        name="out_gram",
    )(c, f, mixed, r1, r2, r2, dattn)


def unpack_kernel(c_ref, s0, s1, s2, s3, perm, wq, wk, wv, gain, gq, gk, gv, gg, gm, go):
    c = c_ref[0]
    qw, kw = QH * HD, KH * HD
    n = perm.shape[0]
    g = gain[...]
    for b in range(CTX):
        for d, ref in enumerate((s0, s1, s2, s3)):

            @pl.when((b ^ c) == d)
            def _():
                flat = dot_nt(ref[:, :n], perm[...])
                gq[:, b * qw : (b + 1) * qw] = flat[:, :qw]
                gk[:, b * kw : (b + 1) * kw] = flat[:, qw : qw + kw]
                gv[:, b * kw : (b + 1) * kw] = flat[:, qw + kw :]
                go[:, b * qw : (b + 1) * qw] = ref[:, n : n + qw].astype(F32)

    total = jnp.zeros_like(g)
    for grad, w in ((gq, wq), (gk, wk), (gv, wv)):
        total = total + jnp.sum(grad[...] * w[...].astype(F32), axis=-1, keepdims=True)
        grad[...] = grad[...] * g
    gg[...] = total
    gm[...] = (
        s0[:, n + qw :].astype(F32)
        + s1[:, n + qw :].astype(F32)
        + s2[:, n + qw :].astype(F32)
        + s3[:, n + qw :].astype(F32)
    )[:, 0:1]


def unpack_call(c, parts, perm, wq, wk, wv, gain):
    rows = parts[0].shape[0]
    vm = pl.BlockSpec(memory_space=pltpu.VMEM)
    return pl.pallas_call(
        unpack_kernel,
        in_specs=[pl.BlockSpec(memory_space=pltpu.SMEM)] + [vm] * 9,
        out_specs=[vm] * 6,
        out_shape=[
            jax.ShapeDtypeStruct((rows, H * HD), F32),
            jax.ShapeDtypeStruct((rows, KVH * HD), F32),
            jax.ShapeDtypeStruct((rows, KVH * HD), F32),
            jax.ShapeDtypeStruct((rows, 1), F32),
            jax.ShapeDtypeStruct((rows, 1), F32),
            jax.ShapeDtypeStruct((rows, CTX * QH * HD), F32),
        ],
        compiler_params=pltpu.CompilerParams(vmem_limit_bytes=40 << 20),
        cost_estimate=cost(5),
        name="unpack",
    )(c, *parts, perm, wq, wk, wv, gain)


def qkv_back_kernel(c_ref, g, w, out):
    out[0, 0] = dot_nt(g[...], w[...]).astype(BF)


def qkv_back_call(c, grads, w, seqs, base):
    width = w.shape[0]
    return pl.pallas_call(
        qkv_back_kernel,
        grid_spec=pltpu.PrefetchScalarGridSpec(
            num_scalar_prefetch=1,
            grid=(2, seqs),
            in_specs=[
                pl.BlockSpec((BLK, 768), lambda d, s, c: (s * CTX + ((d + base) ^ c[0]), 0)),
                pl.BlockSpec((width, 768), lambda d, s, c: (0, 0)),
            ],
            out_specs=pl.BlockSpec((1, 1, BLK, width), lambda d, s, c: (d, s, 0, 0)),
        ),
        out_shape=jax.ShapeDtypeStruct((2, seqs, BLK, width), BF),
        compiler_params=params(40, ("arbitrary", "arbitrary")),
        cost_estimate=cost(3.3),
        name="qkv_back",
    )(c, grads, w)


def final_kernel(part_a, part_b, x, dresid, out):
    dn = part_a[0].astype(F32) + part_b[0].astype(F32)
    out[0] = dresid[0] + rms_back(x[0].astype(F32), dn)


def final_call(part_a, part_b, x, dresid):
    seqs, tok, width = x.shape
    tile = pl.BlockSpec((1, tok, width), lambda s: (s, 0, 0))
    return pl.pallas_call(
        final_kernel,
        grid=(seqs,),
        in_specs=[tile] * 4,
        out_specs=tile,
        out_shape=jax.ShapeDtypeStruct((seqs, tok, width), F32),
        compiler_params=params(40, ("arbitrary",)),
        cost_estimate=cost(4),
        name="final",
    )(part_a, part_b, x, dresid)


CORE = [(i, i ^ 1) for i in range(CTX)]
ROW = [(i, i ^ 2) for i in range(CTX)]


def swap_core(x):
    return lax.ppermute(x, "context", CORE)


def swap_row(x):
    return lax.ppermute(x, "context", ROW)


def gather_blocks(x):
    far = swap_row(x)
    near = swap_core(x)
    return [x, near, far, swap_core(far)]


def after(x, *first):
    return lax.optimization_barrier((x,) + first)[0]


def swap_fsdp(x, bit):
    size = lax.axis_size("fsdp")
    return lax.ppermute(x, "fsdp", [(i, i ^ bit) for i in range(size)])


def gather_fsdp(x):
    near = swap_fsdp(x, 2)
    side = swap_fsdp(x, 1)
    far = swap_fsdp(jnp.stack([x, near]), 4)
    near_side = swap_fsdp(near, 1)
    far_side = swap_fsdp(far, 1)
    return jnp.stack([x, side, near, near_side, far[0], far_side[0], far[1], far_side[1]])


def z_groups():
    size = lax.axis_size("fsdp")
    return [list(range(0, size, 2)), list(range(1, size, 2))]


def reduce_x(mine, theirs, *first):
    total = add_low(after(mine, *first), swap_fsdp(theirs, 1))
    return total.reshape(-1, total.shape[-1])


def reduce_z(x):
    return lax.psum_scatter(x, "fsdp", scatter_dimension=0, tiled=True, axis_index_groups=z_groups())


def add_low(a, b):
    return (a.astype(F32) + b.astype(F32)).astype(BF)


def on_device(
    tokens,
    segments,
    w_query,
    w_key,
    w_value,
    w_out,
    w_gate,
    w_up,
    w_down,
    gain_attn,
    gain_mlp,
    cotangent,
):
    seqs, tok, width = tokens.shape
    rows = seqs * tok
    length = tok * CTX
    qkv_w = (QH + 2 * KH) * HD
    ctx = lax.axis_index("context")
    core = ctx % 2
    c = ctx.astype(jnp.int32).reshape(1)

    last = []

    def step(call, x, *ready):
        x = after(x, *last, *ready)
        out = call(x)
        last[:] = [out[0] if isinstance(out, (tuple, list)) else out]
        return out

    segs = gather_blocks(segments)
    xs = gather_blocks(after(tokens, segs[2]))
    dys = gather_blocks(after(cotangent, xs[2]))

    perm = pack_matrix()
    fsdp = lax.axis_index("fsdp").astype(jnp.int32).reshape(1)
    col_a, col_m = gain_attn.astype(F32)[:, None], gain_mlp.astype(F32)[:, None]
    shard = jnp.concatenate(
        [
            lax.dynamic_slice_in_dim(w_query, ctx * (QH * HD), QH * HD, 1),
            lax.dynamic_slice_in_dim(w_key, ctx * (KH * HD), KH * HD, 1),
            lax.dynamic_slice_in_dim(w_value, ctx * (KH * HD), KH * HD, 1),
        ],
        axis=1,
    )
    shard = jnp.dot(shard, perm, preferred_element_type=F32)
    shard = (shard * col_a).astype(BF)
    quarter = width // CTX
    w_qkv = lax.all_gather(shard, "fsdp", axis=0, tiled=True)
    out_part = gather_fsdp(lax.dynamic_slice_in_dim(w_out, ctx * quarter, quarter, 1))
    out_parts = gather_blocks(out_part)
    down_t = jnp.transpose(w_down)
    ff = w_gate.shape[1] // 2
    w_parts = []
    for n in range(2):
        cols = slice(n * ff, (n + 1) * ff)
        part = jnp.concatenate(
            [
                (w_gate[:, cols].astype(F32) * col_m).astype(BF),
                (w_up[:, cols].astype(F32) * col_m).astype(BF),
                down_t[:, cols],
            ],
            axis=1,
        )
        part = after(part, *(segs[2:3] if n else [shard]))
        w_parts.append(lax.all_gather(part, "fsdp", axis=0, tiled=True))
    w_one, w_two = w_parts

    seg_blocks = jnp.stack(segs)
    whole_seg = jnp.concatenate(
        [lax.dynamic_index_in_dim(seg_blocks, b ^ ctx, 0, keepdims=False) for b in range(CTX)], axis=1
    )
    index = jnp.arange(length, dtype=jnp.int32)
    starts = jnp.concatenate(
        [jnp.ones((seqs, 1), dtype=bool), whole_seg[:, 1:] != whole_seg[:, :-1]], axis=1
    )
    first = lax.cummax(jnp.where(starts, index[None, :], 0), axis=1)
    positions = (index[None, :] - first).astype(F32).reshape(seqs * length, 1)
    freq = np.zeros((LANES,), np.float32)
    base = (THETA ** -(np.arange(HALF, dtype=np.float64) * 2.0 / HD)).astype(np.float32)
    for g in range(KH):
        freq[g * HALF : (g + 1) * HALF] = base
    angles = positions * jnp.asarray(freq)[None, :]
    cos, sin = jnp.cos(angles), jnp.sin(angles)
    low_block = (first[:, ::BLK] // BLK).reshape(seqs * CTX).astype(jnp.int32)
    first_rows = first.reshape(seqs, CTX, 1, BLK)

    normed, q, k, v = step(lambda t: qkv_call(c, xs, t, cos, sin), w_qkv, first_rows)
    mixed, lse = step(
        lambda t: attend_call(c, low_block, t, k, v, first_rows, seqs, length), q, dys[2]
    )
    r1 = swap_core(jnp.stack([mixed[1], mixed[3]]))
    r2 = swap_row(jnp.stack([mixed[2], r1[1]]))
    w_out_full = step(lambda t: assemble_call(c, fsdp, out_parts[:3] + [t]), out_parts[3])
    resid, normed_two = step(lambda t: out_call(c, tokens, mixed, r1, t, w_out_full), r2)

    n2s = [n.reshape(rows, width) for n in gather_blocks(normed_two)]
    dys = [d.reshape(rows, width) for d in dys]
    first_pairs = [step(lambda t: mlp_call(t, dys[d], w_one), n2s[d]) for d in range(CTX)]
    def gram(pairs, *ready):
        hid, gu = [p[0] for p in pairs], [p[1] for p in pairs]
        return step(lambda t: mlp_gram_call(dys, [t] + n2s[1:], hid, gu, 768), n2s[0], *ready)

    share_one = gram(first_pairs)
    s_one = lax.psum_scatter(share_one, "fsdp", scatter_dimension=0, tiled=True)
    second_pairs = [None] * CTX

    def back_rows(d, *ready):
        def call(t):
            terms = [(first_pairs[d][1], slot, w_one, slot) for slot in range(2)]
            return sum_nt_call(terms + [(t, slot, w_two, slot) for slot in range(2)], 512)

        return step(call, second_pairs[d][1], *ready)

    def down_rows(d, *ready):
        call = lambda t: sum_nt_call([(first_pairs[d][0], None, w_one, 2), (t, None, w_two, 2)], 512)
        return step(call, second_pairs[d][0], *ready)

    def back_pair(near, far, *ready):
        for d in (far, near):
            second_pairs[d] = step(lambda t: mlp_call(t, dys[d], w_two), n2s[d])
        low = back_rows(far)
        return back_rows(near, *ready), swap_core(low)

    dn2 = add_low(*back_pair(2, 3))
    dn_b = swap_row(dn2)
    last.append(dn2)
    dn_a = add_low(*back_pair(0, 1))
    share_two = gram(second_pairs)
    s_two = lax.psum_scatter(share_two, "fsdp", scatter_dimension=0, tiled=True)
    dresid, dattn, dmixed = step(
        lambda t: out_back_call(
            c, dn_a.reshape(tokens.shape), t.reshape(tokens.shape), resid, cotangent, w_out_full
        ),
        dn_b,
    )

    b1 = swap_core(jnp.stack([dmixed[1], dmixed[3]]))
    b2_send = jnp.stack([dmixed[2], b1[1]])
    b2 = swap_row(b2_send)
    g_out = step(lambda t: out_gram_call(c, fsdp, mixed, r1, r2, t), dattn.reshape(rows, width))
    got = swap_core(jnp.stack([g_out[1], g_out[3]]))
    g_send = add_low(g_out[2], got[1])
    low3, low2 = down_rows(3), down_rows(2)
    dqkv = step(
        lambda t: attend_back_call(
            c, low_block, q, k, v, mixed, dmixed, b1[0], t, lse, first_rows, cos, sin, seqs, length
        ),
        b2,
        g_send,
    )
    got_row = swap_row(after(g_send, b2))

    g_out = add_low(add_low(g_out[0], got[0]), after(got_row, dqkv))
    x_out = reduce_x(g_out[0], g_out[1])
    qkv_mine, qkv_theirs = step(lambda t: gram_call(fsdp, normed, t), dqkv, g_out)
    far = step(lambda t: qkv_back_call(c, t, w_qkv, seqs, 2), dqkv, x_out)
    dx2 = add_low(far[0], swap_core(far[1]))
    dx_b = swap_row(dx2)
    near = step(lambda t: qkv_back_call(c, t, w_qkv, seqs, 0), dqkv)
    dx_a = add_low(near[0], swap_core(near[1]))
    down2 = add_low(low2, swap_core(low3))
    down_b = swap_row(after(down2, got_row))
    low1, low0 = down_rows(1, down_b, dx2), down_rows(0)
    down_a = add_low(low0, swap_core(low1))
    x_all = jnp.concatenate([reduce_x(qkv_mine, qkv_theirs, near), x_out], axis=1)
    s_attn = reduce_z(x_all)
    s_down, s_gate, s_up = [
        jnp.concatenate([s[:, n * ff : (n + 1) * ff] for s in (s_one, s_two)], axis=1).astype(F32)
        for n in range(3)
    ]
    part_m = jnp.sum(s_gate * w_gate.astype(F32) + s_up * w_up.astype(F32), axis=1, keepdims=True)
    part_m = jnp.broadcast_to(part_m, (part_m.shape[0], LANES)).astype(BF)
    grad_tokens = step(lambda t: final_call(dx_a, t, tokens, dresid), dx_b, x_all, part_m)
    sums = gather_blocks(after(jnp.concatenate([s_attn, part_m], axis=1), grad_tokens))
    output = (
        resid + down_a.astype(F32).reshape(resid.shape) + down_b.astype(F32).reshape(resid.shape)
    ).astype(BF)
    g_query, g_key, g_value, g_gain_a, g_gain_m, g_w_out = step(
        lambda t: unpack_call(c, sums[:3] + [t], perm, w_query, w_key, w_value, col_a), sums[3]
    )
    return (
        output,
        grad_tokens,
        g_query,
        g_key,
        g_value,
        g_w_out,
        s_gate * col_m,
        s_up * col_m,
        jnp.transpose(s_down),
        g_gain_a[:, 0],
        g_gain_m[:, 0],
    )


def solution(mesh):
    split_heads = mesh.shape["context"] == CTX
    return jax.shard_map(
        on_device if split_heads else on_device_general,
        mesh=mesh,
        in_specs=(
            P("fsdp", "context", None),
            P("fsdp", "context"),
            P("fsdp", None),
            P("fsdp", None),
            P("fsdp", None),
            P("fsdp", None),
            P("fsdp", "context"),
            P("fsdp", "context"),
            P("context", "fsdp"),
            P("fsdp"),
            P("fsdp"),
            P("fsdp", "context", None),
        ),
        out_specs=(
            P("fsdp", "context", None),
            P("fsdp", "context", None),
            P("fsdp", None),
            P("fsdp", None),
            P("fsdp", None),
            P("fsdp", None),
            P("fsdp", "context"),
            P("fsdp", "context"),
            P("context", "fsdp"),
            P("fsdp"),
            P("fsdp"),
        ),
        check_vma=False,
    )
```
